32 devices in a mesh: seq: 16 (over z, x, core), tp: 2 (over y).
Axes of the slice: x: 2, y: 2, z: 4, core: 2. Of those that a mesh axis runs over, the one named last changes fastest.
Arguments:
- hidden: bfloat16 [8192, 2048], P(('seq', 'tp')), may hold values from -6 to 6
- layer_input: bfloat16 [8192, 256], P(('seq', 'tp')), may hold values from -6 to 6
- cotangent: bfloat16 [8192, 2048], P(('seq', 'tp')), may hold values from -6 to 6
- span_starts: int32 [8192], replicated, may hold values from 0 to 8191, as said below
- query_weight: bfloat16 [2048, 2048], P('seq', 'tp'), may hold values from -0.125 to 0.125
- key_weight: bfloat16 [2048, 512], P('seq', 'tp'), may hold values from -0.125 to 0.125
- value_weight: bfloat16 [2048, 512], P('seq', 'tp'), may hold values from -0.125 to 0.125
- output_weight: bfloat16 [2048, 2048], P('tp', 'seq'), may hold values from -0.125 to 0.125
- laurel_left: bfloat16 [2048, 64], P(('seq', 'tp')), may hold values from -0.125 to 0.125
- laurel_right: bfloat16 [64, 2048], P(None, ('seq', 'tp')), may hold values from -0.75 to 0.75
- gate_weight: bfloat16 [2048, 8192], P('seq', 'tp'), may hold values from -0.125 to 0.125
- upward_weight: bfloat16 [2048, 8192], P('seq', 'tp'), may hold values from -0.125 to 0.125
- down_weight: bfloat16 [8192, 2048], P('tp', 'seq'), may hold values from -0.0625 to 0.0625
- branch_gate: bfloat16 [2048, 256], P(('seq', 'tp')), may hold values from -0.125 to 0.125
- branch_output: bfloat16 [256, 2048], P(None, ('seq', 'tp')), may hold values from -0.375 to 0.375
- input_gain: float32 [2048], replicated, may hold values from 0.1 to 1.9
- query_gain: float32 [256], replicated, may hold values from 0.1 to 1.9
- key_gain: float32 [256], replicated, may hold values from 0.1 to 1.9
- mixer_gain: float32 [2048], replicated, may hold values from 0.1 to 1.9
- laurel_gain: float32 [2048], replicated, may hold values from 0.1 to 1.9
- prefeed_gain: float32 [2048], replicated, may hold values from 0.1 to 1.9
- postfeed_gain: float32 [2048], replicated, may hold values from 0.1 to 1.9
- branch_gain: float32 [2048], replicated, may hold values from 0.1 to 1.9
Outputs:
- result: bfloat16 [8192, 2048], P(('seq', 'tp'))
- hidden_delta: float32 [8192, 2048], P(('seq', 'tp'))
- layer_delta: float32 [8192, 256], P(('seq', 'tp'))
- query_delta: float32 [2048, 2048], P('seq', 'tp')
- key_delta: float32 [2048, 512], P('seq', 'tp')
- value_delta: float32 [2048, 512], P('seq', 'tp')
- output_delta: float32 [2048, 2048], P('tp', 'seq')
- left_delta: float32 [2048, 64], P(('seq', 'tp'))
- right_delta: float32 [64, 2048], P(None, ('seq', 'tp'))
- gate_delta: float32 [2048, 8192], P('seq', 'tp')
- upward_delta: float32 [2048, 8192], P('seq', 'tp')
- down_delta: float32 [8192, 2048], P('tp', 'seq')
- branch_delta: float32 [2048, 256], P(('seq', 'tp'))
- project_delta: float32 [256, 2048], P(None, ('seq', 'tp'))
- input_slope: float32 [2048], replicated
- query_slope: float32 [256], replicated
- key_slope: float32 [256], replicated
- mixer_slope: float32 [2048], replicated
- laurel_slope: float32 [2048], replicated
- prefeed_slope: float32 [2048], replicated
- postfeed_slope: float32 [2048], replicated
- branch_slope: float32 [2048], replicated
The draws below stay inside these ranges and needn't reach their ends.
Inputs may be any that keep to these rules, and one draw needn't show every extreme that they name: `span_starts`: A picture token holds the index of its span's first token, a text token its own index; every span is exactly 256 consecutive tokens, and every boundary between aligned blocks of 512 tokens lies strictly inside one span.
All inputs are finite; a program needn't handle non-finite values.
Results may differ from the reference program's by a relative error of at most 0.018.
Values may be sent and summed in bfloat16 or wider, within the bound.
No kernel may reach another device: no remote copies, remote signals or barrier semaphores. Data moves between devices by JAX's collectives and lax.ppermute only.
A program may use at most 320 MiB of HBM per device.

```python
import jax
import jax.numpy as jnp
from jax import lax

D = 2048
QH = 8
KVH = 2
HD = 256
FF = 8192
WIN = 512
LR = 64
PLD = 256
PIC = 256
TOK_DEV = 512
TOKENS = 8192


def draw_span_starts(key, part):
    slot_count = TOKENS // TOK_DEV
    shifts = jax.random.randint(jax.random.fold_in(key, 21), (slot_count + 1,), 1, PIC).astype(jnp.int32)
    firsts = jnp.arange(slot_count + 1, dtype=jnp.int32) * TOK_DEV - shifts
    index = jnp.arange(TOKENS, dtype=jnp.int32)
    slot = index // TOK_DEV
    following = firsts[slot + 1]
    current = firsts[slot]
    in_next = (slot + 1 < slot_count) & (index >= following)
    in_cur = (slot >= 1) & (index < current + PIC)
    return jnp.where(in_next, following, jnp.where(in_cur, current, index)).astype(jnp.int32)


def spiked(values, stream_key, source, target, blocks, factor):
    owner, partner = [(jnp.arange(values.shape[axis_at]) // (values.shape[axis_at] // blocks)).reshape([-1 if axis == axis_at else 1 for axis in range(values.ndim)]) for axis_at in (source, target)]
    chosen = jax.random.permutation(stream_key, blocks)[partner]
    strong = (owner == chosen) | (owner == (partner + blocks // 2) % blocks)
    return jnp.where(strong, factor * values, values)


def shard_levels(stream_key, extent, split, low, largest):
    loudness = 1.0
    for dim, parts in split:
        draws = jax.random.uniform(jax.random.fold_in(jax.random.fold_in(stream_key, 6), dim), (parts,), jnp.float32, low / len(split), largest / len(split))
        loudness = loudness * jnp.repeat(jnp.exp(draws), extent[dim] // parts).reshape((-1,) + (1,) * (len(extent) - 1 - dim))
    return loudness


def scatter_about(own_key, dims, scale, reach, shards=(), kind=jnp.bfloat16):
    level = shard_levels(own_key, dims, shards, -0.22, 0.18) if shards else 1.0
    drawn = jax.random.normal(own_key, dims, jnp.float32) * scale * level
    return jnp.minimum(jnp.maximum(drawn, -reach), reach).astype(kind)


def bell_draw_with(stream_key, extent, scale, most, cuts, heavy, kind=jnp.bfloat16):
    array = scale * jax.random.normal(stream_key, extent, jnp.float32)
    if cuts:
        array = array * shard_levels(stream_key, extent, cuts, -0.22, 0.18)
    return jnp.clip(spiked(array, jax.random.fold_in(stream_key, 3), *heavy), -most, most).astype(kind)


def setup_inputs(seed: int = 0) -> dict:
    seeds = jax.random.split(jax.random.key(seed), 24)
    hidden = scatter_about(seeds[0], (TOKENS, D), 1.0, 6.0, ((0, 32),))
    layer_input = scatter_about(seeds[1], (TOKENS, PLD), 1.0, 6.0, ((0, 32),))
    cotangent = bell_draw_with(seeds[2], (TOKENS, D), 1.0, 6.0, ((0, 32),), (0, 1, 32, 2.75))
    span_starts = draw_span_starts(jax.random.fold_in(seeds[23], 71), 0)
    query_weight = scatter_about(seeds[4], (D, QH * HD), D ** -0.5, 0.125, ((0, 16), (1, 2)))
    key_weight = scatter_about(seeds[5], (D, KVH * HD), D ** -0.5, 0.125, ((0, 16), (1, 2)))
    value_weight = scatter_about(seeds[6], (D, KVH * HD), D ** -0.5, 0.125, ((0, 16), (1, 2)))
    output_weight = scatter_about(seeds[7], (QH * HD, D), (QH * HD) ** -0.5, 0.125, ((0, 2), (1, 16)))
    laurel_left = scatter_about(seeds[8], (D, LR), D ** -0.5, 0.125, ((0, 32),))
    laurel_right = scatter_about(seeds[9], (LR, D), LR ** -0.5, 0.75, ((1, 32),))
    gate_weight = scatter_about(seeds[10], (D, FF), D ** -0.5, 0.125, ((0, 16), (1, 2)))
    upward_weight = scatter_about(seeds[11], (D, FF), D ** -0.5, 0.125, ((0, 16), (1, 2)))
    down_weight = scatter_about(seeds[12], (FF, D), FF ** -0.5, 0.0625, ((0, 2), (1, 16)))
    branch_gate = scatter_about(seeds[13], (D, PLD), D ** -0.5, 0.125, ((0, 32),))
    branch_output = scatter_about(seeds[14], (PLD, D), PLD ** -0.5, 0.375, ((1, 32),))
    input_gain = jnp.clip(1.0 + 0.18 * jax.random.normal(seeds[15], (D,), jnp.float32), 0.1, 1.9)
    query_gain = jnp.clip(1.0 + 0.18 * jax.random.normal(seeds[16], (HD,), jnp.float32), 0.1, 1.9)
    key_gain = jnp.clip(1.0 + 0.18 * jax.random.normal(seeds[17], (HD,), jnp.float32), 0.1, 1.9)
    mixer_gain = jnp.clip(1.0 + 0.18 * jax.random.normal(seeds[18], (D,), jnp.float32), 0.1, 1.9)
    laurel_gain = jnp.clip(1.0 + 0.18 * jax.random.normal(seeds[19], (D,), jnp.float32), 0.1, 1.9)
    prefeed_gain = jnp.clip(1.0 + 0.18 * jax.random.normal(seeds[20], (D,), jnp.float32), 0.1, 1.9)
    postfeed_gain = jnp.clip(1.0 + 0.18 * jax.random.normal(seeds[21], (D,), jnp.float32), 0.1, 1.9)
    branch_gain = jnp.clip(1.0 + 0.18 * jax.random.normal(seeds[22], (D,), jnp.float32), 0.1, 1.9)
    return {"hidden": hidden, "layer_input": layer_input, "cotangent": cotangent, "span_starts": span_starts, "query_weight": query_weight, "key_weight": key_weight, "value_weight": value_weight, "output_weight": output_weight, "laurel_left": laurel_left, "laurel_right": laurel_right, "gate_weight": gate_weight, "upward_weight": upward_weight, "down_weight": down_weight, "branch_gate": branch_gate, "branch_output": branch_output, "input_gain": input_gain, "query_gain": query_gain, "key_gain": key_gain, "mixer_gain": mixer_gain, "laurel_gain": laurel_gain, "prefeed_gain": prefeed_gain, "postfeed_gain": postfeed_gain, "branch_gain": branch_gain}


EPSILON = 1e-06
HALF_ROOT = 0.7071067811865476
ROPE_BASE = 10000.0
NEGATIVE = -1e+30
HIGH = lax.Precision.HIGHEST

@jax.custom_vjp
def low(v):
    return lax.optimization_barrier(v.astype(jnp.bfloat16)).astype(jnp.float32)

@jax.custom_vjp
def low_back(v):
    return v

def low_keep(v):
    return (low(v), None)

def low_pass(kept, grad):
    return (grad,)

def back_keep(v):
    return (v, None)

def back_low(kept, grad):
    return (low(grad),)
low.defvjp(low_keep, low_pass)
low_back.defvjp(back_keep, back_low)

def normed(value, gain):
    return value * lax.rsqrt(lax.optimization_barrier(jnp.mean(value * value, axis=-1, keepdims=True)) + EPSILON) * gain

def smooth_gate(value):
    return 0.5 * value * (1.0 + jnp.tanh(0.7978845608028654 * (value + 0.044715 * value * value * value)))

def rotary(value, cosines, sines):
    half = value.shape[-1] // 2
    first = value[..., :half]
    second = value[..., half:]
    return jnp.concatenate([first * cosines - second * sines, second * cosines + first * sines], axis=-1)

def product(left, right):
    return jnp.dot(left, right, precision=HIGH, preferred_element_type=jnp.float32)

def attention(query_low, key_low, value_low, span_starts):
    rows = query_low.shape[0]
    group = QH // KVH
    width = WIN + TOK_DEV + PIC
    scale = HD ** (-0.5)
    keys_pad = jnp.concatenate([jnp.zeros((WIN, KVH, HD), jnp.float32), key_low, jnp.zeros((PIC, KVH, HD), jnp.float32)], axis=0)
    values_pad = jnp.concatenate([jnp.zeros((WIN, KVH, HD), jnp.float32), value_low, jnp.zeros((PIC, KVH, HD), jnp.float32)], axis=0)
    valid_pad = jnp.concatenate([jnp.zeros((WIN,), jnp.int32), jnp.ones((rows,), jnp.int32), jnp.zeros((PIC,), jnp.int32)])
    starts_pad = jnp.concatenate([jnp.full((WIN,), -1, jnp.int32), span_starts, jnp.full((PIC,), -1, jnp.int32)])
    queries = query_low.reshape(rows, KVH, group, HD)

    def one_block(block_index):
        begin = block_index * TOK_DEV
        query_block = lax.dynamic_slice_in_dim(queries, begin, TOK_DEV, 0)
        key_block = lax.dynamic_slice_in_dim(keys_pad, begin, width, 0)
        value_block = lax.dynamic_slice_in_dim(values_pad, begin, width, 0)
        query_starts = lax.dynamic_slice_in_dim(span_starts, begin, TOK_DEV, 0)
        key_valid = lax.dynamic_slice_in_dim(valid_pad, begin, width, 0)
        key_starts = lax.dynamic_slice_in_dim(starts_pad, begin, width, 0)
        distance = jnp.arange(TOK_DEV, dtype=jnp.int32)[:, None] + WIN - jnp.arange(width, dtype=jnp.int32)[None, :]
        window = (distance >= 0) & (distance < WIN)
        visible = (key_valid[None, :] == 1) & (window | (query_starts[:, None] == key_starts[None, :]))
        scores = low_back(jnp.einsum('qkgd,pkd->kgqp', query_block, key_block, precision=HIGH) * scale)
        scores = jnp.where(visible[None, None], scores, NEGATIVE)
        peak = lax.optimization_barrier(jnp.max(scores, axis=-1, keepdims=True))
        expo = jnp.exp(scores - peak)
        weights = low(expo / lax.optimization_barrier(jnp.sum(expo, axis=-1, keepdims=True)))
        attended = jnp.einsum('kgqp,pkd->qkgd', weights, value_block, precision=HIGH)
        return attended.reshape(TOK_DEV, QH * HD)
    blocks = lax.map(jax.checkpoint(one_block), jnp.arange(rows // TOK_DEV, dtype=jnp.int32))
    return blocks.reshape(rows, QH * HD)

def full_forward(weights, gains, inputs, extra, span_starts):
    query_weight, key_weight, value_weight, output_weight, laurel_left, laurel_right, gate_weight, upward_weight, down_weight, branch_gate, branch_output = weights
    input_gain, query_gain, key_gain, mixer_gain, laurel_gain, prefeed_gain, postfeed_gain, branch_gain = gains
    rows = inputs.shape[0]
    normed_in = normed(inputs, input_gain)
    normed_low = low(normed_in)
    query_raw = low_back(product(normed_low, query_weight)).reshape(rows, QH, HD)
    key_raw = low_back(product(normed_low, key_weight)).reshape(rows, KVH, HD)
    value_raw = low_back(product(normed_low, value_weight)).reshape(rows, KVH, HD)
    frequency = ROPE_BASE ** (-(jnp.arange(HD // 2, dtype=jnp.float32) * 2.0) / HD)
    theta = jnp.arange(rows, dtype=jnp.float32)[:, None] * frequency[None, :]
    cosines = jnp.cos(theta)[:, None, :]
    sines = jnp.sin(theta)[:, None, :]
    query_low = low(rotary(normed(query_raw, query_gain), cosines, sines))
    key_low = low(rotary(normed(key_raw, key_gain), cosines, sines))
    value_low = low(value_raw)
    attended = low(low_back(attention(query_low, key_low, value_low, span_starts)))
    mixer_raw = low_back(product(attended, output_weight))
    laurel_mid = low(low_back(product(normed_low, laurel_left)))
    laurel_raw = low_back(product(laurel_mid, laurel_right))
    merged = (inputs + normed(mixer_raw, mixer_gain) + normed_in + normed(laurel_raw, laurel_gain)) * HALF_ROOT
    dense_low = low(normed(merged, prefeed_gain))
    gate_raw = low_back(product(dense_low, gate_weight))
    upward_raw = low_back(product(dense_low, upward_weight))
    inner_low = low(smooth_gate(gate_raw) * upward_raw)
    dense_raw = low_back(product(inner_low, down_weight))
    middle = merged + normed(dense_raw, postfeed_gain)
    middle_low = low(middle)
    branch_raw = low_back(product(middle_low, branch_gate))
    branch_low = low(smooth_gate(branch_raw) * extra)
    project_raw = low_back(product(branch_low, branch_output))
    return middle + normed(project_raw, branch_gain)

def reference(hidden, layer_input, cotangent, span_starts, query_weight, key_weight, value_weight, output_weight, laurel_left, laurel_right, gate_weight, upward_weight, down_weight, branch_gate, branch_output, input_gain, query_gain, key_gain, mixer_gain, laurel_gain, prefeed_gain, postfeed_gain, branch_gain):
    weights = (query_weight.astype(jnp.float32), key_weight.astype(jnp.float32), value_weight.astype(jnp.float32), output_weight.astype(jnp.float32), laurel_left.astype(jnp.float32), laurel_right.astype(jnp.float32), gate_weight.astype(jnp.float32), upward_weight.astype(jnp.float32), down_weight.astype(jnp.float32), branch_gate.astype(jnp.float32), branch_output.astype(jnp.float32))
    gains = (input_gain, query_gain, key_gain, mixer_gain, laurel_gain, prefeed_gain, postfeed_gain, branch_gain)

    def whole(inputs, extra, weights, gains):
        return full_forward(weights, gains, inputs, extra, span_starts)
    final, pullback = jax.vjp(whole, hidden.astype(jnp.float32), layer_input.astype(jnp.float32), weights, gains)
    hidden_delta, layer_delta, weight_deltas, gain_deltas = pullback(cotangent.astype(jnp.float32))
    return (final.astype(jnp.bfloat16), hidden_delta, layer_delta, weight_deltas[0], weight_deltas[1], weight_deltas[2], weight_deltas[3], weight_deltas[4], weight_deltas[5], weight_deltas[6], weight_deltas[7], weight_deltas[8], weight_deltas[9], weight_deltas[10], gain_deltas[0], gain_deltas[1], gain_deltas[2], gain_deltas[3], gain_deltas[4], gain_deltas[5], gain_deltas[6], gain_deltas[7])
```

```python
import jax
import jax.numpy as jnp
from jax import lax
from jax.sharding import PartitionSpec as P

QH = 8
KVH = 2
HD = 256
WIN = 512
PIC = 256


EPSILON = 1e-06
HALF_ROOT = 0.7071067811865476
ROPE_BASE = 10000.0
NEGATIVE = -1e30

LOW = jnp.bfloat16
WIDE = jnp.float32


def normed(value, gain):
    return value * lax.rsqrt(jnp.mean(value * value, axis=-1, keepdims=True) + EPSILON) * gain


def normed_back(value, gain, upstream):
    _, pullback = jax.vjp(normed, value, gain)
    return pullback(upstream)


def smooth_gate(value):
    return (
        0.5
        * value
        * (1.0 + jnp.tanh(0.7978845608028654 * (value + 0.044715 * value * value * value)))
    )


def gate_back(value, upstream):
    _, pullback = jax.vjp(smooth_gate, value)
    return pullback(upstream)[0]


def rotary(value, cosines, sines):
    half = value.shape[-1] // 2
    first = value[..., :half]
    second = value[..., half:]
    return jnp.concatenate(
        [first * cosines - second * sines, second * cosines + first * sines], axis=-1
    )


def product(left, right):
    return jnp.dot(left, right, preferred_element_type=WIDE)


def outer_sum(left, right):
    return lax.dot_general(left, right, (((0,), (0,)), ((), ())), preferred_element_type=WIDE)


def back_product(left, right):
    return lax.dot_general(left, right, (((1,), (1,)), ((), ())), preferred_element_type=WIDE)


def shifted(block, distance):
    devices = range(lax.axis_size("seq"))
    route = [(i - distance, i) for i in devices if i - distance in devices]
    return lax.ppermute(block, "seq", route)


def tp_swap(block):
    return lax.ppermute(block, "tp", [(0, 1), (1, 0)])


def core_swap(block):
    return lax.ppermute(block, "seq", [(i, i ^ 1) for i in range(lax.axis_size("seq"))])


def after(value, *others):
    return lax.optimization_barrier((value, *others))[0]


class Ring:
    def __init__(self):
        self.chips = lax.axis_size("seq") // 2
        rows = self.chips // 2
        self.order = [2 * i for i in range(rows)] + [2 * i + 1 for i in reversed(range(rows))]
        chip = lax.axis_index("seq") // 2
        place = [0] * self.chips
        for position, member in enumerate(self.order):
            place[member] = position
        self.place = place
        self.mine = jnp.asarray(place, jnp.int32)[chip]

    def moved(self, block, step):
        n = self.chips
        route = [
            (self.order[p] * 2 + core, self.order[(p + step) % n] * 2 + core)
            for p in range(n)
            for core in range(2)
        ]
        return lax.ppermute(block, "seq", route)

    def to_relative(self, value):
        width = value.shape[-1] // self.chips
        table = jnp.asarray(self.order, jnp.int32)
        parts = []
        for offset in range(self.chips):
            owner = table[(self.mine + offset) % self.chips]
            parts.append(lax.dynamic_slice_in_dim(value, owner * width, width, value.ndim - 1))
        return jnp.concatenate(parts, axis=-1)

    def from_relative(self, value):
        width = value.shape[-1] // self.chips
        parts = []
        for chip in range(self.chips):
            offset = (self.place[chip] - self.mine) % self.chips
            parts.append(lax.dynamic_slice_in_dim(value, offset * width, width, value.ndim - 1))
        return jnp.concatenate(parts, axis=-1)

    def gathered(self, chunk, ahead, gate=None):
        n = self.chips
        found = [None] * n
        found[0] = chunk
        for step in range(1, max(ahead, n - 1 - ahead) + 1):
            if step <= ahead:
                found[(n - step) % n] = self.moved(found[(n - step + 1) % n], 1)
            if step <= n - 1 - ahead:
                found[step] = self.moved(found[step - 1], -1)
        return found

    def scattered(self, term, ahead):
        n = self.chips
        behind = n - 1 - ahead
        front = back = None
        for step in range(max(ahead, behind)):
            if step < ahead:
                total = term(ahead - step)
                if front is not None:
                    total = total + front.astype(WIDE)
                front = self.moved(total.astype(LOW), 1)
            if step < behind:
                total = term(n - behind + step)
                if back is not None:
                    total = total + back.astype(WIDE)
                back = self.moved(total.astype(LOW), -1)
        return term(0) + front.astype(WIDE) + back.astype(WIDE)


def shards(
    hidden,
    layer_input,
    cotangent,
    span_starts,
    query_weight,
    key_weight,
    value_weight,
    output_weight,
    laurel_left,
    laurel_right,
    gate_weight,
    upward_weight,
    down_weight,
    branch_gate,
    branch_output,
    input_gain,
    query_gain,
    key_gain,
    mixer_gain,
    laurel_gain,
    prefeed_gain,
    postfeed_gain,
    branch_gain,
):
    tp_size = lax.axis_size("tp")
    seq_place = lax.axis_index("seq")
    tp_place = lax.axis_index("tp")
    first_core = (seq_place % 2) == 0
    first_tp = tp_place == 0
    core = seq_place % 2
    ring = Ring()
    chips = ring.chips
    local_rows, width = hidden.shape
    block_rows = local_rows * tp_size
    total_rows = span_starts.shape[0]
    query_heads = QH // tp_size
    span_width = WIN + block_rows + PIC
    scale = HD ** (-0.5)
    part = width // chips

    def ordered(flag, own, other, axis):
        return jnp.where(
            flag,
            jnp.concatenate([own, other], axis=axis),
            jnp.concatenate([other, own], axis=axis),
        )

    def halved(block):
        half = block.shape[1] // 2
        own = lax.dynamic_slice_in_dim(block, core * half, half, 1)
        other = lax.dynamic_slice_in_dim(block, (1 - core) * half, half, 1)
        return own, other

    def paired(own, other):
        return ordered(first_core, own, core_swap(other), 0)

    query_own, query_other = halved(query_weight)
    key_value_own = jnp.where(first_core, key_weight, value_weight)
    key_value_other = jnp.where(first_core, value_weight, key_weight)
    first_pack = paired(
        jnp.concatenate([query_own, key_value_own], axis=1),
        jnp.concatenate([query_other, key_value_other], axis=1),
    )
    small = jnp.concatenate([branch_gate, laurel_left, branch_output.T, laurel_right.T], axis=1)
    small = ordered(first_tp, small, tp_swap(small), 0)
    output_own, output_other = halved(output_weight.T)
    small_own, small_other = halved(small)
    second_pack = paired(
        jnp.concatenate([output_own, small_own], axis=1),
        jnp.concatenate([output_other, small_other], axis=1),
    )
    gate_pack = paired(*halved(gate_weight))
    upward_pack = paired(*halved(upward_weight))
    down_pack = paired(*halved(down_weight.T))

    half_chips = chips // 2
    first_chunks = ring.gathered(first_pack, half_chips)
    second_pack = after(second_pack, first_chunks[1])
    second_chunks = ring.gathered(second_pack, half_chips - 1)
    gate_pack, upward_pack = lax.optimization_barrier(
        (gate_pack, upward_pack, first_chunks[half_chips + 1], second_chunks[1])
    )[:2]
    gate_chunks = ring.gathered(gate_pack, half_chips)
    upward_chunks = ring.gathered(upward_pack, half_chips - 1)
    down_pack = after(down_pack, gate_chunks[half_chips + 1], upward_chunks[half_chips - 1])
    down_half = down_pack.shape[1] // 2
    down_chunks = [
        jnp.concatenate(pair, axis=1)
        for pair in zip(
            ring.gathered(down_pack[:, :down_half], half_chips),
            ring.gathered(down_pack[:, down_half:], half_chips - 1),
        )
    ]

    first_own = jnp.concatenate(first_chunks, axis=0)
    first_other = jnp.concatenate([core_swap(c) for c in first_chunks], axis=0)
    second_own = jnp.concatenate(second_chunks, axis=0)
    second_other = jnp.concatenate([core_swap(c) for c in second_chunks], axis=0)
    output_width = output_own.shape[1]
    side = branch_gate.shape[1]
    small_a = second_own[:, output_width:]
    small_b = second_other[:, output_width:]
    gate_side = jnp.where(first_core, small_a, small_b)
    output_side = jnp.where(first_core, small_b, small_a)
    branch_full, left_full = gate_side[:, :side], gate_side[:, side:]
    project_full, right_full = output_side[:, :side], output_side[:, side:]
    output_own_full = second_own[:, :output_width]
    output_other_full = second_other[:, :output_width]

    start_row = seq_place * block_rows
    local_place = jnp.arange(local_rows, dtype=jnp.int32)
    row_place = start_row + jnp.concatenate(
        [tp_place * local_rows + local_place, (1 - tp_place) * local_rows + local_place]
    )
    key_place = jnp.concatenate(
        [
            row_place - block_rows,
            row_place,
            start_row + block_rows + jnp.arange(PIC, dtype=jnp.int32),
        ]
    )
    padded_starts = jnp.concatenate(
        [jnp.full((block_rows,), -1, jnp.int32), span_starts, jnp.full((PIC,), -1, jnp.int32)]
    )

    def starts_of(block_start):
        halves = [
            lax.dynamic_slice_in_dim(padded_starts, block_start + t * local_rows, local_rows)
            for t in (tp_place, 1 - tp_place)
        ]
        return jnp.concatenate(halves)

    own_starts = starts_of(start_row + block_rows)
    key_starts = jnp.concatenate(
        [
            starts_of(start_row),
            own_starts,
            lax.dynamic_slice_in_dim(padded_starts, start_row + 2 * block_rows, PIC),
        ]
    )
    key_valid = (key_place >= 0) & (key_place < total_rows)
    distance = row_place[:, None] - key_place[None, :]
    window = (distance >= 0) & (distance < WIN)
    visible = key_valid[None, :] & (window | (own_starts[:, None] == key_starts[None, :]))
    frequency = ROPE_BASE ** (-(jnp.arange(HD // 2, dtype=WIDE) * 2.0) / HD)
    theta = row_place.astype(WIDE)[:, None] * frequency[None, :]
    cosines = jnp.cos(theta)[:, None, :]
    sines = jnp.sin(theta)[:, None, :]

    gains = jnp.stack(
        [input_gain, mixer_gain, laurel_gain, prefeed_gain, postfeed_gain, branch_gain]
    )
    gains = ring.to_relative(gains)
    input_gain, mixer_gain, laurel_gain, prefeed_gain, postfeed_gain, branch_gain = (
        gains[i] for i in range(6)
    )
    residual = ring.to_relative(hidden).astype(WIDE)
    upstream = ring.to_relative(cotangent).astype(WIDE)

    def tp_sum(peer, own):
        return own + tp_swap(peer.astype(LOW)).astype(WIDE)

    def tp_rows(block):
        return jnp.concatenate([block, tp_swap(block)], axis=0)

    def group_rows(block):
        pair = tp_rows(block)
        return jnp.concatenate([pair, core_swap(block), core_swap(pair[local_rows:])], axis=0)

    normed_in = normed(residual, input_gain)
    normed_low = normed_in.astype(LOW)
    rows_low = tp_rows(normed_low)
    query_cols = query_own.shape[1]
    raw_own = product(rows_low, first_own)
    raw_other = product(rows_low, first_other)
    query_raw = jnp.concatenate([raw_own[:, :query_cols], raw_other[:, :query_cols]], axis=1)
    query_raw = query_raw.reshape(block_rows, query_heads, HD)
    key_raw = jnp.where(first_core, raw_own[:, query_cols:], raw_other[:, query_cols:])
    value_low = jnp.where(first_core, raw_other[:, query_cols:], raw_own[:, query_cols:])
    value_low = value_low.astype(LOW)
    key_raw = key_raw.reshape(block_rows, 1, HD)
    query_low = rotary(normed(query_raw, query_gain), cosines, sines).astype(LOW)
    key_low = rotary(normed(key_raw, key_gain), cosines, sines).astype(LOW)
    pair_low = jnp.concatenate([key_low.reshape(block_rows, HD), value_low], axis=1)
    early = lax.dynamic_slice_in_dim(pair_low, tp_place * local_rows, PIC, 0)
    pairs_all = jnp.concatenate([shifted(pair_low, 1), pair_low, shifted(early, -1)], axis=0)
    keys_all = pairs_all[:, :HD]
    values_all = pairs_all[:, HD:]
    scores = jnp.einsum("qgd,pd->gqp", query_low, keys_all, preferred_element_type=WIDE) * scale
    scores = jnp.where(visible[None], scores, NEGATIVE)
    peak = jnp.max(scores, axis=-1, keepdims=True)
    log_total = peak + jnp.log(jnp.sum(jnp.exp(scores - peak), axis=-1, keepdims=True))
    weights_low = jnp.exp(scores - log_total).astype(LOW)
    attended = jnp.einsum("gqp,pd->qgd", weights_low, values_all, preferred_element_type=WIDE)
    attended_low = attended.reshape(block_rows, query_heads * HD).astype(LOW)

    def output_product(rows):
        return back_product(rows[:, :output_width], output_own_full) + back_product(
            rows[:, output_width:], output_other_full
        )

    mixer_raw = tp_sum(
        output_product(attended_low[local_rows:]), output_product(attended_low[:local_rows])
    )
    mixer_out = normed(mixer_raw, mixer_gain)
    laurel_mid = product(normed_low, left_full).astype(LOW)
    laurel_raw = back_product(laurel_mid, right_full)
    merged = (residual + mixer_out + normed_in + normed(laurel_raw, laurel_gain)) * HALF_ROOT
    dense_low = normed(merged, prefeed_gain).astype(LOW)

    dense_rows = group_rows(dense_low)
    gate_full = jnp.concatenate(gate_chunks, axis=0)
    upward_full = jnp.concatenate(upward_chunks, axis=0)
    gate_raw = product(dense_rows, gate_full)
    upward_raw = product(dense_rows, upward_full)
    gate_act = smooth_gate(gate_raw)
    inner_low = (gate_act * upward_raw).astype(LOW)

    def group_sum(make):
        far = core_swap(make(slice(block_rows, 2 * block_rows)).astype(LOW)).astype(WIDE)
        peer = make(slice(local_rows, block_rows)) + far[local_rows:]
        return tp_sum(peer, make(slice(0, local_rows)) + far[:local_rows])

    def dense_part(offsets):
        weight = jnp.concatenate([down_chunks[o] for o in offsets], axis=0)
        return group_sum(lambda rows: back_product(inner_low[rows], weight))

    near = 1
    groups = [[chips - 1, 0, 1]]
    while near + 1 < half_chips:
        near += 1
        groups.append([chips - near, near])
    groups.append([half_chips])
    dense_parts = [None] * chips
    for group in groups:
        summed = dense_part(group)
        for i, o in enumerate(group):
            dense_parts[o] = summed[:, i * part : (i + 1) * part]
    dense_raw = jnp.concatenate(dense_parts, axis=1)
    middle = merged + normed(dense_raw, postfeed_gain)
    middle_low = middle.astype(LOW)
    branch_raw = product(middle_low, branch_full)
    side_input = layer_input.astype(WIDE)
    branch_act = smooth_gate(branch_raw)
    branch_low = (branch_act * side_input).astype(LOW)
    project_raw = back_product(branch_low, project_full)
    result = (middle + normed(project_raw, branch_gain)).astype(LOW)

    project_back, branch_slope = normed_back(project_raw, branch_gain, upstream)
    project_low = project_back.astype(LOW)
    branch_low_back = product(project_low, project_full)
    layer_delta = branch_low_back * branch_act
    branch_raw_back = gate_back(branch_raw, branch_low_back * side_input).astype(LOW)
    middle_back = upstream + back_product(branch_raw_back, branch_full)
    dense_raw_back, postfeed_slope = normed_back(dense_raw, postfeed_gain, middle_back)
    dense_rows_back = group_rows(dense_raw_back.astype(LOW))
    down_full = jnp.concatenate(down_chunks, axis=0)
    inner_back = product(dense_rows_back, down_full)
    gate_raw_back = gate_back(gate_raw, inner_back * upward_raw).astype(LOW)
    upward_raw_back = (inner_back * gate_act).astype(LOW)

    def sliced(block, offset):
        return block[:, offset * part : (offset + 1) * part]

    down_delta = ring.scattered(
        lambda o: outer_sum(sliced(dense_rows_back, o), inner_low), half_chips
    )
    gate_delta = ring.scattered(
        lambda o: outer_sum(sliced(dense_rows, o), gate_raw_back), half_chips - 1
    )
    upward_delta = ring.scattered(
        lambda o: outer_sum(sliced(dense_rows, o), upward_raw_back), half_chips
    )
    dense_in_back = group_sum(
        lambda rows: back_product(gate_raw_back[rows], gate_full)
        + back_product(upward_raw_back[rows], upward_full)
    )
    merged_extra, prefeed_slope = normed_back(merged, prefeed_gain, dense_in_back)
    summed_back = (middle_back + merged_extra) * HALF_ROOT
    mixer_raw_back, mixer_slope = normed_back(mixer_raw, mixer_gain, summed_back)
    mixer_rows_back = tp_rows(mixer_raw_back.astype(LOW))
    laurel_raw_back, laurel_slope = normed_back(laurel_raw, laurel_gain, summed_back)
    laurel_raw_low = laurel_raw_back.astype(LOW)
    laurel_mid_back = product(laurel_raw_low, right_full).astype(LOW)

    attended_back = jnp.concatenate(
        [product(mixer_rows_back, output_own_full), product(mixer_rows_back, output_other_full)],
        axis=1,
    ).astype(LOW)
    attended_back = attended_back.reshape(block_rows, query_heads, HD)

    def second_terms(o):
        rows = sliced(mixer_rows_back, o)
        gate_like = jnp.concatenate(
            [
                outer_sum(sliced(middle_low, o), branch_raw_back),
                outer_sum(sliced(normed_low, o), laurel_mid_back),
            ],
            axis=1,
        )
        output_like = jnp.concatenate(
            [
                outer_sum(sliced(project_low, o), branch_low),
                outer_sum(sliced(laurel_raw_low, o), laurel_mid),
            ],
            axis=1,
        )
        own = jnp.concatenate(
            [
                outer_sum(rows, attended_low[:, :output_width]),
                jnp.where(first_core, gate_like, output_like),
            ],
            axis=1,
        )
        other = jnp.concatenate(
            [
                outer_sum(rows, attended_low[:, output_width:]),
                jnp.where(first_core, output_like, gate_like),
            ],
            axis=1,
        )
        return own + core_swap(other.astype(LOW)).astype(WIDE)

    second_delta = ring.scattered(second_terms, half_chips)

    scores_again = (
        jnp.einsum("qgd,pd->gqp", query_low, keys_all, preferred_element_type=WIDE) * scale
    )
    scores_again = jnp.where(visible[None], scores_again, NEGATIVE)
    weights_again = jnp.exp(scores_again - log_total)
    weights_back = jnp.einsum(
        "qgd,pd->gqp", attended_back, values_all, preferred_element_type=WIDE
    )
    values_back = jnp.einsum(
        "gqp,qgd->pd", weights_low, attended_back, preferred_element_type=WIDE
    )
    centre = jnp.sum(weights_again * weights_back, axis=-1, keepdims=True)
    scores_back = (weights_again * (weights_back - centre)).astype(LOW)
    query_back = (
        jnp.einsum("gqp,pd->qgd", scores_back, keys_all, preferred_element_type=WIDE) * scale
    )
    keys_back = (
        jnp.einsum("gqp,qgd->pd", scores_back, query_low, preferred_element_type=WIDE) * scale
    )
    pairs_back = jnp.concatenate([keys_back, values_back], axis=1)
    later = shifted(pairs_back[:block_rows].astype(LOW), -1).astype(WIDE)
    earlier = shifted(pairs_back[2 * block_rows :].astype(LOW), 1).astype(WIDE)
    own_back = pairs_back[block_rows : 2 * block_rows] + later
    nothing = jnp.zeros((block_rows - PIC, 2 * HD), WIDE)
    own_back = own_back + ordered(first_tp, earlier, nothing, 0)
    value_raw_low = own_back[:, HD:].astype(LOW)
    key_rot_back = own_back[:, :HD].reshape(block_rows, 1, HD)
    key_raw_back, key_slope = normed_back(key_raw, key_gain, rotary(key_rot_back, cosines, -sines))
    query_raw_back, query_slope = normed_back(
        query_raw, query_gain, rotary(query_back, cosines, -sines)
    )
    query_raw_low = query_raw_back.reshape(block_rows, query_heads * HD).astype(LOW)
    key_raw_low = key_raw_back.reshape(block_rows, HD).astype(LOW)
    first_own_back = jnp.concatenate(
        [query_raw_low[:, :query_cols], jnp.where(first_core, key_raw_low, value_raw_low)], axis=1
    )
    first_other_back = jnp.concatenate(
        [query_raw_low[:, query_cols:], jnp.where(first_core, value_raw_low, key_raw_low)], axis=1
    )

    def first_terms(o):
        rows = sliced(rows_low, o)
        other = core_swap(outer_sum(rows, first_other_back).astype(LOW)).astype(WIDE)
        return outer_sum(rows, first_own_back) + other

    first_delta = ring.scattered(first_terms, half_chips - 1)

    def rows_back(rows):
        return back_product(first_own_back[rows], first_own) + back_product(
            first_other_back[rows], first_other
        )

    normed_total = (
        tp_sum(rows_back(slice(local_rows, block_rows)), rows_back(slice(0, local_rows)))
        + back_product(laurel_mid_back, left_full)
        + summed_back
    )
    input_back, input_slope = normed_back(residual, input_gain, normed_total)
    hidden_delta = summed_back + input_back

    core_rows = part // 2

    def unpaired(block):
        own = lax.dynamic_slice_in_dim(block, core * core_rows, core_rows, 0)
        other = lax.dynamic_slice_in_dim(block, (1 - core) * core_rows, core_rows, 0)
        return own, core_swap(other.astype(LOW)).astype(WIDE)

    gate_delta = ordered(first_core, *unpaired(gate_delta), 1)
    upward_delta = ordered(first_core, *unpaired(upward_delta), 1)
    down_delta = ordered(first_core, *unpaired(down_delta), 1).T
    first_mine, first_theirs = unpaired(first_delta)
    query_delta = ordered(first_core, first_mine[:, :query_cols], first_theirs[:, :query_cols], 1)
    key_delta = jnp.where(first_core, first_mine[:, query_cols:], first_theirs[:, query_cols:])
    value_delta = jnp.where(first_core, first_theirs[:, query_cols:], first_mine[:, query_cols:])
    second_mine, second_theirs = unpaired(second_delta)
    output_delta = ordered(
        first_core, second_mine[:, :output_width], second_theirs[:, :output_width], 1
    ).T
    small_delta = ordered(
        first_core, second_mine[:, output_width:], second_theirs[:, output_width:], 1
    )
    small_rows = core_rows // 2
    kept = lax.dynamic_slice_in_dim(small_delta, tp_place * small_rows, small_rows, 0)
    given = lax.dynamic_slice_in_dim(small_delta, (1 - tp_place) * small_rows, small_rows, 0)
    small_delta = tp_sum(given, kept)
    rank = laurel_left.shape[1]
    branch_delta = small_delta[:, :side]
    left_delta = small_delta[:, side : side + rank]
    project_delta = small_delta[:, side + rank : 2 * side + rank].T
    right_delta = small_delta[:, 2 * side + rank :].T

    slopes = ring.from_relative(
        jnp.stack(
            [
                input_slope,
                mixer_slope,
                laurel_slope,
                prefeed_slope,
                postfeed_slope,
                branch_slope,
            ]
        )
    )
    slopes = jnp.concatenate(
        [slopes, jnp.pad(jnp.concatenate([query_slope, key_slope]), (0, width - 2 * HD))[None]]
    )
    bit = 1
    while bit < lax.axis_size("seq"):
        slopes = slopes + lax.ppermute(
            slopes, "seq", [(i, i ^ bit) for i in range(lax.axis_size("seq"))]
        )
        bit *= 2
    slopes = slopes + tp_swap(slopes)
    return (
        ring.from_relative(result),
        ring.from_relative(hidden_delta),
        layer_delta,
        query_delta,
        key_delta,
        value_delta,
        output_delta,
        left_delta,
        right_delta,
        gate_delta,
        upward_delta,
        down_delta,
        branch_delta,
        project_delta,
        slopes[0],
        slopes[6, :HD],
        slopes[6, HD : 2 * HD],
        slopes[1],
        slopes[2],
        slopes[3],
        slopes[4],
        slopes[5],
    )


def solution(mesh):
    tokens = P(("seq", "tp"), None)
    spread = P(None, ("seq", "tp"))
    inward = P("seq", "tp")
    outward = P("tp", "seq")
    weights = (
        inward,
        inward,
        inward,
        outward,
        tokens,
        spread,
        inward,
        inward,
        outward,
        tokens,
        spread,
    )
    return jax.shard_map(
        shards,
        mesh=mesh,
        in_specs=(tokens, tokens, tokens, P()) + weights + (P(),) * 8,
        out_specs=(tokens, tokens, tokens) + weights + (P(),) * 8,
        check_vma=False,
    )
```

```python
import jax
import jax.numpy as jnp
from jax import lax
from jax.experimental import pallas as pl
from jax.experimental.pallas import tpu as pltpu
from jax.sharding import PartitionSpec as P

QH = 8
KVH = 2
HD = 256
WIN = 512
PIC = 256


EPSILON = 1e-06
HALF_ROOT = 0.7071067811865476
ROPE_BASE = 10000.0
NEGATIVE = -1e30
GELU_SCALE = 0.7978845608028654
GELU_CUBE = 0.044715

LOW = jnp.bfloat16
WIDE = jnp.float32
VMEM_LIMIT = 56 * 2**20


def normed(value, gain):
    return value * lax.rsqrt(jnp.mean(value * value, axis=-1, keepdims=True) + EPSILON) * gain


def normed_back(value, gain, upstream):
    _, pullback = jax.vjp(normed, value, gain)
    return pullback(upstream)


def smooth_gate(value):
    return (
        0.5 * value * (1.0 + jnp.tanh(GELU_SCALE * (value + GELU_CUBE * value * value * value)))
    )


def gate_back(value, upstream):
    _, pullback = jax.vjp(smooth_gate, value)
    return pullback(upstream)[0]


def rotary(value, cosines, sines):
    half = value.shape[-1] // 2
    first = value[..., :half]
    second = value[..., half:]
    return jnp.concatenate(
        [first * cosines - second * sines, second * cosines + first * sines], axis=-1
    )


def product(left, right):
    return jnp.dot(left, right, preferred_element_type=WIDE)


def outer_sum(left, right):
    return lax.dot_general(left, right, (((0,), (0,)), ((), ())), preferred_element_type=WIDE)


def back_product(left, right):
    return lax.dot_general(left, right, (((1,), (1,)), ((), ())), preferred_element_type=WIDE)


def shape_of(shape, kind):
    return jax.ShapeDtypeStruct(shape, kind)


def kernel_call(body, name, grid, inputs, outputs, scratch=(), flops=0, prefetch=None):
    def spec(entry):
        array, block, where = entry
        if block is None:
            rank = len(array.shape)
            return pl.BlockSpec(array.shape, lambda *_, rank=rank: (0,) * rank)
        return pl.BlockSpec(block, where)

    moved = sum(a.size * a.dtype.itemsize for a, _, _ in list(inputs) + list(outputs))
    call = pl.pallas_call(
        body,
        grid_spec=pltpu.PrefetchScalarGridSpec(
            num_scalar_prefetch=0 if prefetch is None else 1,
            grid=grid,
            in_specs=[spec(e) for e in inputs],
            out_specs=[spec(e) for e in outputs],
            scratch_shapes=list(scratch),
        ),
        out_shape=[shape_of(a.shape, a.dtype) for a, _, _ in outputs],
        compiler_params=pltpu.CompilerParams(
            dimension_semantics=("arbitrary",) * len(grid), vmem_limit_bytes=VMEM_LIMIT
        ),
        cost_estimate=pl.CostEstimate(flops=0, bytes_accessed=0, transcendentals=0),
        name=name,
    )
    operands = [a for a, _, _ in inputs]
    return call(*operands) if prefetch is None else call(prefetch, *operands)


def permuted(arrays, kinds, table, inverse=False):
    count = table.shape[0]
    part = arrays[0].shape[1] // count
    if part % 128:
        if inverse:
            table = jnp.argsort(table)
        results = []
        for array, kind in zip(arrays, kinds):
            parts = [
                lax.dynamic_slice_in_dim(array, table[j] * part, part, 1) for j in range(count)
            ]
            results.append(jnp.concatenate(parts, axis=1).astype(kind))
        return results

    def body(table_ref, *refs):
        for source, target in zip(refs[: len(arrays)], refs[len(arrays) :]):
            for j in range(count):
                here = pl.ds(j * part, part)
                there = pl.ds(pl.multiple_of(table_ref[j] * part, part), part)
                before, behind = (here, there) if inverse else (there, here)
                target[:, behind] = source[:, before].astype(target.dtype)

    return kernel_call(
        body,
        "permuted",
        (1,),
        [(a, None, None) for a in arrays],
        [(shape_of(a.shape, k), None, None) for a, k in zip(arrays, kinds)],
        prefetch=table,
    )


def permuted_rows(array, table, widths, inverse=False):
    count = table.shape[0]
    part = array.shape[0] // count

    def body(table_ref, source, *targets):
        for j in range(count):
            here = pl.ds(j * part, part)
            there = pl.ds(pl.multiple_of(table_ref[j] * part, part), part)
            before, behind = (here, there) if inverse else (there, here)
            at = 0
            for target, wide in zip(targets, widths):
                target[behind, :] = source[before, at : at + wide]
                at += wide

    outs = [(shape_of((array.shape[0], w), array.dtype), None, None) for w in widths]
    return kernel_call(body, "permuted_rows", (1,), [(array, None, None)], outs, prefetch=table)


def weights_given(core, weights):
    rows = weights[0].shape[0]
    halves = [w.shape[1] // 2 for w in weights]

    def body(core_ref, *refs):
        at = 0
        for half, ref in zip(halves, refs):
            refs[-1][:, at : at + half] = ref[...]
            at += half

    return kernel_call(
        body,
        "weights_given",
        (1,),
        [
            (w, (rows, half), lambda _, core_ref: (0, 1 - core_ref[0]))
            for w, half in zip(weights, halves)
        ],
        [(shape_of((rows, sum(halves)), LOW), None, None)],
        prefetch=core,
    )[0]


def weights_merged(core, weights, theirs, groups):
    rows = weights[0].shape[0]
    halves = [w.shape[1] // 2 for w in weights]

    def body(core_ref, *refs):
        other = refs[len(weights)]
        outs = refs[len(weights) + 1 :]
        mine = pl.ds(pl.multiple_of(core_ref[0] * rows, rows), rows)
        given = pl.ds(pl.multiple_of((1 - core_ref[0]) * rows, rows), rows)
        at = 0
        for out, group in zip(outs, groups):
            column = 0
            for i in group:
                wide = halves[i]
                out[mine, column : column + wide] = refs[i][...]
                out[given, column : column + wide] = other[:, at : at + wide]
                column += wide
                at += wide

    return kernel_call(
        body,
        "weights_merged",
        (1,),
        [
            (w, (rows, half), lambda _, core_ref: (0, core_ref[0]))
            for w, half in zip(weights, halves)
        ]
        + [(theirs, None, None)],
        [
            (shape_of((2 * rows, sum(halves[i] for i in group)), LOW), None, None)
            for group in groups
        ],
        prefetch=core,
    )


def expanded(rows, gates, ups, hidden_units):
    tile = 512
    count = len(gates)
    part = gates[0][0].shape[0]

    def body(rows_ref, *refs):
        gate_refs, up_refs = refs[:count], refs[count : 2 * count]
        gate_out, up_out, inner_out = refs[2 * count :]
        x = rows_ref[...]
        gate = product(x, jnp.concatenate([r[...] for r in gate_refs], axis=0))
        up = product(x, jnp.concatenate([r[...] for r in up_refs], axis=0))
        gate_out[...] = gate.astype(LOW)
        up_out[...] = up.astype(LOW)
        inner_out[...] = (smooth_gate(gate) * up).astype(LOW)

    chunks = [
        (a, (part, tile), lambda j, first=first // tile: (0, first + j)) for a, first in gates + ups
    ]
    out = (shape_of((rows.shape[0], hidden_units), LOW), (rows.shape[0], tile), lambda j: (0, j))
    return kernel_call(
        body,
        "expanded",
        (hidden_units // tile,),
        [(rows, None, None)] + chunks,
        [out] * 3,
        flops=4 * rows.size * hidden_units,
    )


def contracted(inner, first_row, row_count, chunks, kind):
    units = inner.shape[1]
    flat = [a for chunk in chunks for a in chunk]
    part = flat[0].shape[0]
    block = min(row_count, 256)

    def body(inner_ref, *refs):
        out_ref = refs[-1]
        at = 0
        for i, chunk in enumerate(chunks):
            column = 0
            total = None
            for a in chunk:
                wide = a.shape[1]
                term = back_product(inner_ref[:, column : column + wide], refs[at][...])
                total = term if total is None else total + term
                column += wide
                at += 1
            out_ref[:, i * part : (i + 1) * part] = total.astype(out_ref.dtype)

    start = first_row // block
    return kernel_call(
        body,
        "contracted",
        (row_count // block,),
        [(inner, (block, units), lambda i: (start + i, 0))] + [(a, None, None) for a in flat],
        [
            (
                shape_of((row_count, part * len(chunks)), kind),
                (block, part * len(chunks)),
                lambda i: (i, 0),
            )
        ],
        flops=2 * row_count * units * part * len(chunks),
    )[0]


def inner_pulled(rows, chunks, gate, up):
    tile = 512
    count, units = gate.shape
    steps = units // tile
    flat, kinds = [], []
    for chunk in chunks:
        for i, a in enumerate(chunk):
            first = 0 if i == 0 else steps - a.shape[1] // tile
            last = a.shape[1] // tile - 1
            flat.append(
                (
                    a,
                    (a.shape[0], tile),
                    lambda j, first=first, last=last: (0, jnp.clip(j - first, 0, last)),
                )
            )

    def body(rows_ref, *refs):
        chunk_refs = refs[: len(flat)]
        gate_ref, up_ref, gate_out, up_out = refs[len(flat) :]
        step = pl.program_id(0)
        parts = []
        at = 0
        for chunk in chunks:
            value = chunk_refs[at][...]
            if len(chunk) == 2:
                value = jnp.where(
                    step < chunk[0].shape[1] // tile, value, chunk_refs[at + 1][...]
                )
            parts.append(value)
            at += len(chunk)
        pulled = product(rows_ref[...], jnp.concatenate(parts, axis=0))
        value = gate_ref[...].astype(WIDE)
        square = value * value
        bent = jnp.tanh(GELU_SCALE * (value + GELU_CUBE * value * square))
        slope = 0.5 * (1.0 + bent) + 0.5 * value * (1.0 - bent * bent) * GELU_SCALE * (
            1.0 + 3.0 * GELU_CUBE * square
        )
        gate_out[...] = (pulled * up_ref[...].astype(WIDE) * slope).astype(LOW)
        up_out[...] = (pulled * (0.5 * value * (1.0 + bent))).astype(LOW)

    block = ((count, tile), lambda j: (0, j))
    return kernel_call(
        body,
        "inner_pulled",
        (steps,),
        [(rows, None, None)] + flat + [(gate,) + block, (up,) + block],
        [(gate,) + block] * 2,
        flops=2 * rows.size * units,
    )


def rows_pulled(gate_back_low, up_back_low, first_row, row_count, gates, ups, kind):
    tile = 1024
    units = gate_back_low.shape[1]
    count = len(gates)
    part = gates[0][0].shape[0]
    width = part * count
    steps = units // tile
    start = first_row // row_count

    def body(gate_ref, up_ref, *refs):
        out_ref, total_ref = refs[-2:]
        step = pl.program_id(0)
        term = back_product(
            gate_ref[...], jnp.concatenate([r[...] for r in refs[:count]], axis=0)
        ) + back_product(
            up_ref[...], jnp.concatenate([r[...] for r in refs[count : 2 * count]], axis=0)
        )

        @pl.when(step == 0)
        def _():
            total_ref[...] = term

        @pl.when((step > 0) & (step < steps - 1))
        def _():
            total_ref[...] += term

        @pl.when(step == steps - 1)
        def _():
            out_ref[...] = (total_ref[...] + term).astype(out_ref.dtype)

    chunks = [
        (a, (part, tile), lambda k, first=first // tile: (0, first + k)) for a, first in gates + ups
    ]
    left = ((row_count, tile), lambda k: (start, k))
    return kernel_call(
        body,
        "rows_pulled",
        (steps,),
        [(gate_back_low,) + left, (up_back_low,) + left] + chunks,
        [(shape_of((row_count, width), kind), None, None)],
        scratch=[pltpu.VMEM((row_count, width), WIDE)],
        flops=4 * row_count * units * width,
    )[0]


def one_term(offset, part, left, right, added, first=0, count=None):
    rows = left.shape[0]
    count = right.shape[1] if count is None else count
    tile = max(t for t in (256, 512, 1024) if count % t == 0 and first % t == 0)

    def body(left_ref, right_ref, *refs):
        turn = refs[-1]

        @pl.when(pl.program_id(0) == 0)
        def _():
            turn[...] = left_ref[...].T

        total = product(turn[...], right_ref[...])
        if added is not None:
            total = total + refs[0][...].astype(WIDE)
        refs[-2][...] = total.astype(LOW)

    inputs = [
        (left, (rows, part), lambda j: (0, offset)),
        (right, (rows, tile), lambda j: (0, first // tile + j)),
    ]
    if added is not None:
        inputs.append((added, (part, tile), lambda j: (offset, first // tile + j)))
    return kernel_call(
        body,
        "one_term",
        (count // tile,),
        inputs,
        [(shape_of((part, count), LOW), (part, tile), lambda j: (0, j))],
        scratch=[pltpu.VMEM((part, rows), LOW)],
    )[0]


def last_term(core, part, left, right, added, front, back, first):
    rows = left.shape[0]
    count = right.shape[1]
    half = part // 2
    if part % 128:
        total = outer_sum(left[:, :part], right)
        if added is not None:
            total = total + added[:part].astype(WIDE)
        total = total + front[:, first : first + count].astype(WIDE)
        total = total + back[:, first : first + count].astype(WIDE)
        kept = lax.dynamic_slice_in_dim(total, core[0] * half, half, 0)
        given = lax.dynamic_slice_in_dim(total, (1 - core[0]) * half, half, 0)
        return kept, given.astype(LOW)
    tile = 256

    def body(core_ref, left_ref, right_ref, front_ref, back_ref, *refs):
        kept_ref, given_ref, turn, total_ref = refs[-4:]

        @pl.when(pl.program_id(0) == 0)
        def _():
            turn[...] = left_ref[...].T

        total = product(turn[...], right_ref[...])
        total = total + front_ref[...].astype(WIDE) + back_ref[...].astype(WIDE)
        if added is not None:
            total = total + refs[0][...].astype(WIDE)
        total_ref[...] = total
        kept_ref[...] = total_ref[pl.ds(pl.multiple_of(core_ref[0] * half, half), half), :]
        given = pl.ds(pl.multiple_of((1 - core_ref[0]) * half, half), half)
        given_ref[...] = total_ref[given, :].astype(LOW)

    for size in (512, 1024):
        if count % size == 0 and first % size == 0:
            tile = size
    inputs = [
        (left, (rows, part), lambda j, _: (0, 0)),
        (right, (rows, tile), lambda j, _: (0, j)),
        (front, (part, tile), lambda j, _: (0, first // tile + j)),
        (back, (part, tile), lambda j, _: (0, first // tile + j)),
    ]
    if added is not None:
        inputs.append((added, (part, tile), lambda j, _: (0, j)))
    block = ((half, tile), lambda j, _: (0, j))
    return kernel_call(
        body,
        "last_term",
        (count // tile,),
        inputs,
        [(shape_of((half, count), WIDE),) + block, (shape_of((half, count), LOW),) + block],
        scratch=[pltpu.VMEM((part, rows), LOW), pltpu.VMEM((part, tile), WIDE)],
        prefetch=core,
    )


def assembled(core, kept, theirs, turned_over=False):
    rows, half = kept.shape

    def body(core_ref, kept_ref, theirs_ref, out_ref):
        mine = (pl.program_id(0) == core_ref[0]).astype(WIDE)
        value = kept_ref[...] * mine + theirs_ref[...].astype(WIDE) * (1.0 - mine)
        out_ref[...] = value.T if turned_over else value

    if turned_over:
        out = (shape_of((2 * half, rows), WIDE), (half, rows), lambda j, _: (j, 0))
    else:
        out = (shape_of((rows, 2 * half), WIDE), (rows, half), lambda j, _: (0, j))
    return kernel_call(
        body, "assembled", (2,), [(kept, None, None), (theirs, None, None)], [out], prefetch=core
    )[0]


def rowwise(body, name, row_inputs, whole_inputs, row_outputs, sum_outputs, block=64):
    count = row_inputs[0].shape[0]
    block = min(block, count)
    taken = len(row_inputs) + len(whole_inputs)

    def run(*refs):
        results = body(*(r[...] for r in refs[:taken]))
        outs = refs[taken:]
        for ref, value in zip(outs, results[: len(row_outputs)]):
            ref[...] = value.astype(ref.dtype)
        for ref, value in zip(outs[len(row_outputs) :], results[len(row_outputs) :]):

            @pl.when(pl.program_id(0) == 0)
            def _(ref=ref, value=value):
                ref[...] = value

            @pl.when(pl.program_id(0) > 0)
            def _(ref=ref, value=value):
                ref[...] += value

    def strip(shape):
        return ((block,) + shape[1:], lambda i: (i, 0))

    return kernel_call(
        run,
        name,
        (count // block,),
        [(a,) + strip(a.shape) for a in row_inputs] + [(a, None, None) for a in whole_inputs],
        [(shape_of((count, w), k),) + strip((count, w)) for w, k in row_outputs]
        + [(shape_of((1, w), WIDE), None, None) for w in sum_outputs],
    )


def stacked(*pieces):
    rows = sum(p.shape[0] for p in pieces)

    def body(*refs):
        at = 0
        for ref, piece in zip(refs, pieces):
            refs[-1][at : at + piece.shape[0], :] = ref[...]
            at += piece.shape[0]

    out = (shape_of((rows, pieces[0].shape[1]), pieces[0].dtype), None, None)
    return kernel_call(body, "stacked", (1,), [(p, None, None) for p in pieces], [out])[0]


def joined_chunks(chunks, first, count):
    part = chunks[0][0].shape[0]

    def body(*refs):
        for i, ref in enumerate(refs[:-1]):
            start = chunks[i][1] + first
            refs[-1][i * part : (i + 1) * part, :] = ref[:, start : start + count]

    out = (shape_of((part * len(chunks), count), LOW), None, None)
    return kernel_call(
        body, "joined_chunks", (1,), [(a, None, None) for a, _ in chunks], [out]
    )[0]


def multiplied(left, right, kind=WIDE):
    rows = left.shape[0]
    block = min(rows, 256)

    def body(left_ref, right_ref, out_ref):
        out_ref[...] = product(left_ref[...], right_ref[...]).astype(out_ref.dtype)

    return kernel_call(
        body,
        "multiplied",
        (rows // block,),
        [(left, (block, left.shape[1]), lambda i: (i, 0)), (right, None, None)],
        [(shape_of((rows, right.shape[1]), kind), (block, right.shape[1]), lambda i: (i, 0))],
    )[0]


def turned_products(pairs, kind):
    width = sum(right.shape[1] for _, right in pairs)
    tall = pairs[0][0].shape[1]
    block = 512
    rows = pairs[0][0].shape[0]

    def body(*refs):
        at = 0
        for i in range(len(pairs)):
            wide = pairs[i][1].shape[1]
            term = outer_sum(refs[2 * i][...], refs[2 * i + 1][...])
            refs[-1][:, at : at + wide] = term.astype(kind)
            at += wide

    inputs = []
    for left, right in pairs:
        inputs.append((left, (left.shape[0], block), lambda i: (0, i)))
        inputs.append((right, None, None))
    out = (shape_of((tall, width), kind), (block, width), lambda i: (i, 0))
    return kernel_call(body, "turned_products", (tall // block,), inputs, [out])[0]


def ring_terms(segments, part, ahead, behind, front, back, cut):
    width = sum(right.shape[1] for _, right, _ in segments)

    def plain(offset, received, first):
        columns = slice(offset * part, (offset + 1) * part)
        parts = []
        for left, right, added in segments:
            term = outer_sum(left[:, columns], right)
            if added is not None:
                term = term + added[columns].astype(WIDE)
            parts.append(term)
        total = jnp.concatenate(parts, axis=1)
        if received is not None:
            edge = (first, width - first - received.shape[1])
            total = total + jnp.pad(received.astype(WIDE), ((0, 0), edge))
        return total.astype(LOW)

    edges = [right.shape[1] for _, right, _ in segments]
    if part % 128:
        if front is None:
            return plain(ahead, None, 0)[:, :cut], plain(behind, None, 0)[:, cut:]
        return plain(ahead, front, 0), plain(behind, back, width - back.shape[1])
    if front is None:
        pair = segments
        if len(segments) == 1:
            left, right, added = segments[0]
            pair = [(left, right, added, 0, cut), (left, right, added, cut, width - cut)]
        return [one_term(ahead, part, *entry) for entry in pair]

    edges += [front.shape[1], width - back.shape[1]]
    tile = max(t for t in (256, 512, 1024) if all(e % t == 0 for e in edges))
    steps = width // tile
    front_steps, back_first = front.shape[1] // tile, steps - back.shape[1] // tile
    inputs, scratch, spans = [], [], []
    at = 0
    for left, right, added in segments:
        rows = left.shape[0]
        size = right.shape[1] // tile

        def column(j, at=at, size=size):
            return jnp.clip(j - at, 0, size - 1)

        inputs.append((left, (rows, part), lambda j: (0, ahead)))
        inputs.append((left, (rows, part), lambda j: (0, behind)))
        inputs.append((right, (rows, tile), lambda j, column=column: (0, column(j))))
        if added is not None:
            inputs.append((added, (part, tile), lambda j, column=column: (ahead, column(j))))
            inputs.append((added, (part, tile), lambda j, column=column: (behind, column(j))))
        same = [i for i, (other, _, _) in enumerate(segments) if other is left][0]
        scratch.append(pltpu.VMEM((2, part, rows) if len(spans) == same else (8, 128), LOW))
        spans.append((at, at + size, added is not None, same))
        at += size
    inputs.append((front, (part, tile), lambda j: (0, jnp.clip(j, 0, front_steps - 1))))
    inputs.append((back, (part, tile), lambda j: (0, jnp.clip(j - back_first, 0, steps))))

    def body(*refs):
        refs = list(refs)
        turned = refs[len(inputs) + 2 :]
        front_ref, back_ref = refs[len(inputs) - 2 : len(inputs)]
        outs = refs[len(inputs) : len(inputs) + 2]
        step = pl.program_id(0)
        had_front = (step < front_steps).astype(WIDE)
        had_back = (step >= back_first).astype(WIDE)
        place = 0
        for at, (first, last, adds, same) in enumerate(spans):
            mine = refs[place : place + (5 if adds else 3)]
            place += len(mine)
            turn = turned[same]

            if same == at:

                @pl.when(step == 0)
                def _(mine=mine, turn=turn):
                    turn[0] = mine[0][...].T
                    turn[1] = mine[1][...].T

            @pl.when((step >= first) & (step < last))
            def _(mine=mine, turn=turn, adds=adds):
                right = mine[2][...]
                for way, received, had in ((0, front_ref, had_front), (1, back_ref, had_back)):
                    total = product(turn[way], right) + received[...].astype(WIDE) * had
                    if adds:
                        total = total + mine[3 + way][...].astype(WIDE)
                    outs[way][...] = total.astype(LOW)

    out = (shape_of((part, width), LOW), (part, tile), lambda j: (0, j))
    flops = sum(4 * part * right.size for _, right, _ in segments)
    return kernel_call(
        body, "ring_terms", (steps,), inputs, [out, out], scratch=scratch, flops=flops
    )


def turned(value, gain, cosines, sines):
    scale = lax.rsqrt(jnp.mean(value * value, axis=-1, keepdims=True) + EPSILON)
    return rotary(value * scale * gain, cosines, sines).astype(LOW), scale


def hidden_scores(places):
    query_place, query_start, key_place, key_start, total_rows = places
    distance = query_place - key_place
    near = (distance >= 0) & (distance < WIN)
    visible = (key_place >= 0) & (key_place < total_rows) & (near | (query_start == key_start))
    return jnp.where(visible, 0.0, NEGATIVE)


def head_specs(own, other, heads_own):
    rows = own.shape[0]
    return [
        (own, (rows, HD), lambda h: (0, jnp.minimum(h, heads_own - 1))),
        (other, (rows, HD), lambda h: (0, jnp.maximum(h - heads_own, 0))),
    ]


def attention(own, other, heads, gain, cosines, sines, keys, values, places, total_rows):
    rows = own.shape[0]
    heads_own = heads // 2
    scale = HD ** (-0.5)

    def body(own_ref, other_ref, gain_ref, cos_ref, sin_ref, pair_ref, qp, qs, kp, ks, out_own, out_other, log_ref, hide_ref):
        head = pl.program_id(0)

        @pl.when(head == 0)
        def _():
            hide_ref[...] = hidden_scores((qp[...], qs[...], kp[...], ks[...], total_rows))

        raw = jnp.where(head < heads_own, own_ref[...], other_ref[...])
        query, _ = turned(raw, gain_ref[...], cos_ref[...], sin_ref[...])
        scores = back_product(pair_ref[:, :HD], query) * scale + hide_ref[...]
        peak = jnp.max(scores, axis=0, keepdims=True)
        log_total = peak + jnp.log(jnp.sum(jnp.exp(scores - peak), axis=0, keepdims=True))
        weights = jnp.exp(scores - log_total).astype(LOW)
        result = outer_sum(weights, pair_ref[:, HD:]).astype(LOW)
        log_ref[0] = log_total

        @pl.when(head < heads_own)
        def _():
            out_own[...] = result

        @pl.when(head >= heads_own)
        def _():
            out_other[...] = result

    whole = [(a, None, None) for a in (gain, cosines, sines, keys) + tuple(places)]
    half = shape_of((rows, heads_own * HD), LOW)
    return kernel_call(
        body,
        "attention",
        (heads,),
        head_specs(own, other, heads_own) + whole,
        head_specs(half, half, heads_own)
        + [(shape_of((heads, 1, rows), WIDE), (1, 1, rows), lambda h: (h, 0, 0))],
        scratch=[pltpu.VMEM((keys.shape[0], rows), WIDE)],
    )


def attention_back(own, other, heads, gain, cosines, sines, keys, places, total_rows, log_total, upstream, weights_own, weights_other):
    rows = own.shape[0]
    heads_own = heads // 2
    scale = HD ** (-0.5)
    tail = keys.shape[0] - 2 * rows

    def body(own_ref, other_ref, weight_own, weight_other, gain_ref, cos_ref, sin_ref, pair_ref, up_ref, qp, qs, kp, ks, log_ref, query_own, query_other, before_out, here_out, after_out, slope_out, hide_ref, total_ref):
        head = pl.program_id(0)

        @pl.when(head == 0)
        def _():
            hide_ref[...] = hidden_scores((qp[...], qs[...], kp[...], ks[...], total_rows))
            total_ref[...] = jnp.zeros_like(total_ref)
            slope_out[...] = jnp.zeros_like(slope_out)

        raw = jnp.where(head < heads_own, own_ref[...], other_ref[...])
        weight = jnp.where(head < heads_own, weight_own[...], weight_other[...])
        up = product(up_ref[...], weight).astype(LOW)
        gain_row, cos, sin = gain_ref[...], cos_ref[...], sin_ref[...]
        query, shrink = turned(raw, gain_row, cos, sin)
        key = pair_ref[:, :HD]
        scores = back_product(key, query) * scale + hide_ref[...]
        weights = jnp.exp(scores - log_ref[0])
        pulled = back_product(pair_ref[:, HD:], up)
        centre = jnp.sum(weights * pulled, axis=0, keepdims=True)
        scores_back = (weights * (pulled - centre)).astype(LOW)
        total_ref[:, :HD] += product(scores_back, query) * scale
        total_ref[:, HD:] += product(weights.astype(LOW), up)
        turned_back = outer_sum(scores_back, key) * scale
        normed_up = rotary(turned_back, cos, -sin)
        shape = raw * shrink
        slope_out[...] += jnp.sum(normed_up * shape, axis=0, keepdims=True)
        inner = normed_up * gain_row
        raw_back = shrink * (inner - shape * jnp.mean(inner * shape, axis=-1, keepdims=True))

        @pl.when(head < heads_own)
        def _():
            query_own[...] = raw_back.astype(LOW)

        @pl.when(head >= heads_own)
        def _():
            query_other[...] = raw_back.astype(LOW)

        @pl.when(head == heads - 1)
        def _():
            before_out[...] = total_ref[:rows].astype(LOW)
            here_out[...] = total_ref[rows : 2 * rows]
            after_out[...] = total_ref[2 * rows :].astype(LOW)

    whole = [(a, None, None) for a in (gain, cosines, sines, keys, upstream) + tuple(places)]
    half = shape_of((rows, heads_own * HD), LOW)
    deep = weights_own.shape[0]
    weight_specs = [
        (weights_own, (deep, HD), lambda h: (0, jnp.minimum(h, heads_own - 1))),
        (weights_other, (deep, HD), lambda h: (0, jnp.maximum(h - heads_own, 0))),
    ]
    return kernel_call(
        body,
        "attention_back",
        (heads,),
        head_specs(own, other, heads_own)
        + weight_specs
        + whole
        + [(log_total, (1, 1, rows), lambda h: (h, 0, 0))],
        head_specs(half, half, heads_own)
        + [
            (shape_of((rows, 2 * HD), LOW), None, None),
            (shape_of((rows, 2 * HD), WIDE), None, None),
            (shape_of((tail, 2 * HD), LOW), None, None),
            (shape_of((1, HD), WIDE), None, None),
        ],
        scratch=[pltpu.VMEM((keys.shape[0], rows), WIDE), pltpu.VMEM((keys.shape[0], 2 * HD), WIDE)],
    )


def keyed(own, other, cols, cosines, sines, gain, flag):
    def body(mine, theirs, cos, sin, gain_row, flag_row):
        first, second = mine[:, cols:], theirs[:, cols:]
        key = jnp.where(flag_row > 0, first, second)
        value = jnp.where(flag_row > 0, second, first)
        return (jnp.concatenate([rotary(normed(key, gain_row), cos, sin), value], axis=1),)

    return rowwise(
        body, "keyed", [own, other, cosines, sines], [gain, flag], [(2 * HD, LOW)], [], 256
    )[0]


def keyed_back(tp_table, here, later, earlier, query_own, query_other, own, other, cols, cosines, sines, gain, flag):
    rows = here.shape[0]
    block = earlier.shape[0]

    def body(tp_ref, here_ref, later_ref, earlier_ref, query_mine, query_theirs, mine, theirs, cos, sin, gain_row, flag_row, own_out, other_out, slope_out):
        got = (pl.program_id(0) == tp_ref[0]).astype(WIDE)
        total = here_ref[...] + later_ref[...].astype(WIDE) + earlier_ref[...].astype(WIDE) * got
        flagged = flag_row[...] > 0
        key = jnp.where(flagged, mine[...], theirs[...])
        key_back, slope = normed_back(
            key, gain_row[...], rotary(total[:, :HD], cos[...], -sin[...])
        )
        value_back = total[:, HD:]
        wide = query_mine.shape[1]
        own_out[:, :wide] = query_mine[...]
        other_out[:, :wide] = query_theirs[...]
        own_out[:, wide:] = jnp.where(flagged, key_back, value_back).astype(LOW)
        other_out[:, wide:] = jnp.where(flagged, value_back, key_back).astype(LOW)

        @pl.when(pl.program_id(0) == 0)
        def _():
            slope_out[...] = slope

        @pl.when(pl.program_id(0) > 0)
        def _():
            slope_out[...] += slope

    def strip(array):
        return (array, (block, array.shape[1]), lambda i, _: (i, 0))

    raw = [(a, (block, HD), lambda i, _: (i, cols // HD)) for a in (own, other)]
    out = strip(shape_of((rows, cols + HD), LOW))
    return kernel_call(
        body,
        "keyed_back",
        (rows // block,),
        [strip(here), strip(later), (earlier, None, None), strip(query_own), strip(query_other)]
        + raw
        + [strip(cosines), strip(sines), (gain, None, None), (flag, None, None)],
        [out, out, (shape_of((1, HD), WIDE), None, None)],
        prefetch=tp_table,
    )


def merged_rows(residual, mine, theirs, low, left, right, gains):
    def body(residual, mine, theirs, low, left, right, gains):
        gain_in, gain_mixer, gain_laurel, gain_next = (gains[i : i + 1] for i in range(4))
        mixer = mine + theirs.astype(WIDE)
        middle = product(low, left).astype(LOW)
        laurel = back_product(middle, right)
        total = (
            residual
            + normed(mixer, gain_mixer)
            + normed(residual, gain_in)
            + normed(laurel, gain_laurel)
        ) * HALF_ROOT
        return mixer, laurel, middle, total, normed(total, gain_next)

    width = residual.shape[1]
    kinds = [(width, WIDE), (width, WIDE), (left.shape[1], LOW), (width, WIDE), (width, LOW)]
    return rowwise(
        body, "merged_rows", [residual, mine, theirs, low], [left, right, gains], kinds, []
    )


def branched(merged, upstream, extra, dense, orders, branch, project, gains):
    def body(merged, upstream, extra, *rest):
        sums = rest[: 3 * len(orders)]
        branch, project, gains = rest[3 * len(orders) :]
        gain_dense, gain_branch = gains[4:5], gains[5:6]
        parts = {}
        for i, group in enumerate(orders):
            near, far, peer = sums[3 * i : 3 * i + 3]
            total = near + far.astype(WIDE) + peer.astype(WIDE)
            part = total.shape[1] // len(group)
            for k, offset in enumerate(group):
                parts[offset] = total[:, k * part : (k + 1) * part]
        dense = jnp.concatenate([parts[o] for o in sorted(parts)], axis=1)
        middle = merged + normed(dense, gain_dense)
        middle_low = middle.astype(LOW)
        raw = product(middle_low, branch)
        extra = extra.astype(WIDE)
        active = smooth_gate(raw)
        low = (active * extra).astype(LOW)
        projected = back_product(low, project)
        result = middle + normed(projected, gain_branch)
        project_back, branch_slope = normed_back(projected, gain_branch, upstream)
        project_low = project_back.astype(LOW)
        pulled = product(project_low, project)
        raw_back = gate_back(raw, pulled * extra).astype(LOW)
        middle_back = upstream + back_product(raw_back, branch)
        dense_back, dense_slope = normed_back(dense, gain_dense, middle_back)
        return (
            result, pulled * active, project_low, low, raw_back, middle_low, middle_back,
            dense_back, branch_slope, dense_slope,
        )

    width, side = merged.shape[1], extra.shape[1]
    kinds = [
        (width, LOW), (side, WIDE), (width, LOW), (side, LOW), (side, LOW), (width, LOW),
        (width, WIDE), (width, LOW),
    ]
    return rowwise(
        body,
        "branched",
        [merged, upstream, extra] + [a for group in dense for a in group],
        [branch, project, gains],
        kinds,
        [width, width],
    )


def merged_back(near, far, peer, merged, middle_back, mixer, laurel, right, gains):
    def body(merged, near, far, peer, middle_back, mixer, laurel, right, gains):
        gain_next, gain_mixer, gain_laurel = gains[3:4], gains[1:2], gains[2:3]
        pulled = near + far.astype(WIDE) + peer.astype(WIDE)
        extra, next_slope = normed_back(merged, gain_next, pulled)
        total = (middle_back + extra) * HALF_ROOT
        mixer_back, mixer_slope = normed_back(mixer, gain_mixer, total)
        laurel_back, laurel_slope = normed_back(laurel, gain_laurel, total)
        laurel_low = laurel_back.astype(LOW)
        middle = product(laurel_low, right)
        return total, mixer_back, laurel_low, middle, next_slope, mixer_slope, laurel_slope

    width = merged.shape[1]
    kinds = [(width, WIDE), (width, LOW), (width, LOW), (right.shape[1], LOW)]
    return rowwise(
        body,
        "merged_back",
        [merged, near, far, peer, middle_back, mixer, laurel],
        [right, gains],
        kinds,
        [width] * 3,
    )


def opened_back(mine, theirs, middle, total, residual, left, gain):
    def body(mine, theirs, middle, total, residual, left, gains):
        gain = gains[0:1]
        pulled = mine + theirs.astype(WIDE) + back_product(middle, left) + total
        back, slope = normed_back(residual, gain, pulled)
        return total + back, slope

    width = residual.shape[1]
    return rowwise(
        body,
        "opened_back",
        [mine, theirs, middle, total, residual],
        [left, gain],
        [(width, WIDE)],
        [width],
    )


def doubled(own, other, first_row, row_count, weights_own, weights_other, kind):
    def body(own_ref, other_ref, weight_own, weight_other, out_ref):
        total = back_product(own_ref[...], weight_own[...])
        total = total + back_product(other_ref[...], weight_other[...])
        out_ref[...] = total.astype(kind)

    start = first_row // row_count
    tall = weights_own.shape[0]
    block = 512
    return kernel_call(
        body,
        "doubled",
        (tall // block,),
        [
            (own, (row_count, own.shape[1]), lambda i: (start, 0)),
            (other, (row_count, other.shape[1]), lambda i: (start, 0)),
            (weights_own, (block, own.shape[1]), lambda i: (i, 0)),
            (weights_other, (block, other.shape[1]), lambda i: (i, 0)),
        ],
        [(shape_of((row_count, tall), kind), (row_count, block), lambda i: (0, i))],
    )[0]


def added_low(near, far, first_row):
    rows = near.shape[0] - first_row

    def body(near_ref, far_ref, out_ref):
        out_ref[...] = (near_ref[...] + far_ref[...].astype(WIDE)).astype(LOW)

    block = ((rows, near.shape[1]), lambda i: (first_row // rows, 0))
    return kernel_call(
        body,
        "added_low",
        (1,),
        [(near,) + block, (far,) + block],
        [(shape_of((rows, near.shape[1]), LOW), None, None)],
    )[0]


def shifted(block, distance):
    devices = range(lax.axis_size("seq"))
    route = [(i - distance, i) for i in devices if i - distance in devices]
    return lax.ppermute(block, "seq", route)


def tp_swap(block):
    return lax.ppermute(block, "tp", [(0, 1), (1, 0)])


def core_swap(block):
    return lax.ppermute(block, "seq", [(i, i ^ 1) for i in range(lax.axis_size("seq"))])


class Line:
    def __init__(self, mark):
        self.mark = mark

    def pin(self, values):
        values, self.mark = lax.optimization_barrier((values, self.mark))
        return values


class Ring:
    def __init__(self):
        self.chips = lax.axis_size("seq") // 2
        rows = self.chips // 2
        self.order = [2 * i for i in range(rows)] + [2 * i + 1 for i in reversed(range(rows))]
        place = [0] * self.chips
        for position, member in enumerate(self.order):
            place[member] = position
        mine = jnp.asarray(place, jnp.int32)[lax.axis_index("seq") // 2]
        offsets = (mine + jnp.arange(self.chips, dtype=jnp.int32)) % self.chips
        self.owners = jnp.asarray(self.order, jnp.int32)[offsets]

    def moved(self, block, step):
        n = self.chips
        route = [
            (self.order[p] * 2 + core, self.order[(p + step) % n] * 2 + core)
            for p in range(n)
            for core in range(2)
        ]
        return lax.ppermute(block, "seq", route)


class Gather:
    def __init__(self, ring, line, chunk, cut):
        self.ring = ring
        self.line = line
        self.cut = cut
        self.found = [None] * ring.chips
        self.found[0] = chunk
        self.count = 0

    def send(self):
        n = self.ring.chips
        self.count += 1
        k = self.count
        behind, ahead = (n - k + 1) % n, k - 1
        held = self.line.pin({o: self.found[o] for o in {behind, ahead}})
        self.found[behind], self.found[ahead] = held[behind], held[ahead]
        if k < n // 2:
            self.found[n - k] = self.ring.moved(held[behind], 1)
            self.found[k] = self.ring.moved(held[ahead], -1)
        else:
            self.found[k] = (
                self.ring.moved(held[behind][:, : self.cut], 1),
                self.ring.moved(held[ahead][:, self.cut :], -1),
            )

    def land(self):
        n = self.ring.chips
        new = {n - self.count, self.count}
        landed = self.line.pin({o: self.found[o] for o in new})
        for o in new:
            self.found[o] = landed[o]

    def finish(self):
        while self.count < self.ring.chips // 2:
            self.send()
            self.land()

    def columns(self, first, count):
        listed = []
        for chunk in self.found:
            if isinstance(chunk, tuple):
                half = first >= self.cut
                listed.append((chunk[half], first - self.cut * half))
            else:
                listed.append((chunk, first))
        return listed

    def joined(self, first, count):
        return jnp.concatenate(
            [a[:, start : start + count] for a, start in self.columns(first, count)], axis=0
        )


class Scatter:
    def __init__(self, ring, line, segments, part, cut):
        self.ring = ring
        self.line = line
        self.segments = segments
        self.part = part
        self.cut = cut
        self.count = 0
        self.front = self.back = None

    def prepare(self):
        n = self.ring.chips
        pair = ring_terms(
            self.segments,
            self.part,
            n // 2 - self.count,
            n // 2 + self.count,
            self.front,
            self.back,
            self.cut,
        )
        self.front, self.back = self.line.pin(tuple(pair))
        self.count += 1

    def send(self):
        front, back = self.line.pin((self.front, self.back))
        self.front, self.back = self.ring.moved(front, 1), self.ring.moved(back, -1)

    def land(self):
        self.front, self.back = self.line.pin((self.front, self.back))

    def left(self):
        return self.ring.chips // 2 - self.count

    def total(self, core):
        front, back = self.line.pin((self.front, self.back))
        results = []
        at = 0
        for left, right, added in self.segments:
            results.append(
                last_term(core, self.part, left, right, added, front, back, at)
            )
            at += right.shape[1]
        return results


def shards(
    hidden,
    layer_input,
    cotangent,
    span_starts,
    query_weight,
    key_weight,
    value_weight,
    output_weight,
    laurel_left,
    laurel_right,
    gate_weight,
    upward_weight,
    down_weight,
    branch_gate,
    branch_output,
    input_gain,
    query_gain,
    key_gain,
    mixer_gain,
    laurel_gain,
    prefeed_gain,
    postfeed_gain,
    branch_gain,
):
    tp_size = lax.axis_size("tp")
    seq_place = lax.axis_index("seq")
    tp_place = lax.axis_index("tp")
    core = seq_place % 2
    first_core = core == 0
    first_tp = tp_place == 0
    ring = Ring()
    line = Line(input_gain)
    pin = line.pin
    chips = ring.chips
    half_chips = chips // 2
    local_rows, width = hidden.shape
    block_rows = local_rows * tp_size
    total_rows = span_starts.shape[0]
    query_heads = QH // tp_size
    part = width // chips
    everywhere = ("seq", "tp")

    core_table = core[None].astype(jnp.int32)
    tp_table = tp_place[None].astype(jnp.int32)
    query_cols, output_width = query_weight.shape[1] // 2, output_weight.shape[0] // 2
    key_value = jnp.concatenate([key_weight, value_weight], axis=1)
    first_cols = query_cols + key_weight.shape[1]
    first_weights = (query_weight, key_value, output_weight.T)
    first_given = pin(weights_given(core_table, first_weights))
    first_theirs = core_swap(first_given)
    dense_weights = (gate_weight, upward_weight, down_weight.T)
    units = gate_weight.shape[1] // 2
    side, rank = branch_gate.shape[1], laurel_left.shape[1]
    gains = jnp.stack(
        [line.mark, mixer_gain, laurel_gain, prefeed_gain, postfeed_gain, branch_gain] * 2
    )[:8]
    small = jnp.concatenate([branch_gate, branch_output.T, laurel_left, laurel_right.T], axis=1)
    dense_weights, gains, small = pin((dense_weights, gains, small))
    dense_given = pin(weights_given(core_table, dense_weights))
    (first_pack,) = pin(
        weights_merged(core_table, first_weights, pin(first_theirs), ((0, 1, 2),))
    )
    first = Gather(ring, line, first_pack, first_cols)
    swapped_chunks = [None] * chips

    def swap_chunks(*offsets):
        for o in offsets:
            chunk = first.found[o]
            swapped_chunks[o] = (
                tuple(core_swap(a) for a in chunk) if isinstance(chunk, tuple) else core_swap(chunk)
            )

    def land_chunks(*offsets):
        for o in offsets:
            swapped_chunks[o] = pin(swapped_chunks[o])

    first.send()
    small_full = lax.all_gather(small, everywhere, axis=0, tiled=True)
    residual, upstream, gains = pin(
        permuted([hidden, cotangent, gains], [WIDE, WIDE, WIDE], ring.owners)
    )
    line.mark = gains
    (normed_low,) = rowwise(
        lambda value, gains: (normed(value, gains[0:1]),),
        "opened",
        [residual],
        [gains],
        [(width, LOW)],
        [],
    )
    normed_low = pin(normed_low)
    first.land()

    first.send()
    dense_theirs = core_swap(dense_given)
    rows_theirs = tp_swap(normed_low)
    swap_chunks(0, chips - 1, 1)
    expand_pack, down_pack = pin(
        weights_merged(core_table, dense_weights, pin(dense_theirs), ((0, 1), (2,)))
    )
    land_chunks(0, chips - 1, 1)
    first.land()
    while first.count < half_chips - 1:
        first.send()
        swap_chunks(chips - first.count + 1, first.count - 1)
        land_chunks(chips - first.count + 1, first.count - 1)
        first.land()
    expand = Gather(ring, line, expand_pack, units)
    down = Gather(ring, line, down_pack, units // 2)
    first.send()
    swap_chunks(half_chips + 1, half_chips - 1)
    start_row = seq_place * block_rows
    padded_starts = jnp.concatenate(
        [jnp.full((block_rows,), -1, jnp.int32), span_starts, jnp.full((PIC,), -1, jnp.int32)]
    )
    span = 2 * block_rows + PIC
    ahead_of = jnp.arange(span, dtype=jnp.int32)
    swapped = jnp.where(
        ahead_of < 2 * block_rows, ahead_of ^ (tp_place * local_rows), ahead_of
    )
    key_place = start_row - block_rows + swapped
    starts = lax.dynamic_slice_in_dim(padded_starts, start_row, span)
    blocks = [starts[i * local_rows : (i + 1) * local_rows] for i in range(4)]
    key_start = jnp.where(
        first_tp,
        starts,
        jnp.concatenate([blocks[1], blocks[0], blocks[3], blocks[2], starts[2 * block_rows :]]),
    )
    row_place = key_place[block_rows : 2 * block_rows]
    row_start = key_start[block_rows : 2 * block_rows]
    places = (row_place[None, :], row_start[None, :], key_place[:, None], key_start[:, None])
    frequency = ROPE_BASE ** (-(jnp.arange(HD // 2, dtype=WIDE) * 2.0) / HD)
    theta = row_place.astype(WIDE)[:, None] * frequency[None, :]
    flag = jnp.broadcast_to(jnp.where(first_core, 1.0, 0.0), (1, HD))
    cosines, sines, places, flag = pin((jnp.cos(theta), jnp.sin(theta), places, flag))
    query_gain_row, key_gain_row = query_gain[None, :], key_gain[None, :]
    land_chunks(half_chips + 1, half_chips - 1)
    rows_theirs = pin(rows_theirs)
    first.land()

    expand.send()
    swap_chunks(half_chips)
    land_chunks(half_chips)
    rows_low = pin(stacked(normed_low, rows_theirs))

    def columns(found, start, count):
        listed = []
        for chunk in found:
            if isinstance(chunk, tuple):
                half = start >= first_cols
                listed.append((chunk[half], start - first_cols * half))
            else:
                listed.append((chunk, start))
        return joined_chunks(listed, 0, count)

    first_own = pin(columns(first.found, 0, first_cols))
    first_other = pin(columns(swapped_chunks, 0, first_cols))
    raw_own = pin(multiplied(rows_low, first_own))
    raw_other = pin(multiplied(rows_low, first_other))
    pair_low = pin(
        keyed(raw_own, raw_other, query_cols, cosines, sines, key_gain_row, flag)
    )
    early = pin(lax.dynamic_slice_in_dim(pair_low, tp_place * local_rows, PIC, 0))
    pairs_before, pairs_after = shifted(pair_low, 1), shifted(early, -1)
    output_own_full = pin(columns(first.found, first_cols, output_width))
    output_other_full = pin(columns(swapped_chunks, first_cols, output_width))
    pairs_before, pairs_after, small_full = pin((pairs_before, pairs_after, small_full))
    expand.land()
    expand.send()
    pairs_all = pin(stacked(pairs_before, pair_low, pairs_after))
    attended_own, attended_other, log_total = pin(
        attention(
            raw_own, raw_other, query_heads, query_gain_row, cosines, sines, pairs_all, pairs_all,
            places, total_rows,
        )
    )

    def output_product(first_row, kind):
        return pin(
            doubled(
                attended_own, attended_other, first_row, local_rows, output_own_full,
                output_other_full, kind,
            )
        )

    mixer_theirs = tp_swap(output_product(local_rows, LOW))
    mixer_mine = output_product(0, WIDE)
    branch_full, project_full, left_full, right_full = pin(
        permuted_rows(small_full, ring.owners, (side, side, rank, rank))
    )
    mixer_theirs = pin(mixer_theirs)
    expand.land()
    expand.send()
    mixer_raw, laurel_raw, laurel_mid, merged, dense_low = pin(
        merged_rows(
            residual, mixer_mine, mixer_theirs, normed_low, left_full, right_full, gains
        )
    )

    theirs, far = tp_swap(dense_low), core_swap(dense_low)
    theirs, far = pin((theirs, far))
    expand.land()
    while expand.count < half_chips - 1:
        expand.send()
        expand.land()
    expand.send()
    last = pin(core_swap(theirs))
    dense_rows = pin(stacked(dense_low, theirs, far, last))
    expand.land()
    down.send()
    gate_columns, upward_columns = pin(
        (
            [a for a, _ in expand.columns(0, units)],
            [a for a, _ in expand.columns(units, units)],
        )
    )
    gates = list(zip(gate_columns, (f for _, f in expand.columns(0, units))))
    upwards = list(zip(upward_columns, (f for _, f in expand.columns(units, units))))
    gate_raw, upward_raw, inner_low = pin(expanded(dense_rows, gates, upwards, units))
    down.land()
    orders, dense_sums = [], []

    def down_chunk(offset):
        chunk = down.found[offset]
        return chunk if isinstance(chunk, tuple) else (chunk,)

    def dense_send(offsets):
        chunks = pin([down_chunk(o) for o in offsets])
        far = pin(contracted(inner_low, block_rows, block_rows, chunks, LOW))
        far = core_swap(far)
        near = pin(contracted(inner_low, 0, block_rows, chunks, WIDE))
        far = pin(far)
        peer = pin(added_low(near, far, local_rows))
        orders.append(offsets)
        dense_sums.append((near, far, tp_swap(peer)))

    for near in range(1, half_chips + 1):
        if down.count < half_chips:
            down.send()
        if near == 1:
            dense_send([chips - 1, 0, 1])
        else:
            dense_send([chips - near, near] if near < half_chips else [near])
        if near < half_chips:
            down.land()
    dense_sums = pin(dense_sums)
    (
        result, layer_delta, project_low, branch_low, branch_raw_back, middle_low, middle_back,
        dense_low_back, branch_slope, postfeed_slope,
    ) = pin(
        branched(
            merged, upstream, layer_input, dense_sums, orders, branch_full, project_full,
            gains,
        )
    )

    theirs, far = tp_swap(dense_low_back), core_swap(dense_low_back)
    theirs, far = pin((theirs, far))
    last = pin(core_swap(theirs))
    dense_rows_back = pin(stacked(dense_low_back, theirs, far, last))
    down_ring = Scatter(ring, line, [(dense_rows_back, inner_low, None)], part, units // 2)
    down_ring.prepare()
    down_ring.send()
    gate_raw_back, upward_raw_back = pin(
        inner_pulled(
            pin(dense_rows_back), [down_chunk(o) for o in range(chips)], gate_raw, upward_raw
        )
    )
    gate_ring = Scatter(ring, line, [(dense_rows, gate_raw_back, None)], part, units // 2)
    upward_ring = Scatter(ring, line, [(dense_rows, upward_raw_back, None)], part, units // 2)
    gate_ring.prepare()
    down_ring.land()
    gate_ring.send()
    upward_ring.prepare()
    gate_ring.land()
    upward_ring.send()
    down_ring.prepare()
    upward_ring.land()

    def dense_back(first_row, row_count, kind):
        left, right = pin((gate_raw_back, upward_raw_back))
        return pin(rows_pulled(left, right, first_row, row_count, gates, upwards, kind))

    down_ring.send()
    far_given = dense_back(block_rows, block_rows, LOW)
    gate_ring.prepare()
    down_ring.land()
    gate_ring.send()
    far_back = core_swap(far_given)
    near_back = dense_back(0, block_rows, WIDE)
    upward_ring.prepare()
    far_back = pin(far_back)
    gate_ring.land()
    upward_ring.send()
    peer_given = pin(added_low(near_back, far_back, local_rows))
    down_ring.prepare()
    upward_ring.land()
    down_ring.send()
    peer_back = tp_swap(peer_given)
    gate_ring.prepare()
    peer_back = pin(peer_back)
    down_ring.land()
    gate_ring.send()
    (
        summed_back, mixer_low_back, laurel_raw_low, laurel_mid_back, prefeed_slope, mixer_slope,
        laurel_slope,
    ) = pin(
        merged_back(
            near_back, far_back, peer_back, merged, middle_back, mixer_raw, laurel_raw,
            right_full, gains,
        )
    )
    upward_ring.prepare()
    gate_ring.land()
    upward_ring.send()
    mixer_theirs_back = tp_swap(mixer_low_back)
    small_delta = turned_products(
        [
            (middle_low, branch_raw_back),
            (project_low, branch_low),
            (normed_low, laurel_mid_back),
            (laurel_raw_low, laurel_mid),
        ],
        LOW,
    )
    (small_delta,) = pin(
        permuted_rows(pin(small_delta), ring.owners, (2 * side + 2 * rank,), inverse=True)
    )
    down_ring.prepare()
    mixer_theirs_back = pin(mixer_theirs_back)
    upward_ring.land()
    down_ring.send()
    small_delta = lax.psum_scatter(small_delta, everywhere, scatter_dimension=0, tiled=True)
    mixer_rows_back = pin(stacked(mixer_low_back, mixer_theirs_back))
    query_own_back, query_other_back, pairs_sent, pairs_here, pairs_late, query_slope = pin(
        attention_back(
            raw_own, raw_other, query_heads, query_gain_row, cosines, sines, pairs_all, places,
            total_rows, log_total, mixer_rows_back, output_own_full, output_other_full,
        )
    )
    gate_ring.prepare()
    down_ring.land()
    gate_ring.send()
    later, earlier = shifted(pairs_sent, -1), shifted(pairs_late, 1)
    output_given = pin(turned_products([(mixer_rows_back, attended_other)], LOW))
    upward_ring.prepare()
    later, earlier = pin((later, earlier))
    gate_ring.land()
    upward_ring.send()
    output_theirs = core_swap(output_given)
    first_own_back, first_other_back, key_slope = pin(
        keyed_back(
            tp_table, pairs_here, later, earlier, query_own_back, query_other_back, raw_own,
            raw_other, query_cols, cosines, sines, key_gain_row, flag,
        )
    )
    first_given_back = pin(turned_products([(rows_low, first_other_back)], LOW))
    first_theirs_back = core_swap(first_given_back)

    def rows_back(first_row, kind):
        return pin(
            doubled(
                first_own_back, first_other_back, first_row, local_rows, first_own, first_other,
                kind,
            )
        )

    rows_given = rows_back(local_rows, LOW)
    first_theirs_back, output_theirs = pin((first_theirs_back, output_theirs))
    upward_ring.land()
    for stream in (down_ring, gate_ring, upward_ring):
        while stream.left():
            stream.prepare()
            stream.send()
            stream.land()
    first_ring = Scatter(
        ring, line, [(rows_low, first_own_back, first_theirs_back)], part, first_cols - HD
    )
    output_ring = Scatter(
        ring, line, [(mixer_rows_back, attended_own, output_theirs)], part, output_width // 2
    )
    output_ring.prepare()
    output_ring.send()
    rows_theirs = tp_swap(rows_given)
    first_ring.prepare()
    rows_mine = rows_back(0, WIDE)
    output_ring.land()
    first_ring.send()
    output_ring.prepare()
    rows_theirs = pin(rows_theirs)
    first_ring.land()
    output_ring.send()
    first_ring.prepare()
    hidden_delta, input_slope = opened_back(
        rows_mine, rows_theirs, laurel_mid_back, summed_back, residual, left_full, line.mark
    )
    slopes = jnp.concatenate(
        [
            input_slope,
            mixer_slope,
            laurel_slope,
            prefeed_slope,
            postfeed_slope,
            branch_slope,
            jnp.pad(jnp.concatenate([query_slope, key_slope], axis=1), ((0, 1), (0, width - 2 * HD))),
        ],
    )
    result, hidden_delta, gain_slopes = permuted(
        [result, hidden_delta, slopes], [LOW, WIDE, WIDE], ring.owners, inverse=True
    )
    slopes = jnp.concatenate([gain_slopes[:6], slopes[6:]])
    line.mark = hidden_delta
    output_ring.land()
    slopes = lax.all_gather(pin(slopes)[None], everywhere, axis=0, tiled=True)
    first_ring.send()
    output_ring.prepare()
    ((down_kept, down_given),) = pin(down_ring.total(core_table))
    first_ring.land()
    output_ring.send()
    down_theirs = core_swap(down_given)
    first_ring.prepare()
    down_theirs = pin(down_theirs)
    output_ring.land()
    first_ring.send()
    output_ring.prepare()
    ((gate_kept, gate_given),) = pin(gate_ring.total(core_table))
    first_ring.land()
    output_ring.send()
    gate_theirs = core_swap(gate_given)
    first_ring.prepare()
    ((upward_kept, upward_given),) = pin(upward_ring.total(core_table))
    gate_theirs = pin(gate_theirs)
    output_ring.land()
    first_ring.send()
    upward_theirs = core_swap(upward_given)
    down_delta = pin(assembled(core_table, down_kept, down_theirs, True))
    gate_delta = pin(assembled(core_table, gate_kept, gate_theirs))
    upward_theirs = pin(upward_theirs)
    first_ring.land()
    for stream in (output_ring, first_ring):
        while stream.left():
            stream.prepare()
            stream.send()
            stream.land()
    ((first_kept, first_given),) = pin(first_ring.total(core_table))
    first_theirs = core_swap(first_given)
    ((output_kept, output_given),) = pin(output_ring.total(core_table))
    output_theirs = core_swap(output_given)
    upward_delta = pin(assembled(core_table, upward_kept, upward_theirs))
    slopes, first_theirs, output_theirs = pin((slopes, first_theirs, output_theirs))
    slopes = jnp.sum(slopes, axis=0)
    output_delta = assembled(core_table, output_kept, output_theirs, True)
    first_theirs = first_theirs.astype(WIDE)
    query_delta = assembled(core_table, first_kept[:, :query_cols], first_theirs[:, :query_cols])
    key_delta = jnp.where(first_core, first_kept[:, query_cols:], first_theirs[:, query_cols:])
    value_delta = jnp.where(first_core, first_theirs[:, query_cols:], first_kept[:, query_cols:])
    small_delta = small_delta.astype(WIDE)
    return (
        result,
        line.mark,
        layer_delta,
        query_delta,
        key_delta,
        value_delta,
        output_delta,
        small_delta[:, 2 * side : 2 * side + rank],
        small_delta[:, 2 * side + rank :].T,
        gate_delta,
        upward_delta,
        down_delta,
        small_delta[:, :side],
        small_delta[:, side : 2 * side].T,
        slopes[0],
        slopes[6, :HD],
        slopes[6, HD : 2 * HD],
        slopes[1],
        slopes[2],
        slopes[3],
        slopes[4],
        slopes[5],
    )


def solution(mesh):
    tokens = P(("seq", "tp"), None)
    spread = P(None, ("seq", "tp"))
    inward = P("seq", "tp")
    outward = P("tp", "seq")
    weights = (
        inward,
        inward,
        inward,
        outward,
        tokens,
        spread,
        inward,
        inward,
        outward,
        tokens,
        spread,
    )
    return jax.shard_map(
        shards,
        mesh=mesh,
        in_specs=(tokens, tokens, tokens, P()) + weights + (P(),) * 8,
        out_specs=(tokens, tokens, tokens) + weights + (P(),) * 8,
        check_vma=False,
    )
```

```python
import jax
import jax.numpy as jnp
from jax import lax
from jax.experimental import pallas as pl
from jax.experimental.pallas import tpu as pltpu
from jax.sharding import PartitionSpec as P

QH = 8
KVH = 2
HD = 256
WIN = 512
PIC = 256


EPSILON = 1e-06
HALF_ROOT = 0.7071067811865476
ROPE_BASE = 10000.0
NEGATIVE = -1e30
GELU_SCALE = 0.7978845608028654
GELU_CUBE = 0.044715

LOW = jnp.bfloat16
WIDE = jnp.float32
VMEM_LIMIT = 56 * 2**20


def normed(value, gain):
    return value * lax.rsqrt(jnp.mean(value * value, axis=-1, keepdims=True) + EPSILON) * gain


def normed_back(value, gain, upstream):
    _, pullback = jax.vjp(normed, value, gain)
    return pullback(upstream)


def smooth_gate(value):
    return (
        0.5 * value * (1.0 + jnp.tanh(GELU_SCALE * (value + GELU_CUBE * value * value * value)))
    )


def gate_back(value, upstream):
    _, pullback = jax.vjp(smooth_gate, value)
    return pullback(upstream)[0]


def rotary(value, cosines, sines):
    half = value.shape[-1] // 2
    first = value[..., :half]
    second = value[..., half:]
    return jnp.concatenate(
        [first * cosines - second * sines, second * cosines + first * sines], axis=-1
    )


def product(left, right):
    return jnp.dot(left, right, preferred_element_type=WIDE)


def outer_sum(left, right):
    return lax.dot_general(left, right, (((0,), (0,)), ((), ())), preferred_element_type=WIDE)


def back_product(left, right):
    return lax.dot_general(left, right, (((1,), (1,)), ((), ())), preferred_element_type=WIDE)


def shape_of(shape, kind):
    return jax.ShapeDtypeStruct(shape, kind)


def kernel_call(body, name, grid, inputs, outputs, scratch=(), flops=0, prefetch=None):
    def spec(entry):
        array, block, where = entry
        if block is None:
            rank = len(array.shape)
            return pl.BlockSpec(array.shape, lambda *_, rank=rank: (0,) * rank)
        return pl.BlockSpec(block, where)

    moved = sum(a.size * a.dtype.itemsize for a, _, _ in list(inputs) + list(outputs))
    call = pl.pallas_call(
        body,
        grid_spec=pltpu.PrefetchScalarGridSpec(
            num_scalar_prefetch=0 if prefetch is None else 1,
            grid=grid,
            in_specs=[spec(e) for e in inputs],
            out_specs=[spec(e) for e in outputs],
            scratch_shapes=list(scratch),
        ),
        out_shape=[shape_of(a.shape, a.dtype) for a, _, _ in outputs],
        compiler_params=pltpu.CompilerParams(
            dimension_semantics=("arbitrary",) * len(grid), vmem_limit_bytes=VMEM_LIMIT
        ),
        cost_estimate=pl.CostEstimate(flops=0, bytes_accessed=0, transcendentals=0),
        name=name,
    )
    operands = [a for a, _, _ in inputs]
    return call(*operands) if prefetch is None else call(prefetch, *operands)


def permuted(arrays, kinds, table, inverse=False):
    count = table.shape[0]
    part = arrays[0].shape[1] // count
    if part % 128:
        if inverse:
            table = jnp.argsort(table)
        results = []
        for array, kind in zip(arrays, kinds):
            parts = [
                lax.dynamic_slice_in_dim(array, table[j] * part, part, 1) for j in range(count)
            ]
            results.append(jnp.concatenate(parts, axis=1).astype(kind))
        return results

    def body(table_ref, *refs):
        for source, target in zip(refs[: len(arrays)], refs[len(arrays) :]):
            for j in range(count):
                here = pl.ds(j * part, part)
                there = pl.ds(pl.multiple_of(table_ref[j] * part, part), part)
                before, behind = (here, there) if inverse else (there, here)
                target[:, behind] = source[:, before].astype(target.dtype)

    return kernel_call(
        body,
        "permuted",
        (1,),
        [(a, None, None) for a in arrays],
        [(shape_of(a.shape, k), None, None) for a, k in zip(arrays, kinds)],
        prefetch=table,
    )


def permuted_rows(array, table, widths, inverse=False):
    count = table.shape[0]
    part = array.shape[0] // count

    def body(table_ref, source, *targets):
        for j in range(count):
            here = pl.ds(j * part, part)
            there = pl.ds(pl.multiple_of(table_ref[j] * part, part), part)
            before, behind = (here, there) if inverse else (there, here)
            at = 0
            for target, wide in zip(targets, widths):
                target[behind, :] = source[before, at : at + wide]
                at += wide

    outs = [(shape_of((array.shape[0], w), array.dtype), None, None) for w in widths]
    return kernel_call(body, "permuted_rows", (1,), [(array, None, None)], outs, prefetch=table)


def weights_given(core, weights):
    rows = weights[0].shape[0]
    halves = [w.shape[1] // 2 for w in weights]

    def body(core_ref, *refs):
        at = 0
        for half, ref in zip(halves, refs):
            refs[-1][:, at : at + half] = ref[...]
            at += half

    return kernel_call(
        body,
        "weights_given",
        (1,),
        [
            (w, (rows, half), lambda _, core_ref: (0, 1 - core_ref[0]))
            for w, half in zip(weights, halves)
        ],
        [(shape_of((rows, sum(halves)), LOW), None, None)],
        prefetch=core,
    )[0]


def weights_merged(core, weights, theirs, groups):
    rows = weights[0].shape[0]
    halves = [w.shape[1] // 2 for w in weights]

    def body(core_ref, *refs):
        other = refs[len(weights)]
        outs = refs[len(weights) + 1 :]
        mine = pl.ds(pl.multiple_of(core_ref[0] * rows, rows), rows)
        given = pl.ds(pl.multiple_of((1 - core_ref[0]) * rows, rows), rows)
        at = 0
        for out, group in zip(outs, groups):
            column = 0
            for i in group:
                wide = halves[i]
                out[mine, column : column + wide] = refs[i][...]
                out[given, column : column + wide] = other[:, at : at + wide]
                column += wide
                at += wide

    return kernel_call(
        body,
        "weights_merged",
        (1,),
        [
            (w, (rows, half), lambda _, core_ref: (0, core_ref[0]))
            for w, half in zip(weights, halves)
        ]
        + [(theirs, None, None)],
        [
            (shape_of((2 * rows, sum(halves[i] for i in group)), LOW), None, None)
            for group in groups
        ],
        prefetch=core,
    )


def expanded(rows, gates, ups, hidden_units):
    tile = 512
    count = len(gates)
    part = gates[0][0].shape[0]

    def body(rows_ref, *refs):
        gate_refs, up_refs = refs[:count], refs[count : 2 * count]
        gate_out, up_out, inner_out = refs[2 * count :]
        x = rows_ref[...]
        gate = product(x, jnp.concatenate([r[...] for r in gate_refs], axis=0))
        up = product(x, jnp.concatenate([r[...] for r in up_refs], axis=0))
        gate_out[...] = gate.astype(LOW)
        up_out[...] = up.astype(LOW)
        inner_out[...] = (smooth_gate(gate) * up).astype(LOW)

    chunks = [
        (a, (part, tile), lambda j, first=first // tile: (0, first + j)) for a, first in gates + ups
    ]
    out = (shape_of((rows.shape[0], hidden_units), LOW), (rows.shape[0], tile), lambda j: (0, j))
    return kernel_call(
        body,
        "expanded",
        (hidden_units // tile,),
        [(rows, None, None)] + chunks,
        [out] * 3,
        flops=4 * rows.size * hidden_units,
    )


def contracted(inner, first_row, row_count, chunks, kind):
    units = inner.shape[1]
    flat = [a for chunk in chunks for a in chunk]
    part = flat[0].shape[0]
    block = min(row_count, 256)

    def body(inner_ref, *refs):
        out_ref = refs[-1]
        at = 0
        for i, chunk in enumerate(chunks):
            column = 0
            total = None
            for a in chunk:
                wide = a.shape[1]
                term = back_product(inner_ref[:, column : column + wide], refs[at][...])
                total = term if total is None else total + term
                column += wide
                at += 1
            out_ref[:, i * part : (i + 1) * part] = total.astype(out_ref.dtype)

    start = first_row // block
    return kernel_call(
        body,
        "contracted",
        (row_count // block,),
        [(inner, (block, units), lambda i: (start + i, 0))] + [(a, None, None) for a in flat],
        [
            (
                shape_of((row_count, part * len(chunks)), kind),
                (block, part * len(chunks)),
                lambda i: (i, 0),
            )
        ],
        flops=2 * row_count * units * part * len(chunks),
    )[0]


def inner_pulled(rows, chunks, gate, up):
    tile = 512
    count, units = gate.shape
    steps = units // tile
    flat, kinds = [], []
    for chunk in chunks:
        for i, a in enumerate(chunk):
            first = 0 if i == 0 else steps - a.shape[1] // tile
            last = a.shape[1] // tile - 1
            flat.append(
                (
                    a,
                    (a.shape[0], tile),
                    lambda j, first=first, last=last: (0, jnp.clip(j - first, 0, last)),
                )
            )

    def body(rows_ref, *refs):
        chunk_refs = refs[: len(flat)]
        gate_ref, up_ref, gate_out, up_out = refs[len(flat) :]
        step = pl.program_id(0)
        parts = []
        at = 0
        for chunk in chunks:
            value = chunk_refs[at][...]
            if len(chunk) == 2:
                value = jnp.where(
                    step < chunk[0].shape[1] // tile, value, chunk_refs[at + 1][...]
                )
            parts.append(value)
            at += len(chunk)
        pulled = product(rows_ref[...], jnp.concatenate(parts, axis=0))
        gate_out[...] = (pulled * gate_ref[...].astype(WIDE)).astype(LOW)
        up_out[...] = (pulled * up_ref[...].astype(WIDE)).astype(LOW)

    block = ((count, tile), lambda j: (0, j))
    return kernel_call(
        body,
        "inner_pulled",
        (steps,),
        [(rows, None, None)] + flat + [(gate,) + block, (up,) + block],
        [(gate,) + block] * 2,
        flops=2 * rows.size * units,
    )


def gate_slopes(gate, up):
    def body(gate, up):
        value = gate.astype(WIDE)
        square = value * value
        bent = jnp.tanh(GELU_SCALE * (value + GELU_CUBE * value * square))
        slope = 0.5 * (1.0 + bent) + 0.5 * value * (1.0 - bent * bent) * GELU_SCALE * (
            1.0 + 3.0 * GELU_CUBE * square
        )
        return up.astype(WIDE) * slope, 0.5 * value * (1.0 + bent)

    kinds = [(gate.shape[1], LOW)] * 2
    return rowwise(body, "gate_slopes", [gate, up], [], kinds, [])


def rows_pulled(gate_back_low, up_back_low, first_row, row_count, gates, ups, kind):
    tile = 1024
    units = gate_back_low.shape[1]
    count = len(gates)
    part = gates[0][0].shape[0]
    width = part * count
    steps = units // tile
    start = first_row // row_count

    def body(gate_ref, up_ref, *refs):
        out_ref, total_ref = refs[-2:]
        step = pl.program_id(0)
        term = back_product(
            gate_ref[...], jnp.concatenate([r[...] for r in refs[:count]], axis=0)
        ) + back_product(
            up_ref[...], jnp.concatenate([r[...] for r in refs[count : 2 * count]], axis=0)
        )

        @pl.when(step == 0)
        def _():
            total_ref[...] = term

        @pl.when((step > 0) & (step < steps - 1))
        def _():
            total_ref[...] += term

        @pl.when(step == steps - 1)
        def _():
            out_ref[...] = (total_ref[...] + term).astype(out_ref.dtype)

    chunks = [
        (a, (part, tile), lambda k, first=first // tile: (0, first + k)) for a, first in gates + ups
    ]
    left = ((row_count, tile), lambda k: (start, k))
    return kernel_call(
        body,
        "rows_pulled",
        (steps,),
        [(gate_back_low,) + left, (up_back_low,) + left] + chunks,
        [(shape_of((row_count, width), kind), None, None)],
        scratch=[pltpu.VMEM((row_count, width), WIDE)],
        flops=4 * row_count * units * width,
    )[0]


def one_term(offset, part, left, right, added, first=0, count=None):
    rows = left.shape[0]
    count = right.shape[1] if count is None else count
    tile = max(t for t in (256, 512, 1024) if count % t == 0 and first % t == 0)

    def body(left_ref, right_ref, *refs):
        turn = refs[-1]

        @pl.when(pl.program_id(0) == 0)
        def _():
            turn[...] = left_ref[...].T

        total = product(turn[...], right_ref[...])
        if added is not None:
            total = total + refs[0][...].astype(WIDE)
        refs[-2][...] = total.astype(LOW)

    inputs = [
        (left, (rows, part), lambda j: (0, offset)),
        (right, (rows, tile), lambda j: (0, first // tile + j)),
    ]
    if added is not None:
        inputs.append((added, (part, tile), lambda j: (offset, first // tile + j)))
    return kernel_call(
        body,
        "one_term",
        (count // tile,),
        inputs,
        [(shape_of((part, count), LOW), (part, tile), lambda j: (0, j))],
        scratch=[pltpu.VMEM((part, rows), LOW)],
    )[0]


def two_terms(offset, part, left, right, added):
    rows = left.shape[0]
    half = right.shape[1] // 2
    tile = min(half, 512)
    steps = half // tile

    def body(left_ref, first_ref, second_ref, *refs):
        turn = refs[-1]

        @pl.when(pl.program_id(0) == 0)
        def _():
            turn[...] = left_ref[...].T

        first = product(turn[...], first_ref[...])
        second = product(turn[...], second_ref[...])
        if added is not None:
            first = first + refs[0][...].astype(WIDE)
            second = second + refs[1][...].astype(WIDE)
        refs[-3][...] = first.astype(LOW)
        refs[-2][...] = second.astype(LOW)

    inputs = [
        (left, (rows, part), lambda j: (0, offset)),
        (right, (rows, tile), lambda j: (0, j)),
        (right, (rows, tile), lambda j: (0, steps + j)),
    ]
    if added is not None:
        inputs.append((added, (part, tile), lambda j: (offset, j)))
        inputs.append((added, (part, tile), lambda j: (offset, steps + j)))
    out = (shape_of((part, half), LOW), (part, tile), lambda j: (0, j))
    return kernel_call(
        body,
        "two_terms",
        (steps,),
        inputs,
        [out, out],
        scratch=[pltpu.VMEM((part, rows), LOW)],
    )


def last_term(core, part, left, right, added, front, back, first):
    rows = left.shape[0]
    count = right.shape[1]
    half = part // 2
    if part % 128:
        total = outer_sum(left[:, :part], right)
        if added is not None:
            total = total + added[:part].astype(WIDE)
        total = total + front[:, first : first + count].astype(WIDE)
        total = total + back[:, first : first + count].astype(WIDE)
        kept = lax.dynamic_slice_in_dim(total, core[0] * half, half, 0)
        given = lax.dynamic_slice_in_dim(total, (1 - core[0]) * half, half, 0)
        return kept, given.astype(LOW)
    tile = 256

    def body(core_ref, left_ref, right_ref, front_ref, back_ref, *refs):
        kept_ref, given_ref, turn, total_ref = refs[-4:]

        @pl.when(pl.program_id(0) == 0)
        def _():
            turn[...] = left_ref[...].T

        total = product(turn[...], right_ref[...])
        total = total + front_ref[...].astype(WIDE) + back_ref[...].astype(WIDE)
        if added is not None:
            total = total + refs[0][...].astype(WIDE)
        total_ref[...] = total
        kept_ref[...] = total_ref[pl.ds(pl.multiple_of(core_ref[0] * half, half), half), :]
        given = pl.ds(pl.multiple_of((1 - core_ref[0]) * half, half), half)
        given_ref[...] = total_ref[given, :].astype(LOW)

    for size in (512, 1024):
        if count % size == 0 and first % size == 0:
            tile = size
    inputs = [
        (left, (rows, part), lambda j, _: (0, 0)),
        (right, (rows, tile), lambda j, _: (0, j)),
        (front, (part, tile), lambda j, _: (0, first // tile + j)),
        (back, (part, tile), lambda j, _: (0, first // tile + j)),
    ]
    if added is not None:
        inputs.append((added, (part, tile), lambda j, _: (0, j)))
    block = ((half, tile), lambda j, _: (0, j))
    return kernel_call(
        body,
        "last_term",
        (count // tile,),
        inputs,
        [(shape_of((half, count), WIDE),) + block, (shape_of((half, count), LOW),) + block],
        scratch=[pltpu.VMEM((part, rows), LOW), pltpu.VMEM((part, tile), WIDE)],
        prefetch=core,
    )


def assembled(core, kept, theirs, turned_over=False):
    rows, half = kept.shape

    def body(core_ref, kept_ref, theirs_ref, out_ref):
        mine = (pl.program_id(0) == core_ref[0]).astype(WIDE)
        value = kept_ref[...] * mine + theirs_ref[...].astype(WIDE) * (1.0 - mine)
        out_ref[...] = value.T if turned_over else value

    if turned_over:
        out = (shape_of((2 * half, rows), WIDE), (half, rows), lambda j, _: (j, 0))
    else:
        out = (shape_of((rows, 2 * half), WIDE), (rows, half), lambda j, _: (0, j))
    return kernel_call(
        body, "assembled", (2,), [(kept, None, None), (theirs, None, None)], [out], prefetch=core
    )[0]


def parted(core, kept, theirs, cols):
    rows, wide = kept.shape
    rest = wide - cols

    def body(core_ref, kept_ref, theirs_ref, both_ref, first_ref, second_ref):
        first_core = (core_ref[0] == 0).astype(WIDE)
        mine, other = kept_ref[...], theirs_ref[...].astype(WIDE)
        low = mine * first_core + other * (1.0 - first_core)
        high = other * first_core + mine * (1.0 - first_core)
        both_ref[:, :cols] = low[:, :cols]
        both_ref[:, cols:] = high[:, :cols]
        first_ref[...] = low[:, cols:]
        second_ref[...] = high[:, cols:]

    return kernel_call(
        body,
        "parted",
        (1,),
        [(kept, None, None), (theirs, None, None)],
        [
            (shape_of((rows, 2 * cols), WIDE), None, None),
            (shape_of((rows, rest), WIDE), None, None),
            (shape_of((rows, rest), WIDE), None, None),
        ],
        prefetch=core,
    )


def rowwise(body, name, row_inputs, whole_inputs, row_outputs, sum_outputs, block=128):
    count = row_inputs[0].shape[0]
    block = min(block, count)
    taken = len(row_inputs) + len(whole_inputs)

    def run(*refs):
        results = body(*(r[...] for r in refs[:taken]))
        outs = refs[taken:]
        for ref, value in zip(outs, results[: len(row_outputs)]):
            ref[...] = value.astype(ref.dtype)
        for ref, value in zip(outs[len(row_outputs) :], results[len(row_outputs) :]):

            @pl.when(pl.program_id(0) == 0)
            def _(ref=ref, value=value):
                ref[...] = value

            @pl.when(pl.program_id(0) > 0)
            def _(ref=ref, value=value):
                ref[...] += value

    def strip(shape):
        return ((block,) + shape[1:], lambda i: (i, 0))

    return kernel_call(
        run,
        name,
        (count // block,),
        [(a,) + strip(a.shape) for a in row_inputs] + [(a, None, None) for a in whole_inputs],
        [(shape_of((count, w), k),) + strip((count, w)) for w, k in row_outputs]
        + [(shape_of((1, w), WIDE), None, None) for w in sum_outputs],
    )


def stacked(*pieces):
    rows = sum(p.shape[0] for p in pieces)

    def body(*refs):
        at = 0
        for ref, piece in zip(refs, pieces):
            refs[-1][at : at + piece.shape[0], :] = ref[...]
            at += piece.shape[0]

    out = (shape_of((rows, pieces[0].shape[1]), pieces[0].dtype), None, None)
    return kernel_call(body, "stacked", (1,), [(p, None, None) for p in pieces], [out])[0]


def joined_chunks(chunks, first, count):
    part = chunks[0][0].shape[0]

    def body(*refs):
        for i, ref in enumerate(refs[:-1]):
            start = chunks[i][1] + first
            refs[-1][i * part : (i + 1) * part, :] = ref[:, start : start + count]

    out = (shape_of((part * len(chunks), count), LOW), None, None)
    return kernel_call(
        body, "joined_chunks", (1,), [(a, None, None) for a, _ in chunks], [out]
    )[0]


def multiplied(left, right, kind=WIDE):
    rows = left.shape[0]
    block = min(rows, 256)

    def body(left_ref, right_ref, out_ref):
        out_ref[...] = product(left_ref[...], right_ref[...]).astype(out_ref.dtype)

    return kernel_call(
        body,
        "multiplied",
        (rows // block,),
        [(left, (block, left.shape[1]), lambda i: (i, 0)), (right, None, None)],
        [(shape_of((rows, right.shape[1]), kind), (block, right.shape[1]), lambda i: (i, 0))],
    )[0]


def turned_products(pairs, kind):
    width = sum(right.shape[1] for _, right in pairs)
    tall = pairs[0][0].shape[1]
    block = 512
    rows = pairs[0][0].shape[0]

    def body(*refs):
        at = 0
        for i in range(len(pairs)):
            wide = pairs[i][1].shape[1]
            term = outer_sum(refs[2 * i][...], refs[2 * i + 1][...])
            refs[-1][:, at : at + wide] = term.astype(kind)
            at += wide

    inputs = []
    for left, right in pairs:
        inputs.append((left, (left.shape[0], block), lambda i: (0, i)))
        inputs.append((right, None, None))
    out = (shape_of((tall, width), kind), (block, width), lambda i: (i, 0))
    return kernel_call(body, "turned_products", (tall // block,), inputs, [out])[0]


def ring_terms(segments, part, ahead, behind, front, back, cut):
    width = sum(right.shape[1] for _, right, _ in segments)

    def plain(offset, received, first):
        columns = slice(offset * part, (offset + 1) * part)
        parts = []
        for left, right, added in segments:
            term = outer_sum(left[:, columns], right)
            if added is not None:
                term = term + added[columns].astype(WIDE)
            parts.append(term)
        total = jnp.concatenate(parts, axis=1)
        if received is not None:
            edge = (first, width - first - received.shape[1])
            total = total + jnp.pad(received.astype(WIDE), ((0, 0), edge))
        return total.astype(LOW)

    edges = [right.shape[1] for _, right, _ in segments]
    if part % 128:
        if front is None:
            return plain(ahead, None, 0)[:, :cut], plain(behind, None, 0)[:, cut:]
        return plain(ahead, front, 0), plain(behind, back, width - back.shape[1])
    if front is None:
        pair = segments
        if len(segments) == 1:
            left, right, added = segments[0]
            if 2 * cut == width:
                return two_terms(ahead, part, left, right, added)
            pair = [(left, right, added, 0, cut), (left, right, added, cut, width - cut)]
        return [one_term(ahead, part, *entry) for entry in pair]

    edges += [front.shape[1], width - back.shape[1]]
    tile = max(t for t in (256, 512, 1024) if all(e % t == 0 for e in edges))
    steps = width // tile
    front_steps, back_first = front.shape[1] // tile, steps - back.shape[1] // tile
    inputs, scratch, spans = [], [], []
    at = 0
    for left, right, added in segments:
        rows = left.shape[0]
        size = right.shape[1] // tile

        def column(j, at=at, size=size):
            return jnp.clip(j - at, 0, size - 1)

        inputs.append((left, (rows, part), lambda j: (0, ahead)))
        inputs.append((left, (rows, part), lambda j: (0, behind)))
        inputs.append((right, (rows, tile), lambda j, column=column: (0, column(j))))
        if added is not None:
            inputs.append((added, (part, tile), lambda j, column=column: (ahead, column(j))))
            inputs.append((added, (part, tile), lambda j, column=column: (behind, column(j))))
        same = [i for i, (other, _, _) in enumerate(segments) if other is left][0]
        scratch.append(pltpu.VMEM((2, part, rows) if len(spans) == same else (8, 128), LOW))
        spans.append((at, at + size, added is not None, same))
        at += size
    inputs.append((front, (part, tile), lambda j: (0, jnp.clip(j, 0, front_steps - 1))))
    inputs.append((back, (part, tile), lambda j: (0, jnp.clip(j - back_first, 0, steps))))

    def body(*refs):
        refs = list(refs)
        turned = refs[len(inputs) + 2 :]
        front_ref, back_ref = refs[len(inputs) - 2 : len(inputs)]
        outs = refs[len(inputs) : len(inputs) + 2]
        step = pl.program_id(0)
        had_front = (step < front_steps).astype(WIDE)
        had_back = (step >= back_first).astype(WIDE)
        place = 0
        for at, (first, last, adds, same) in enumerate(spans):
            mine = refs[place : place + (5 if adds else 3)]
            place += len(mine)
            turn = turned[same]

            if same == at:

                @pl.when(step == 0)
                def _(mine=mine, turn=turn):
                    turn[0] = mine[0][...].T
                    turn[1] = mine[1][...].T

            @pl.when((step >= first) & (step < last))
            def _(mine=mine, turn=turn, adds=adds):
                right = mine[2][...]
                for way, received, had in ((0, front_ref, had_front), (1, back_ref, had_back)):
                    total = product(turn[way], right) + received[...].astype(WIDE) * had
                    if adds:
                        total = total + mine[3 + way][...].astype(WIDE)
                    outs[way][...] = total.astype(LOW)

    out = (shape_of((part, width), LOW), (part, tile), lambda j: (0, j))
    flops = sum(4 * part * right.size for _, right, _ in segments)
    return kernel_call(
        body, "ring_terms", (steps,), inputs, [out, out], scratch=scratch, flops=flops
    )


def turned(value, gain, cosines, sines):
    scale = lax.rsqrt(jnp.mean(value * value, axis=-1, keepdims=True) + EPSILON)
    return rotary(value * scale * gain, cosines, sines).astype(LOW), scale


def hidden_scores(places):
    query_place, query_start, key_place, key_start, total_rows = places
    distance = query_place - key_place
    near = (distance >= 0) & (distance < WIN)
    visible = (key_place >= 0) & (key_place < total_rows) & (near | (query_start == key_start))
    return jnp.where(visible, 0.0, NEGATIVE)


def head_specs(own, other, heads_own):
    rows = own.shape[0]
    return [
        (own, (rows, HD), lambda h: (0, jnp.minimum(h, heads_own - 1))),
        (other, (rows, HD), lambda h: (0, jnp.maximum(h - heads_own, 0))),
    ]


def attention(own, other, heads, gain, cosines, sines, keys, values, places, total_rows):
    rows = own.shape[0]
    heads_own = heads // 2
    scale = HD ** (-0.5)

    def body(own_ref, other_ref, gain_ref, cos_ref, sin_ref, pair_ref, qp, qs, kp, ks, out_own, out_other, log_ref, hide_ref):
        head = pl.program_id(0)

        @pl.when(head == 0)
        def _():
            hide_ref[...] = hidden_scores((qp[...], qs[...], kp[...], ks[...], total_rows))

        raw = jnp.where(head < heads_own, own_ref[...], other_ref[...])
        query, _ = turned(raw, gain_ref[...], cos_ref[...], sin_ref[...])
        scores = back_product(pair_ref[:, :HD], query) * scale + hide_ref[...]
        peak = jnp.max(scores, axis=0, keepdims=True)
        log_total = peak + jnp.log(jnp.sum(jnp.exp(scores - peak), axis=0, keepdims=True))
        weights = jnp.exp(scores - log_total).astype(LOW)
        result = outer_sum(weights, pair_ref[:, HD:]).astype(LOW)
        log_ref[0] = log_total

        @pl.when(head < heads_own)
        def _():
            out_own[...] = result

        @pl.when(head >= heads_own)
        def _():
            out_other[...] = result

    whole = [(a, None, None) for a in (gain, cosines, sines, keys) + tuple(places)]
    half = shape_of((rows, heads_own * HD), LOW)
    return kernel_call(
        body,
        "attention",
        (heads,),
        head_specs(own, other, heads_own) + whole,
        head_specs(half, half, heads_own)
        + [(shape_of((heads, 1, rows), WIDE), (1, 1, rows), lambda h: (h, 0, 0))],
        scratch=[pltpu.VMEM((keys.shape[0], rows), WIDE)],
    )


def attention_back(own, other, heads, gain, cosines, sines, keys, places, total_rows, log_total, upstream, weights_own, weights_other):
    rows = own.shape[0]
    heads_own = heads // 2
    scale = HD ** (-0.5)
    tail = keys.shape[0] - 2 * rows

    def body(own_ref, other_ref, weight_own, weight_other, gain_ref, cos_ref, sin_ref, pair_ref, up_ref, qp, qs, kp, ks, log_ref, query_own, query_other, before_out, here_out, after_out, slope_out, hide_ref, total_ref):
        head = pl.program_id(0)

        @pl.when(head == 0)
        def _():
            hide_ref[...] = hidden_scores((qp[...], qs[...], kp[...], ks[...], total_rows))
            total_ref[...] = jnp.zeros_like(total_ref)
            slope_out[...] = jnp.zeros_like(slope_out)

        raw = jnp.where(head < heads_own, own_ref[...], other_ref[...])
        weight = jnp.where(head < heads_own, weight_own[...], weight_other[...])
        up = product(up_ref[...], weight).astype(LOW)
        gain_row, cos, sin = gain_ref[...], cos_ref[...], sin_ref[...]
        query, shrink = turned(raw, gain_row, cos, sin)
        key = pair_ref[:, :HD]
        scores = back_product(key, query) * scale + hide_ref[...]
        weights = jnp.exp(scores - log_ref[0])
        pulled = back_product(pair_ref[:, HD:], up)
        centre = jnp.sum(weights * pulled, axis=0, keepdims=True)
        scores_back = (weights * (pulled - centre)).astype(LOW)
        total_ref[:, :HD] += product(scores_back, query) * scale
        total_ref[:, HD:] += product(weights.astype(LOW), up)
        turned_back = outer_sum(scores_back, key) * scale
        normed_up = rotary(turned_back, cos, -sin)
        shape = raw * shrink
        slope_out[...] += jnp.sum(normed_up * shape, axis=0, keepdims=True)
        inner = normed_up * gain_row
        raw_back = shrink * (inner - shape * jnp.mean(inner * shape, axis=-1, keepdims=True))

        @pl.when(head < heads_own)
        def _():
            query_own[...] = raw_back.astype(LOW)

        @pl.when(head >= heads_own)
        def _():
            query_other[...] = raw_back.astype(LOW)

        @pl.when(head == heads - 1)
        def _():
            before_out[...] = total_ref[:rows].astype(LOW)
            here_out[...] = total_ref[rows : 2 * rows]
            after_out[...] = total_ref[2 * rows :].astype(LOW)

    whole = [(a, None, None) for a in (gain, cosines, sines, keys, upstream) + tuple(places)]
    half = shape_of((rows, heads_own * HD), LOW)
    deep = weights_own.shape[0]
    weight_specs = [
        (weights_own, (deep, HD), lambda h: (0, jnp.minimum(h, heads_own - 1))),
        (weights_other, (deep, HD), lambda h: (0, jnp.maximum(h - heads_own, 0))),
    ]
    return kernel_call(
        body,
        "attention_back",
        (heads,),
        head_specs(own, other, heads_own)
        + weight_specs
        + whole
        + [(log_total, (1, 1, rows), lambda h: (h, 0, 0))],
        head_specs(half, half, heads_own)
        + [
            (shape_of((rows, 2 * HD), LOW), None, None),
            (shape_of((rows, 2 * HD), WIDE), None, None),
            (shape_of((tail, 2 * HD), LOW), None, None),
            (shape_of((1, HD), WIDE), None, None),
        ],
        scratch=[pltpu.VMEM((keys.shape[0], rows), WIDE), pltpu.VMEM((keys.shape[0], 2 * HD), WIDE)],
    )


def keyed(own, other, cols, cosines, sines, gain, flag):
    def body(mine, theirs, cos, sin, gain_row, flag_row):
        first, second = mine[:, cols:], theirs[:, cols:]
        key = jnp.where(flag_row > 0, first, second)
        value = jnp.where(flag_row > 0, second, first)
        return (jnp.concatenate([rotary(normed(key, gain_row), cos, sin), value], axis=1),)

    return rowwise(
        body, "keyed", [own, other, cosines, sines], [gain, flag], [(2 * HD, LOW)], [], 256
    )[0]


def keyed_back(tp_table, here, later, earlier, query_own, query_other, own, other, cols, cosines, sines, gain, flag):
    rows = here.shape[0]
    block = earlier.shape[0]

    def body(tp_ref, here_ref, later_ref, earlier_ref, query_mine, query_theirs, mine, theirs, cos, sin, gain_row, flag_row, own_out, other_out, slope_out):
        got = (pl.program_id(0) == tp_ref[0]).astype(WIDE)
        total = here_ref[...] + later_ref[...].astype(WIDE) + earlier_ref[...].astype(WIDE) * got
        flagged = flag_row[...] > 0
        key = jnp.where(flagged, mine[...], theirs[...])
        key_back, slope = normed_back(
            key, gain_row[...], rotary(total[:, :HD], cos[...], -sin[...])
        )
        value_back = total[:, HD:]
        wide = query_mine.shape[1]
        own_out[:, :wide] = query_mine[...]
        other_out[:, :wide] = query_theirs[...]
        own_out[:, wide:] = jnp.where(flagged, key_back, value_back).astype(LOW)
        other_out[:, wide:] = jnp.where(flagged, value_back, key_back).astype(LOW)

        @pl.when(pl.program_id(0) == 0)
        def _():
            slope_out[...] = slope

        @pl.when(pl.program_id(0) > 0)
        def _():
            slope_out[...] += slope

    def strip(array):
        return (array, (block, array.shape[1]), lambda i, _: (i, 0))

    raw = [(a, (block, HD), lambda i, _: (i, cols // HD)) for a in (own, other)]
    out = strip(shape_of((rows, cols + HD), LOW))
    return kernel_call(
        body,
        "keyed_back",
        (rows // block,),
        [strip(here), strip(later), (earlier, None, None), strip(query_own), strip(query_other)]
        + raw
        + [strip(cosines), strip(sines), (gain, None, None), (flag, None, None)],
        [out, out, (shape_of((1, HD), WIDE), None, None)],
        prefetch=tp_table,
    )


def merged_rows(residual, mine, theirs, low, left, right, gains):
    def body(residual, mine, theirs, low, left, right, gains):
        gain_in, gain_mixer, gain_laurel, gain_next = (gains[i : i + 1] for i in range(4))
        mixer = mine + theirs.astype(WIDE)
        middle = product(low, left).astype(LOW)
        laurel = back_product(middle, right)
        total = (
            residual
            + normed(mixer, gain_mixer)
            + normed(residual, gain_in)
            + normed(laurel, gain_laurel)
        ) * HALF_ROOT
        return mixer, laurel, middle, total, normed(total, gain_next)

    width = residual.shape[1]
    kinds = [(width, WIDE), (width, WIDE), (left.shape[1], LOW), (width, WIDE), (width, LOW)]
    return rowwise(
        body, "merged_rows", [residual, mine, theirs, low], [left, right, gains], kinds, []
    )


def branched(merged, upstream, extra, dense, orders, branch, project, gains):
    def body(merged, upstream, extra, *rest):
        sums = rest[: 3 * len(orders)]
        branch, project, gains = rest[3 * len(orders) :]
        gain_dense, gain_branch = gains[4:5], gains[5:6]
        parts = {}
        for i, group in enumerate(orders):
            near, far, peer = sums[3 * i : 3 * i + 3]
            total = near + far.astype(WIDE) + peer.astype(WIDE)
            part = total.shape[1] // len(group)
            for k, offset in enumerate(group):
                parts[offset] = total[:, k * part : (k + 1) * part]
        dense = jnp.concatenate([parts[o] for o in sorted(parts)], axis=1)
        middle = merged + normed(dense, gain_dense)
        middle_low = middle.astype(LOW)
        raw = product(middle_low, branch)
        extra = extra.astype(WIDE)
        active = smooth_gate(raw)
        low = (active * extra).astype(LOW)
        projected = back_product(low, project)
        result = middle + normed(projected, gain_branch)
        project_back, branch_slope = normed_back(projected, gain_branch, upstream)
        project_low = project_back.astype(LOW)
        pulled = product(project_low, project)
        raw_back = gate_back(raw, pulled * extra).astype(LOW)
        middle_back = upstream + back_product(raw_back, branch)
        dense_back, dense_slope = normed_back(dense, gain_dense, middle_back)
        return (
            result, pulled * active, project_low, low, raw_back, middle_low, middle_back,
            dense_back, branch_slope, dense_slope,
        )

    width, side = merged.shape[1], extra.shape[1]
    kinds = [
        (width, LOW), (side, WIDE), (width, LOW), (side, LOW), (side, LOW), (width, LOW),
        (width, WIDE), (width, LOW),
    ]
    return rowwise(
        body,
        "branched",
        [merged, upstream, extra] + [a for group in dense for a in group],
        [branch, project, gains],
        kinds,
        [width, width],
    )


def merged_back(near, far, peer, merged, middle_back, mixer, laurel, right, gains):
    def body(merged, near, far, peer, middle_back, mixer, laurel, right, gains):
        gain_next, gain_mixer, gain_laurel = gains[3:4], gains[1:2], gains[2:3]
        pulled = near + far.astype(WIDE) + peer.astype(WIDE)
        extra, next_slope = normed_back(merged, gain_next, pulled)
        total = (middle_back + extra) * HALF_ROOT
        mixer_back, mixer_slope = normed_back(mixer, gain_mixer, total)
        laurel_back, laurel_slope = normed_back(laurel, gain_laurel, total)
        laurel_low = laurel_back.astype(LOW)
        middle = product(laurel_low, right)
        return total, mixer_back, laurel_low, middle, next_slope, mixer_slope, laurel_slope

    width = merged.shape[1]
    kinds = [(width, WIDE), (width, LOW), (width, LOW), (right.shape[1], LOW)]
    return rowwise(
        body,
        "merged_back",
        [merged, near, far, peer, middle_back, mixer, laurel],
        [right, gains],
        kinds,
        [width] * 3,
    )


def opened_back(mine, theirs, middle, total, residual, left, gain):
    def body(mine, theirs, middle, total, residual, left, gains):
        gain = gains[0:1]
        pulled = mine + theirs.astype(WIDE) + back_product(middle, left) + total
        back, slope = normed_back(residual, gain, pulled)
        return total + back, slope

    width = residual.shape[1]
    return rowwise(
        body,
        "opened_back",
        [mine, theirs, middle, total, residual],
        [left, gain],
        [(width, WIDE)],
        [width],
    )


def doubled(own, other, first_row, row_count, weights_own, weights_other, kind):
    def body(own_ref, other_ref, weight_own, weight_other, out_ref):
        total = back_product(own_ref[...], weight_own[...])
        total = total + back_product(other_ref[...], weight_other[...])
        out_ref[...] = total.astype(kind)

    start = first_row // row_count
    tall = weights_own.shape[0]
    block = 512
    return kernel_call(
        body,
        "doubled",
        (tall // block,),
        [
            (own, (row_count, own.shape[1]), lambda i: (start, 0)),
            (other, (row_count, other.shape[1]), lambda i: (start, 0)),
            (weights_own, (block, own.shape[1]), lambda i: (i, 0)),
            (weights_other, (block, other.shape[1]), lambda i: (i, 0)),
        ],
        [(shape_of((row_count, tall), kind), (row_count, block), lambda i: (0, i))],
    )[0]


def added_low(near, far, first_row):
    rows = near.shape[0] - first_row

    def body(near_ref, far_ref, out_ref):
        out_ref[...] = (near_ref[...] + far_ref[...].astype(WIDE)).astype(LOW)

    block = ((rows, near.shape[1]), lambda i: (first_row // rows, 0))
    return kernel_call(
        body,
        "added_low",
        (1,),
        [(near,) + block, (far,) + block],
        [(shape_of((rows, near.shape[1]), LOW), None, None)],
    )[0]


def shifted(block, distance):
    devices = range(lax.axis_size("seq"))
    route = [(i - distance, i) for i in devices if i - distance in devices]
    return lax.ppermute(block, "seq", route)


def tp_swap(block):
    return lax.ppermute(block, "tp", [(0, 1), (1, 0)])


def core_swap(block):
    return lax.ppermute(block, "seq", [(i, i ^ 1) for i in range(lax.axis_size("seq"))])


class Line:
    def __init__(self, mark):
        self.mark = mark

    def pin(self, values):
        values, self.mark = lax.optimization_barrier((values, self.mark))
        return values


class Ring:
    def __init__(self):
        self.chips = lax.axis_size("seq") // 2
        rows = self.chips // 2
        self.order = [2 * i for i in range(rows)] + [2 * i + 1 for i in reversed(range(rows))]
        place = [0] * self.chips
        for position, member in enumerate(self.order):
            place[member] = position
        mine = jnp.asarray(place, jnp.int32)[lax.axis_index("seq") // 2]
        offsets = (mine + jnp.arange(self.chips, dtype=jnp.int32)) % self.chips
        self.owners = jnp.asarray(self.order, jnp.int32)[offsets]

    def moved(self, block, step):
        n = self.chips
        route = [
            (self.order[p] * 2 + core, self.order[(p + step) % n] * 2 + core)
            for p in range(n)
            for core in range(2)
        ]
        return lax.ppermute(block, "seq", route)


class Gather:
    def __init__(self, ring, line, chunk, cut):
        self.ring = ring
        self.line = line
        self.cut = cut
        self.found = [None] * ring.chips
        self.found[0] = chunk
        self.count = 0

    def send(self):
        n = self.ring.chips
        self.count += 1
        k = self.count
        behind, ahead = (n - k + 1) % n, k - 1
        held = self.line.pin({o: self.found[o] for o in {behind, ahead}})
        self.found[behind], self.found[ahead] = held[behind], held[ahead]
        if k < n // 2:
            self.found[n - k] = self.ring.moved(held[behind], 1)
            self.found[k] = self.ring.moved(held[ahead], -1)
        else:
            self.found[k] = (
                self.ring.moved(held[behind][:, : self.cut], 1),
                self.ring.moved(held[ahead][:, self.cut :], -1),
            )

    def land(self):
        n = self.ring.chips
        new = {n - self.count, self.count}
        landed = self.line.pin({o: self.found[o] for o in new})
        for o in new:
            self.found[o] = landed[o]

    def finish(self):
        while self.count < self.ring.chips // 2:
            self.send()
            self.land()

    def columns(self, first, count):
        listed = []
        for chunk in self.found:
            if isinstance(chunk, tuple):
                half = first >= self.cut
                listed.append((chunk[half], first - self.cut * half))
            else:
                listed.append((chunk, first))
        return listed

    def joined(self, first, count):
        return jnp.concatenate(
            [a[:, start : start + count] for a, start in self.columns(first, count)], axis=0
        )


class Scatter:
    def __init__(self, ring, line, segments, part, cut):
        self.ring = ring
        self.line = line
        self.segments = segments
        self.part = part
        self.cut = cut
        self.count = 0
        self.front = self.back = None

    def prepare(self):
        n = self.ring.chips
        pair = ring_terms(
            self.segments,
            self.part,
            n // 2 - self.count,
            n // 2 + self.count,
            self.front,
            self.back,
            self.cut,
        )
        self.front, self.back = self.line.pin(tuple(pair))
        self.count += 1

    def send(self):
        front, back = self.line.pin((self.front, self.back))
        self.front, self.back = self.ring.moved(front, 1), self.ring.moved(back, -1)

    def land(self):
        self.front, self.back = self.line.pin((self.front, self.back))

    def left(self):
        return self.ring.chips // 2 - self.count

    def total(self, core):
        front, back = self.line.pin((self.front, self.back))
        results = []
        at = 0
        for left, right, added in self.segments:
            results.append(
                last_term(core, self.part, left, right, added, front, back, at)
            )
            at += right.shape[1]
        return results


def shards(
    hidden,
    layer_input,
    cotangent,
    span_starts,
    query_weight,
    key_weight,
    value_weight,
    output_weight,
    laurel_left,
    laurel_right,
    gate_weight,
    upward_weight,
    down_weight,
    branch_gate,
    branch_output,
    input_gain,
    query_gain,
    key_gain,
    mixer_gain,
    laurel_gain,
    prefeed_gain,
    postfeed_gain,
    branch_gain,
):
    tp_size = lax.axis_size("tp")
    seq_place = lax.axis_index("seq")
    tp_place = lax.axis_index("tp")
    core = seq_place % 2
    first_core = core == 0
    first_tp = tp_place == 0
    ring = Ring()
    line = Line(input_gain)
    pin = line.pin
    chips = ring.chips
    half_chips = chips // 2
    local_rows, width = hidden.shape
    block_rows = local_rows * tp_size
    total_rows = span_starts.shape[0]
    query_heads = QH // tp_size
    part = width // chips
    everywhere = ("seq", "tp")

    core_table = core[None].astype(jnp.int32)
    tp_table = tp_place[None].astype(jnp.int32)
    query_cols, output_width = query_weight.shape[1] // 2, output_weight.shape[0] // 2
    key_value = jnp.concatenate([key_weight, value_weight], axis=1)
    first_cols = query_cols + key_weight.shape[1]
    first_weights = (query_weight, key_value, output_weight.T)
    first_given = pin(weights_given(core_table, first_weights))
    first_theirs = core_swap(first_given)
    dense_weights = (gate_weight, upward_weight, down_weight.T)
    units = gate_weight.shape[1] // 2
    side, rank = branch_gate.shape[1], laurel_left.shape[1]
    gains = jnp.stack(
        [line.mark, mixer_gain, laurel_gain, prefeed_gain, postfeed_gain, branch_gain] * 2
    )[:8]
    small = jnp.concatenate([branch_gate, branch_output.T, laurel_left, laurel_right.T], axis=1)
    dense_weights, gains, small = pin((dense_weights, gains, small))
    dense_given = pin(weights_given(core_table, dense_weights))
    (first_pack,) = pin(
        weights_merged(core_table, first_weights, pin(first_theirs), ((0, 1, 2),))
    )
    first = Gather(ring, line, first_pack, first_cols)
    swapped_chunks = [None] * chips

    def swap_chunks(*offsets):
        for o in offsets:
            chunk = first.found[o]
            swapped_chunks[o] = (
                tuple(core_swap(a) for a in chunk) if isinstance(chunk, tuple) else core_swap(chunk)
            )

    def land_chunks(*offsets):
        for o in offsets:
            swapped_chunks[o] = pin(swapped_chunks[o])

    first.send()
    residual, upstream, gains = pin(
        permuted([hidden, cotangent, gains], [WIDE, WIDE, WIDE], ring.owners)
    )
    line.mark = gains
    (normed_low,) = rowwise(
        lambda value, gains: (normed(value, gains[0:1]),),
        "opened",
        [residual],
        [gains],
        [(width, LOW)],
        [],
    )
    normed_low = pin(normed_low)
    first.land()

    first.send()
    dense_theirs = core_swap(dense_given)
    rows_theirs = tp_swap(normed_low)
    swap_chunks(0, chips - 1, 1)
    expand_pack, down_pack = pin(
        weights_merged(core_table, dense_weights, pin(dense_theirs), ((0, 1), (2,)))
    )
    land_chunks(0, chips - 1, 1)
    first.land()
    while first.count < half_chips - 1:
        first.send()
        swap_chunks(chips - first.count + 1, first.count - 1)
        land_chunks(chips - first.count + 1, first.count - 1)
        first.land()
    expand = Gather(ring, line, expand_pack, units)
    down = Gather(ring, line, down_pack, units // 2)
    first.send()
    swap_chunks(half_chips + 1, half_chips - 1)
    start_row = seq_place * block_rows
    padded_starts = jnp.concatenate(
        [jnp.full((block_rows,), -1, jnp.int32), span_starts, jnp.full((PIC,), -1, jnp.int32)]
    )
    span = 2 * block_rows + PIC
    ahead_of = jnp.arange(span, dtype=jnp.int32)
    swapped = jnp.where(
        ahead_of < 2 * block_rows, ahead_of ^ (tp_place * local_rows), ahead_of
    )
    key_place = start_row - block_rows + swapped
    starts = lax.dynamic_slice_in_dim(padded_starts, start_row, span)
    blocks = [starts[i * local_rows : (i + 1) * local_rows] for i in range(4)]
    key_start = jnp.where(
        first_tp,
        starts,
        jnp.concatenate([blocks[1], blocks[0], blocks[3], blocks[2], starts[2 * block_rows :]]),
    )
    row_place = key_place[block_rows : 2 * block_rows]
    row_start = key_start[block_rows : 2 * block_rows]
    places = (row_place[None, :], row_start[None, :], key_place[:, None], key_start[:, None])
    frequency = ROPE_BASE ** (-(jnp.arange(HD // 2, dtype=WIDE) * 2.0) / HD)
    theta = row_place.astype(WIDE)[:, None] * frequency[None, :]
    flag = jnp.broadcast_to(jnp.where(first_core, 1.0, 0.0), (1, HD))
    cosines, sines, places, flag = pin((jnp.cos(theta), jnp.sin(theta), places, flag))
    query_gain_row, key_gain_row = query_gain[None, :], key_gain[None, :]
    land_chunks(half_chips + 1, half_chips - 1)
    rows_theirs = pin(rows_theirs)
    first.land()

    expand.send()
    small_full = lax.all_gather(pin(small), everywhere, axis=0, tiled=True)
    swap_chunks(half_chips)
    land_chunks(half_chips)
    rows_low = pin(stacked(normed_low, rows_theirs))

    def columns(found, start, count):
        listed = []
        for chunk in found:
            if isinstance(chunk, tuple):
                half = start >= first_cols
                listed.append((chunk[half], start - first_cols * half))
            else:
                listed.append((chunk, start))
        return joined_chunks(listed, 0, count)

    first_own = pin(columns(first.found, 0, first_cols))
    first_other = pin(columns(swapped_chunks, 0, first_cols))
    raw_own = pin(multiplied(rows_low, first_own))
    raw_other = pin(multiplied(rows_low, first_other))
    pair_low = pin(
        keyed(raw_own, raw_other, query_cols, cosines, sines, key_gain_row, flag)
    )
    early = pin(lax.dynamic_slice_in_dim(pair_low, tp_place * local_rows, PIC, 0))
    pairs_before, pairs_after = shifted(pair_low, 1), shifted(early, -1)
    output_own_full = pin(columns(first.found, first_cols, output_width))
    output_other_full = pin(columns(swapped_chunks, first_cols, output_width))
    pairs_before, pairs_after = pin((pairs_before, pairs_after))
    expand.land()
    expand.send()
    pairs_all = pin(stacked(pairs_before, pair_low, pairs_after))
    attended_own, attended_other, log_total = pin(
        attention(
            raw_own, raw_other, query_heads, query_gain_row, cosines, sines, pairs_all, pairs_all,
            places, total_rows,
        )
    )

    def output_product(first_row, kind):
        return pin(
            doubled(
                attended_own, attended_other, first_row, local_rows, output_own_full,
                output_other_full, kind,
            )
        )

    mixer_theirs = tp_swap(output_product(local_rows, LOW))
    mixer_mine = output_product(0, WIDE)
    mixer_theirs, small_full = pin((mixer_theirs, small_full))
    expand.land()
    expand.send()
    branch_full, project_full, left_full, right_full = pin(
        permuted_rows(small_full, ring.owners, (side, side, rank, rank))
    )
    mixer_raw, laurel_raw, laurel_mid, merged, dense_low = pin(
        merged_rows(
            residual, mixer_mine, mixer_theirs, normed_low, left_full, right_full, gains
        )
    )

    theirs, far = tp_swap(dense_low), core_swap(dense_low)
    theirs, far = pin((theirs, far))
    expand.land()
    while expand.count < half_chips - 1:
        expand.send()
        expand.land()
    expand.send()
    last = pin(core_swap(theirs))
    dense_rows = pin(stacked(dense_low, theirs, far, last))
    expand.land()
    down.send()
    gate_columns, upward_columns = pin(
        (
            [a for a, _ in expand.columns(0, units)],
            [a for a, _ in expand.columns(units, units)],
        )
    )
    gates = list(zip(gate_columns, (f for _, f in expand.columns(0, units))))
    upwards = list(zip(upward_columns, (f for _, f in expand.columns(units, units))))
    gate_raw, upward_raw, inner_low = pin(expanded(dense_rows, gates, upwards, units))
    down.land()
    orders, dense_sums = [], []

    def down_chunk(offset):
        chunk = down.found[offset]
        return chunk if isinstance(chunk, tuple) else (chunk,)

    def dense_send(offsets):
        chunks = pin([down_chunk(o) for o in offsets])
        far = pin(contracted(inner_low, block_rows, block_rows, chunks, LOW))
        far = core_swap(far)
        near = pin(contracted(inner_low, 0, block_rows, chunks, WIDE))
        far = pin(far)
        peer = pin(added_low(near, far, local_rows))
        orders.append(offsets)
        dense_sums.append((near, far, tp_swap(peer)))

    for near in range(1, half_chips + 1):
        if down.count < half_chips:
            down.send()
        if near == 1:
            dense_send([chips - 1, 0, 1])
        else:
            dense_send([chips - near, near] if near < half_chips else [near])
        if near < half_chips:
            down.land()
        if near > 1:
            dense_sums[near - 2] = pin(dense_sums[near - 2])
    dense_sums[-1] = pin(dense_sums[-1])
    (
        result, layer_delta, project_low, branch_low, branch_raw_back, middle_low, middle_back,
        dense_low_back, branch_slope, postfeed_slope,
    ) = pin(
        branched(
            merged, upstream, layer_input, dense_sums, orders, branch_full, project_full,
            gains,
        )
    )

    theirs, far = tp_swap(dense_low_back), core_swap(dense_low_back)
    gate_raw, upward_raw = pin(gate_slopes(*pin((gate_raw, upward_raw))))
    theirs, far = pin((theirs, far))
    last = pin(core_swap(theirs))
    dense_rows_back = pin(stacked(dense_low_back, theirs, far, last))
    down_ring = Scatter(ring, line, [(dense_rows_back, inner_low, None)], part, units // 2)
    down_ring.prepare()
    down_ring.send()
    gate_raw_back, upward_raw_back = pin(
        inner_pulled(
            pin(dense_rows_back), [down_chunk(o) for o in range(chips)], gate_raw, upward_raw
        )
    )
    gate_ring = Scatter(ring, line, [(dense_rows, gate_raw_back, None)], part, units // 2)
    upward_ring = Scatter(ring, line, [(dense_rows, upward_raw_back, None)], part, units // 2)
    gate_ring.prepare()
    down_ring.land()
    gate_ring.send()
    upward_ring.prepare()
    gate_ring.land()
    upward_ring.send()
    down_ring.prepare()
    upward_ring.land()

    def dense_back(first_row, row_count, kind):
        left, right = pin((gate_raw_back, upward_raw_back))
        return pin(rows_pulled(left, right, first_row, row_count, gates, upwards, kind))

    down_ring.send()
    far_given = dense_back(block_rows, block_rows, LOW)
    gate_ring.prepare()
    down_ring.land()
    gate_ring.send()
    far_back = core_swap(far_given)
    near_back = dense_back(0, block_rows, WIDE)
    upward_ring.prepare()
    far_back = pin(far_back)
    gate_ring.land()
    upward_ring.send()
    peer_given = pin(added_low(near_back, far_back, local_rows))
    down_ring.prepare()
    upward_ring.land()
    down_ring.send()
    peer_back = tp_swap(peer_given)
    (result,) = pin(permuted([result], [LOW], ring.owners, inverse=True))
    gate_ring.prepare()
    peer_back = pin(peer_back)
    down_ring.land()
    gate_ring.send()
    (
        summed_back, mixer_low_back, laurel_raw_low, laurel_mid_back, prefeed_slope, mixer_slope,
        laurel_slope,
    ) = pin(
        merged_back(
            near_back, far_back, peer_back, merged, middle_back, mixer_raw, laurel_raw,
            right_full, gains,
        )
    )
    upward_ring.prepare()
    gate_ring.land()
    upward_ring.send()
    mixer_theirs_back = tp_swap(mixer_low_back)
    small_delta = turned_products(
        [
            (middle_low, branch_raw_back),
            (project_low, branch_low),
            (normed_low, laurel_mid_back),
            (laurel_raw_low, laurel_mid),
        ],
        LOW,
    )
    (small_delta,) = pin(
        permuted_rows(pin(small_delta), ring.owners, (2 * side + 2 * rank,), inverse=True)
    )
    down_ring.prepare()
    mixer_theirs_back = pin(mixer_theirs_back)
    upward_ring.land()
    down_ring.send()
    small_delta = lax.psum_scatter(small_delta, everywhere, scatter_dimension=0, tiled=True)
    mixer_rows_back = pin(stacked(mixer_low_back, mixer_theirs_back))
    query_own_back, query_other_back, pairs_sent, pairs_here, pairs_late, query_slope = pin(
        attention_back(
            raw_own, raw_other, query_heads, query_gain_row, cosines, sines, pairs_all, places,
            total_rows, log_total, mixer_rows_back, output_own_full, output_other_full,
        )
    )
    gate_ring.prepare()
    down_ring.land()
    gate_ring.send()
    later, earlier = shifted(pairs_sent, -1), shifted(pairs_late, 1)
    output_given = pin(turned_products([(mixer_rows_back, attended_other)], LOW))
    upward_ring.prepare()
    later, earlier = pin((later, earlier))
    gate_ring.land()
    upward_ring.send()
    output_theirs = core_swap(output_given)
    first_own_back, first_other_back, key_slope = pin(
        keyed_back(
            tp_table, pairs_here, later, earlier, query_own_back, query_other_back, raw_own,
            raw_other, query_cols, cosines, sines, key_gain_row, flag,
        )
    )
    first_given_back = pin(turned_products([(rows_low, first_other_back)], LOW))
    first_theirs_back = core_swap(first_given_back)

    def rows_back(first_row, kind):
        return pin(
            doubled(
                first_own_back, first_other_back, first_row, local_rows, first_own, first_other,
                kind,
            )
        )

    rows_given = rows_back(local_rows, LOW)
    output_theirs = pin(output_theirs)
    output_ring = Scatter(
        ring, line, [(mixer_rows_back, attended_own, output_theirs)], part, output_width // 2
    )
    output_ring.prepare()
    rows_mine = rows_back(0, WIDE)
    while down_ring.left():
        down_ring.prepare()
        down_ring.send()
        down_ring.land()
    ((down_kept, down_given),) = pin(down_ring.total(core_table))
    first_theirs_back = pin(first_theirs_back)
    upward_ring.land()
    for stream in (gate_ring, upward_ring):
        while stream.left():
            stream.prepare()
            stream.send()
            stream.land()
    first_ring = Scatter(
        ring, line, [(rows_low, first_own_back, first_theirs_back)], part, first_cols - HD
    )
    output_ring.send()
    rows_theirs = tp_swap(rows_given)
    down_theirs = core_swap(down_given)
    first_ring.prepare()
    output_ring.land()
    first_ring.send()
    output_ring.prepare()
    rows_theirs = pin(rows_theirs)
    first_ring.land()
    output_ring.send()
    first_ring.prepare()
    hidden_delta, input_slope = opened_back(
        rows_mine, rows_theirs, laurel_mid_back, summed_back, residual, left_full, line.mark
    )
    slopes = jnp.concatenate(
        [
            input_slope,
            mixer_slope,
            laurel_slope,
            prefeed_slope,
            postfeed_slope,
            branch_slope,
            jnp.pad(jnp.concatenate([query_slope, key_slope], axis=1), ((0, 1), (0, width - 2 * HD))),
        ],
    )
    hidden_delta, gain_slopes = permuted(
        [hidden_delta, slopes], [WIDE, WIDE], ring.owners, inverse=True
    )
    slopes = jnp.concatenate([gain_slopes[:6], slopes[6:]])
    line.mark = hidden_delta
    output_ring.land()
    slopes = lax.all_gather(pin(slopes)[None], everywhere, axis=0, tiled=True)
    first_ring.send()
    output_ring.prepare()
    ((gate_kept, gate_given),) = pin(gate_ring.total(core_table))
    first_ring.land()
    output_ring.send()
    gate_theirs = core_swap(gate_given)
    first_ring.prepare()
    ((upward_kept, upward_given),) = pin(upward_ring.total(core_table))
    down_theirs, gate_theirs = pin((down_theirs, gate_theirs))
    output_ring.land()
    first_ring.send()
    upward_theirs = core_swap(upward_given)
    output_ring.prepare()
    down_delta = pin(assembled(core_table, down_kept, down_theirs, True))
    first_ring.land()
    output_ring.send()
    upward_theirs = pin(upward_theirs)
    first_ring.prepare()
    gate_delta = pin(assembled(core_table, gate_kept, gate_theirs))
    output_ring.land()
    while output_ring.left():
        output_ring.prepare()
        output_ring.send()
        output_ring.land()
    first_ring.send()
    upward_delta = pin(assembled(core_table, upward_kept, upward_theirs))
    ((output_kept, output_given),) = pin(output_ring.total(core_table))
    output_theirs = core_swap(output_given)
    slopes = pin(jnp.sum(pin(slopes), axis=0))
    output_theirs = pin(output_theirs)
    first_ring.land()
    while first_ring.left():
        first_ring.prepare()
        first_ring.send()
        first_ring.land()
    ((first_kept, first_given),) = pin(first_ring.total(core_table))
    first_theirs = core_swap(first_given)
    output_delta = pin(assembled(core_table, output_kept, output_theirs, True))
    query_delta, key_delta, value_delta = parted(
        core_table, first_kept, pin(first_theirs), query_cols
    )
    small_delta = small_delta.astype(WIDE)
    return (
        result,
        line.mark,
        layer_delta,
        query_delta,
        key_delta,
        value_delta,
        output_delta,
        small_delta[:, 2 * side : 2 * side + rank],
        small_delta[:, 2 * side + rank :].T,
        gate_delta,
        upward_delta,
        down_delta,
        small_delta[:, :side],
        small_delta[:, side : 2 * side].T,
        slopes[0],
        slopes[6, :HD],
        slopes[6, HD : 2 * HD],
        slopes[1],
        slopes[2],
        slopes[3],
        slopes[4],
        slopes[5],
    )


def solution(mesh):
    tokens = P(("seq", "tp"), None)
    spread = P(None, ("seq", "tp"))
    inward = P("seq", "tp")
    outward = P("tp", "seq")
    weights = (
        inward,
        inward,
        inward,
        outward,
        tokens,
        spread,
        inward,
        inward,
        outward,
        tokens,
        spread,
    )
    return jax.shard_map(
        shards,
        mesh=mesh,
        in_specs=(tokens, tokens, tokens, P()) + weights + (P(),) * 8,
        out_specs=(tokens, tokens, tokens) + weights + (P(),) * 8,
        check_vma=False,
    )
```

```python
import jax
import jax.numpy as jnp
from jax import lax
from jax.experimental import pallas as pl
from jax.experimental.pallas import tpu as pltpu
from jax.sharding import PartitionSpec as P

QH = 8
KVH = 2
HD = 256
WIN = 512
PIC = 256


EPSILON = 1e-06
HALF_ROOT = 0.7071067811865476
ROPE_BASE = 10000.0
NEGATIVE = -1e30
GELU_SCALE = 0.7978845608028654
GELU_CUBE = 0.044715

LOW = jnp.bfloat16
WIDE = jnp.float32
VMEM_LIMIT = 56 * 2**20


def normed(value, gain):
    return value * lax.rsqrt(jnp.mean(value * value, axis=-1, keepdims=True) + EPSILON) * gain


def normed_back(value, gain, upstream):
    _, pullback = jax.vjp(normed, value, gain)
    return pullback(upstream)


def smooth_gate(value):
    return (
        0.5 * value * (1.0 + jnp.tanh(GELU_SCALE * (value + GELU_CUBE * value * value * value)))
    )


def gate_back(value, upstream):
    _, pullback = jax.vjp(smooth_gate, value)
    return pullback(upstream)[0]


def rotary(value, cosines, sines):
    half = value.shape[-1] // 2
    first = value[..., :half]
    second = value[..., half:]
    return jnp.concatenate(
        [first * cosines - second * sines, second * cosines + first * sines], axis=-1
    )


def product(left, right):
    return jnp.dot(left, right, preferred_element_type=WIDE)


def outer_sum(left, right):
    return lax.dot_general(left, right, (((0,), (0,)), ((), ())), preferred_element_type=WIDE)


def back_product(left, right):
    return lax.dot_general(left, right, (((1,), (1,)), ((), ())), preferred_element_type=WIDE)


def shape_of(shape, kind):
    return jax.ShapeDtypeStruct(shape, kind)


def kernel_call(body, name, grid, inputs, outputs, scratch=(), flops=0, prefetch=None):
    def spec(entry):
        array, block, where = entry
        if block is None:
            rank = len(array.shape)
            return pl.BlockSpec(array.shape, lambda *_, rank=rank: (0,) * rank)
        return pl.BlockSpec(block, where)

    moved = sum(a.size * a.dtype.itemsize for a, _, _ in list(inputs) + list(outputs))
    call = pl.pallas_call(
        body,
        grid_spec=pltpu.PrefetchScalarGridSpec(
            num_scalar_prefetch=0 if prefetch is None else 1,
            grid=grid,
            in_specs=[spec(e) for e in inputs],
            out_specs=[spec(e) for e in outputs],
            scratch_shapes=list(scratch),
        ),
        out_shape=[shape_of(a.shape, a.dtype) for a, _, _ in outputs],
        compiler_params=pltpu.CompilerParams(
            dimension_semantics=("arbitrary",) * len(grid), vmem_limit_bytes=VMEM_LIMIT
        ),
        cost_estimate=pl.CostEstimate(flops=0, bytes_accessed=0, transcendentals=0),
        name=name,
    )
    operands = [a for a, _, _ in inputs]
    return call(*operands) if prefetch is None else call(prefetch, *operands)


def permuted(arrays, kinds, table, inverse=False):
    count = table.shape[0]
    part = arrays[0].shape[1] // count
    if part % 128:
        if inverse:
            table = jnp.argsort(table)
        results = []
        for array, kind in zip(arrays, kinds):
            parts = [
                lax.dynamic_slice_in_dim(array, table[j] * part, part, 1) for j in range(count)
            ]
            results.append(jnp.concatenate(parts, axis=1).astype(kind))
        return results

    def body(table_ref, *refs):
        for source, target in zip(refs[: len(arrays)], refs[len(arrays) :]):
            for j in range(count):
                here = pl.ds(j * part, part)
                there = pl.ds(pl.multiple_of(table_ref[j] * part, part), part)
                before, behind = (here, there) if inverse else (there, here)
                target[:, behind] = source[:, before].astype(target.dtype)

    return kernel_call(
        body,
        "permuted",
        (1,),
        [(a, None, None) for a in arrays],
        [(shape_of(a.shape, k), None, None) for a, k in zip(arrays, kinds)],
        prefetch=table,
    )


def permuted_rows(array, table, widths, inverse=False):
    count = table.shape[0]
    part = array.shape[0] // count

    def body(table_ref, source, *targets):
        for j in range(count):
            here = pl.ds(j * part, part)
            there = pl.ds(pl.multiple_of(table_ref[j] * part, part), part)
            before, behind = (here, there) if inverse else (there, here)
            at = 0
            for target, wide in zip(targets, widths):
                target[behind, :] = source[before, at : at + wide]
                at += wide

    outs = [(shape_of((array.shape[0], w), array.dtype), None, None) for w in widths]
    return kernel_call(body, "permuted_rows", (1,), [(array, None, None)], outs, prefetch=table)


def halves_of(core, weights):
    inputs, widths = [], []
    for weight in weights:
        if isinstance(weight, tuple):
            inputs += [(w, None, None) for w in weight]
            widths.append(weight[0].shape[1])
        elif isinstance(weight, list):
            half = weight[0].shape[0] // 2
            block = (half, weight[0].shape[1])
            inputs.append((weight[0], block, lambda _, core_ref: (core(core_ref), 0)))
            widths.append(half)
        else:
            half = weight.shape[1] // 2
            block = (weight.shape[0], half)
            inputs.append((weight, block, lambda _, core_ref: (0, core(core_ref))))
            widths.append(half)
    return inputs, widths


def half_values(core, weights, refs):
    values = []
    at = 0
    for weight in weights:
        if isinstance(weight, tuple):
            first = (core == 0).astype(WIDE)
            low = refs[at][...].astype(WIDE) * first + refs[at + 1][...].astype(WIDE) * (1.0 - first)
            values.append(low.astype(LOW))
            at += 2
        else:
            value = refs[at][...]
            values.append(value.T if isinstance(weight, list) else value)
            at += 1
    return values


def weights_given(core, weights):
    inputs, widths = halves_of(lambda core_ref: 1 - core_ref[0], weights)

    def body(core_ref, *refs):
        at = 0
        for wide, value in zip(widths, half_values(1 - core_ref[0], weights, refs)):
            refs[-1][:, at : at + wide] = value
            at += wide

    rows = weights[0].shape[0]
    return kernel_call(
        body,
        "weights_given",
        (1,),
        inputs,
        [(shape_of((rows, sum(widths)), LOW), None, None)],
        prefetch=core,
    )[0]


def weights_merged(core, weights, theirs, groups):
    inputs, widths = halves_of(lambda core_ref: core_ref[0], weights)
    rows = weights[0].shape[0]

    def body(core_ref, *refs):
        other = refs[len(inputs)]
        outs = refs[len(inputs) + 1 :]
        values = half_values(core_ref[0], weights, refs)
        mine = pl.ds(pl.multiple_of(core_ref[0] * rows, rows), rows)
        given = pl.ds(pl.multiple_of((1 - core_ref[0]) * rows, rows), rows)
        at = 0
        for out, group in zip(outs, groups):
            column = 0
            for i in group:
                wide = widths[i]
                out[mine, column : column + wide] = values[i]
                out[given, column : column + wide] = other[:, at : at + wide]
                column += wide
                at += wide

    return kernel_call(
        body,
        "weights_merged",
        (1,),
        inputs + [(theirs, None, None)],
        [(shape_of((2 * rows, sum(widths[i] for i in group)), LOW), None, None) for group in groups],
        prefetch=core,
    )


def expanded(rows, gates, ups, hidden_units):
    tile = 512
    count = len(gates)
    part = gates[0][0].shape[0]

    def body(rows_ref, *refs):
        gate_refs, up_refs = refs[:count], refs[count : 2 * count]
        gate_out, up_out, inner_out = refs[2 * count :]
        x = rows_ref[...]
        gate = product(x, jnp.concatenate([r[...] for r in gate_refs], axis=0))
        up = product(x, jnp.concatenate([r[...] for r in up_refs], axis=0))
        gate_out[...] = gate.astype(LOW)
        up_out[...] = up.astype(LOW)
        inner_out[...] = (smooth_gate(gate) * up).astype(LOW)

    chunks = [
        (a, (part, tile), lambda j, first=first // tile: (0, first + j)) for a, first in gates + ups
    ]
    out = (shape_of((rows.shape[0], hidden_units), LOW), (rows.shape[0], tile), lambda j: (0, j))
    return kernel_call(
        body,
        "expanded",
        (hidden_units // tile,),
        [(rows, None, None)] + chunks,
        [out] * 3,
        flops=4 * rows.size * hidden_units,
    )


def contracted(inner, first_row, row_count, chunks, kind):
    units = inner.shape[1]
    flat = [a for chunk in chunks for a in chunk]
    part = flat[0].shape[0]
    block = min(row_count, 256)

    def body(inner_ref, *refs):
        out_ref = refs[-1]
        at = 0
        for i, chunk in enumerate(chunks):
            column = 0
            total = None
            for a in chunk:
                wide = a.shape[1]
                term = back_product(inner_ref[:, column : column + wide], refs[at][...])
                total = term if total is None else total + term
                column += wide
                at += 1
            out_ref[:, i * part : (i + 1) * part] = total.astype(out_ref.dtype)

    start = first_row // block
    return kernel_call(
        body,
        "contracted",
        (row_count // block,),
        [(inner, (block, units), lambda i: (start + i, 0))] + [(a, None, None) for a in flat],
        [
            (
                shape_of((row_count, part * len(chunks)), kind),
                (block, part * len(chunks)),
                lambda i: (i, 0),
            )
        ],
        flops=2 * row_count * units * part * len(chunks),
    )[0]


def inner_pulled(rows, chunks, gate, up):
    tile = 512
    count, units = gate.shape
    steps = units // tile
    flat, kinds = [], []
    for chunk in chunks:
        for i, a in enumerate(chunk):
            first = 0 if i == 0 else steps - a.shape[1] // tile
            last = a.shape[1] // tile - 1
            flat.append(
                (
                    a,
                    (a.shape[0], tile),
                    lambda j, first=first, last=last: (0, jnp.clip(j - first, 0, last)),
                )
            )

    def body(rows_ref, *refs):
        chunk_refs = refs[: len(flat)]
        gate_ref, up_ref, gate_out, up_out = refs[len(flat) :]
        step = pl.program_id(0)
        parts = []
        at = 0
        for chunk in chunks:
            value = chunk_refs[at][...]
            if len(chunk) == 2:
                value = jnp.where(
                    step < chunk[0].shape[1] // tile, value, chunk_refs[at + 1][...]
                )
            parts.append(value)
            at += len(chunk)
        pulled = product(rows_ref[...], jnp.concatenate(parts, axis=0))
        gate_out[...] = (pulled * gate_ref[...].astype(WIDE)).astype(LOW)
        up_out[...] = (pulled * up_ref[...].astype(WIDE)).astype(LOW)

    block = ((count, tile), lambda j: (0, j))
    return kernel_call(
        body,
        "inner_pulled",
        (steps,),
        [(rows, None, None)] + flat + [(gate,) + block, (up,) + block],
        [(gate,) + block] * 2,
        flops=2 * rows.size * units,
    )


def gate_slopes(gate, up):
    def body(gate, up):
        value = gate.astype(WIDE)
        square = value * value
        bent = jnp.tanh(GELU_SCALE * (value + GELU_CUBE * value * square))
        slope = 0.5 * (1.0 + bent) + 0.5 * value * (1.0 - bent * bent) * GELU_SCALE * (
            1.0 + 3.0 * GELU_CUBE * square
        )
        return up.astype(WIDE) * slope, 0.5 * value * (1.0 + bent)

    kinds = [(gate.shape[1], LOW)] * 2
    return rowwise(body, "gate_slopes", [gate, up], [], kinds, [])


def rows_pulled(gate_back_low, up_back_low, first_row, row_count, gates, ups, kind):
    tile = 1024
    units = gate_back_low.shape[1]
    count = len(gates)
    part = gates[0][0].shape[0]
    width = part * count
    steps = units // tile
    start = first_row // row_count

    def body(gate_ref, up_ref, *refs):
        out_ref, total_ref = refs[-2:]
        step = pl.program_id(0)
        term = back_product(
            gate_ref[...], jnp.concatenate([r[...] for r in refs[:count]], axis=0)
        ) + back_product(
            up_ref[...], jnp.concatenate([r[...] for r in refs[count : 2 * count]], axis=0)
        )

        @pl.when(step == 0)
        def _():
            total_ref[...] = term

        @pl.when((step > 0) & (step < steps - 1))
        def _():
            total_ref[...] += term

        @pl.when(step == steps - 1)
        def _():
            out_ref[...] = (total_ref[...] + term).astype(out_ref.dtype)

    chunks = [
        (a, (part, tile), lambda k, first=first // tile: (0, first + k)) for a, first in gates + ups
    ]
    left = ((row_count, tile), lambda k: (start, k))
    return kernel_call(
        body,
        "rows_pulled",
        (steps,),
        [(gate_back_low,) + left, (up_back_low,) + left] + chunks,
        [(shape_of((row_count, width), kind), None, None)],
        scratch=[pltpu.VMEM((row_count, width), WIDE)],
        flops=4 * row_count * units * width,
    )[0]


def one_term(offset, part, left, right, added, first=0, count=None):
    rows = left.shape[0]
    count = right.shape[1] if count is None else count
    tile = max(t for t in (256, 512, 1024) if count % t == 0 and first % t == 0)

    def body(left_ref, right_ref, *refs):
        turn = refs[-1]

        @pl.when(pl.program_id(0) == 0)
        def _():
            turn[...] = left_ref[...].T

        total = product(turn[...], right_ref[...])
        if added is not None:
            total = total + refs[0][...].astype(WIDE)
        refs[-2][...] = total.astype(LOW)

    inputs = [
        (left, (rows, part), lambda j: (0, offset)),
        (right, (rows, tile), lambda j: (0, first // tile + j)),
    ]
    if added is not None:
        inputs.append((added, (part, tile), lambda j: (offset, first // tile + j)))
    return kernel_call(
        body,
        "one_term",
        (count // tile,),
        inputs,
        [(shape_of((part, count), LOW), (part, tile), lambda j: (0, j))],
        scratch=[pltpu.VMEM((part, rows), LOW)],
    )[0]


def two_terms(offset, part, left, right, added):
    rows = left.shape[0]
    half = right.shape[1] // 2
    tile = min(half, 512)
    steps = half // tile

    def body(left_ref, first_ref, second_ref, *refs):
        turn = refs[-1]

        @pl.when(pl.program_id(0) == 0)
        def _():
            turn[...] = left_ref[...].T

        first = product(turn[...], first_ref[...])
        second = product(turn[...], second_ref[...])
        if added is not None:
            first = first + refs[0][...].astype(WIDE)
            second = second + refs[1][...].astype(WIDE)
        refs[-3][...] = first.astype(LOW)
        refs[-2][...] = second.astype(LOW)

    inputs = [
        (left, (rows, part), lambda j: (0, offset)),
        (right, (rows, tile), lambda j: (0, j)),
        (right, (rows, tile), lambda j: (0, steps + j)),
    ]
    if added is not None:
        inputs.append((added, (part, tile), lambda j: (offset, j)))
        inputs.append((added, (part, tile), lambda j: (offset, steps + j)))
    out = (shape_of((part, half), LOW), (part, tile), lambda j: (0, j))
    return kernel_call(
        body,
        "two_terms",
        (steps,),
        inputs,
        [out, out],
        scratch=[pltpu.VMEM((part, rows), LOW)],
    )


def last_term(core, part, left, right, added, front, back, first):
    rows = left.shape[0]
    count = right.shape[1]
    half = part // 2
    if part % 128:
        total = outer_sum(left[:, :part], right)
        if added is not None:
            total = total + added[:part].astype(WIDE)
        total = total + front[:, first : first + count].astype(WIDE)
        total = total + back[:, first : first + count].astype(WIDE)
        kept = lax.dynamic_slice_in_dim(total, core[0] * half, half, 0)
        given = lax.dynamic_slice_in_dim(total, (1 - core[0]) * half, half, 0)
        return kept, given.astype(LOW)
    tile = 256

    def body(core_ref, left_ref, right_ref, front_ref, back_ref, *refs):
        kept_ref, given_ref, turn, total_ref = refs[-4:]

        @pl.when(pl.program_id(0) == 0)
        def _():
            turn[...] = left_ref[...].T

        total = product(turn[...], right_ref[...])
        total = total + front_ref[...].astype(WIDE) + back_ref[...].astype(WIDE)
        if added is not None:
            total = total + refs[0][...].astype(WIDE)
        total_ref[...] = total
        kept_ref[...] = total_ref[pl.ds(pl.multiple_of(core_ref[0] * half, half), half), :]
        given = pl.ds(pl.multiple_of((1 - core_ref[0]) * half, half), half)
        given_ref[...] = total_ref[given, :].astype(LOW)

    for size in (512, 1024):
        if count % size == 0 and first % size == 0:
            tile = size
    inputs = [
        (left, (rows, part), lambda j, _: (0, 0)),
        (right, (rows, tile), lambda j, _: (0, j)),
        (front, (part, tile), lambda j, _: (0, first // tile + j)),
        (back, (part, tile), lambda j, _: (0, first // tile + j)),
    ]
    if added is not None:
        inputs.append((added, (part, tile), lambda j, _: (0, j)))
    block = ((half, tile), lambda j, _: (0, j))
    return kernel_call(
        body,
        "last_term",
        (count // tile,),
        inputs,
        [(shape_of((half, count), WIDE),) + block, (shape_of((half, count), LOW),) + block],
        scratch=[pltpu.VMEM((part, rows), LOW), pltpu.VMEM((part, tile), WIDE)],
        prefetch=core,
    )


def assembled(core, kept, theirs, turned_over=False):
    rows, half = kept.shape

    def body(core_ref, kept_ref, theirs_ref, out_ref):
        mine = (pl.program_id(0) == core_ref[0]).astype(WIDE)
        value = kept_ref[...] * mine + theirs_ref[...].astype(WIDE) * (1.0 - mine)
        out_ref[...] = value.T if turned_over else value

    if turned_over:
        out = (shape_of((2 * half, rows), WIDE), (half, rows), lambda j, _: (j, 0))
    else:
        out = (shape_of((rows, 2 * half), WIDE), (rows, half), lambda j, _: (0, j))
    return kernel_call(
        body, "assembled", (2,), [(kept, None, None), (theirs, None, None)], [out], prefetch=core
    )[0]


def parted(core, kept, theirs, cols):
    rows, wide = kept.shape
    rest = wide - cols

    def body(core_ref, kept_ref, theirs_ref, both_ref, first_ref, second_ref):
        first_core = (core_ref[0] == 0).astype(WIDE)
        mine, other = kept_ref[...], theirs_ref[...].astype(WIDE)
        low = mine * first_core + other * (1.0 - first_core)
        high = other * first_core + mine * (1.0 - first_core)
        both_ref[:, :cols] = low[:, :cols]
        both_ref[:, cols:] = high[:, :cols]
        first_ref[...] = low[:, cols:]
        second_ref[...] = high[:, cols:]

    return kernel_call(
        body,
        "parted",
        (1,),
        [(kept, None, None), (theirs, None, None)],
        [
            (shape_of((rows, 2 * cols), WIDE), None, None),
            (shape_of((rows, rest), WIDE), None, None),
            (shape_of((rows, rest), WIDE), None, None),
        ],
        prefetch=core,
    )


def rowwise(body, name, row_inputs, whole_inputs, row_outputs, sum_outputs, block=128):
    count = row_inputs[0].shape[0]
    block = min(block, count)
    taken = len(row_inputs) + len(whole_inputs)

    def run(*refs):
        results = body(*(r[...] for r in refs[:taken]))
        outs = refs[taken:]
        for ref, value in zip(outs, results[: len(row_outputs)]):
            ref[...] = value.astype(ref.dtype)
        for ref, value in zip(outs[len(row_outputs) :], results[len(row_outputs) :]):

            @pl.when(pl.program_id(0) == 0)
            def _(ref=ref, value=value):
                ref[...] = value

            @pl.when(pl.program_id(0) > 0)
            def _(ref=ref, value=value):
                ref[...] += value

    def strip(shape):
        return ((block,) + shape[1:], lambda i: (i, 0))

    return kernel_call(
        run,
        name,
        (count // block,),
        [(a,) + strip(a.shape) for a in row_inputs] + [(a, None, None) for a in whole_inputs],
        [(shape_of((count, w), k),) + strip((count, w)) for w, k in row_outputs]
        + [(shape_of((1, w), WIDE), None, None) for w in sum_outputs],
    )


def stacked(*pieces):
    rows = sum(p.shape[0] for p in pieces)

    def body(*refs):
        at = 0
        for ref, piece in zip(refs, pieces):
            refs[-1][at : at + piece.shape[0], :] = ref[...]
            at += piece.shape[0]

    out = (shape_of((rows, pieces[0].shape[1]), pieces[0].dtype), None, None)
    return kernel_call(body, "stacked", (1,), [(p, None, None) for p in pieces], [out])[0]


def joined_chunks(chunks, first, count):
    part = chunks[0][0].shape[0]

    def body(*refs):
        for i, ref in enumerate(refs[:-1]):
            start = chunks[i][1] + first
            refs[-1][i * part : (i + 1) * part, :] = ref[:, start : start + count]

    out = (shape_of((part * len(chunks), count), LOW), None, None)
    return kernel_call(
        body, "joined_chunks", (1,), [(a, None, None) for a, _ in chunks], [out]
    )[0]


def multiplied(left, right, kind=WIDE):
    rows = left.shape[0]
    block = min(rows, 256)

    def body(left_ref, right_ref, out_ref):
        out_ref[...] = product(left_ref[...], right_ref[...]).astype(out_ref.dtype)

    return kernel_call(
        body,
        "multiplied",
        (rows // block,),
        [(left, (block, left.shape[1]), lambda i: (i, 0)), (right, None, None)],
        [(shape_of((rows, right.shape[1]), kind), (block, right.shape[1]), lambda i: (i, 0))],
    )[0]


def turned_products(pairs, kind):
    width = sum(right.shape[1] for _, right in pairs)
    tall = pairs[0][0].shape[1]
    block = 512
    rows = pairs[0][0].shape[0]

    def body(*refs):
        at = 0
        for i in range(len(pairs)):
            wide = pairs[i][1].shape[1]
            term = outer_sum(refs[2 * i][...], refs[2 * i + 1][...])
            refs[-1][:, at : at + wide] = term.astype(kind)
            at += wide

    inputs = []
    for left, right in pairs:
        inputs.append((left, (left.shape[0], block), lambda i: (0, i)))
        inputs.append((right, None, None))
    out = (shape_of((tall, width), kind), (block, width), lambda i: (i, 0))
    return kernel_call(body, "turned_products", (tall // block,), inputs, [out])[0]


def ring_terms(segments, part, ahead, behind, front, back, cut):
    width = sum(right.shape[1] for _, right, _ in segments)

    def plain(offset, received, first):
        columns = slice(offset * part, (offset + 1) * part)
        parts = []
        for left, right, added in segments:
            term = outer_sum(left[:, columns], right)
            if added is not None:
                term = term + added[columns].astype(WIDE)
            parts.append(term)
        total = jnp.concatenate(parts, axis=1)
        if received is not None:
            edge = (first, width - first - received.shape[1])
            total = total + jnp.pad(received.astype(WIDE), ((0, 0), edge))
        return total.astype(LOW)

    edges = [right.shape[1] for _, right, _ in segments]
    if part % 128:
        if front is None:
            return plain(ahead, None, 0)[:, :cut], plain(behind, None, 0)[:, cut:]
        return plain(ahead, front, 0), plain(behind, back, width - back.shape[1])
    if front is None:
        pair = segments
        if len(segments) == 1:
            left, right, added = segments[0]
            if 2 * cut == width:
                return two_terms(ahead, part, left, right, added)
            pair = [(left, right, added, 0, cut), (left, right, added, cut, width - cut)]
        return [one_term(ahead, part, *entry) for entry in pair]

    edges += [front.shape[1], width - back.shape[1]]
    tile = max(t for t in (256, 512, 1024) if all(e % t == 0 for e in edges))
    steps = width // tile
    front_steps, back_first = front.shape[1] // tile, steps - back.shape[1] // tile
    inputs, scratch, spans = [], [], []
    at = 0
    for left, right, added in segments:
        rows = left.shape[0]
        size = right.shape[1] // tile

        def column(j, at=at, size=size):
            return jnp.clip(j - at, 0, size - 1)

        inputs.append((left, (rows, part), lambda j: (0, ahead)))
        inputs.append((left, (rows, part), lambda j: (0, behind)))
        inputs.append((right, (rows, tile), lambda j, column=column: (0, column(j))))
        if added is not None:
            inputs.append((added, (part, tile), lambda j, column=column: (ahead, column(j))))
            inputs.append((added, (part, tile), lambda j, column=column: (behind, column(j))))
        same = [i for i, (other, _, _) in enumerate(segments) if other is left][0]
        scratch.append(pltpu.VMEM((2, part, rows) if len(spans) == same else (8, 128), LOW))
        spans.append((at, at + size, added is not None, same))
        at += size
    inputs.append((front, (part, tile), lambda j: (0, jnp.clip(j, 0, front_steps - 1))))
    inputs.append((back, (part, tile), lambda j: (0, jnp.clip(j - back_first, 0, steps))))

    def body(*refs):
        refs = list(refs)
        turned = refs[len(inputs) + 2 :]
        front_ref, back_ref = refs[len(inputs) - 2 : len(inputs)]
        outs = refs[len(inputs) : len(inputs) + 2]
        step = pl.program_id(0)
        had_front = (step < front_steps).astype(WIDE)
        had_back = (step >= back_first).astype(WIDE)
        place = 0
        for at, (first, last, adds, same) in enumerate(spans):
            mine = refs[place : place + (5 if adds else 3)]
            place += len(mine)
            turn = turned[same]

            if same == at:

                @pl.when(step == 0)
                def _(mine=mine, turn=turn):
                    turn[0] = mine[0][...].T
                    turn[1] = mine[1][...].T

            @pl.when((step >= first) & (step < last))
            def _(mine=mine, turn=turn, adds=adds):
                right = mine[2][...]
                for way, received, had in ((0, front_ref, had_front), (1, back_ref, had_back)):
                    total = product(turn[way], right) + received[...].astype(WIDE) * had
                    if adds:
                        total = total + mine[3 + way][...].astype(WIDE)
                    outs[way][...] = total.astype(LOW)

    out = (shape_of((part, width), LOW), (part, tile), lambda j: (0, j))
    flops = sum(4 * part * right.size for _, right, _ in segments)
    return kernel_call(
        body, "ring_terms", (steps,), inputs, [out, out], scratch=scratch, flops=flops
    )


def turned(value, gain, cosines, sines):
    scale = lax.rsqrt(jnp.mean(value * value, axis=-1, keepdims=True) + EPSILON)
    return rotary(value * scale * gain, cosines, sines).astype(LOW), scale


def hidden_scores(places):
    query_place, query_start, key_place, key_start, total_rows = places
    distance = query_place - key_place
    near = (distance >= 0) & (distance < WIN)
    visible = (key_place >= 0) & (key_place < total_rows) & (near | (query_start == key_start))
    return jnp.where(visible, 0.0, NEGATIVE)


def head_specs(own, other, heads_own):
    rows = own.shape[0]
    return [
        (own, (rows, HD), lambda h: (0, jnp.minimum(h, heads_own - 1))),
        (other, (rows, HD), lambda h: (0, jnp.maximum(h - heads_own, 0))),
    ]


def attention(own, other, heads, gain, cosines, sines, keys, values, places, total_rows):
    rows = own.shape[0]
    heads_own = heads // 2
    scale = HD ** (-0.5)

    def body(own_ref, other_ref, gain_ref, cos_ref, sin_ref, pair_ref, qp, qs, kp, ks, out_own, out_other, log_ref, hide_ref):
        head = pl.program_id(0)

        @pl.when(head == 0)
        def _():
            hide_ref[...] = hidden_scores((qp[...], qs[...], kp[...], ks[...], total_rows))

        raw = jnp.where(head < heads_own, own_ref[...], other_ref[...])
        query, _ = turned(raw, gain_ref[...], cos_ref[...], sin_ref[...])
        scores = back_product(pair_ref[:, :HD], query) * scale + hide_ref[...]
        peak = jnp.max(scores, axis=0, keepdims=True)
        log_total = peak + jnp.log(jnp.sum(jnp.exp(scores - peak), axis=0, keepdims=True))
        weights = jnp.exp(scores - log_total).astype(LOW)
        result = outer_sum(weights, pair_ref[:, HD:]).astype(LOW)
        log_ref[0] = log_total

        @pl.when(head < heads_own)
        def _():
            out_own[...] = result

        @pl.when(head >= heads_own)
        def _():
            out_other[...] = result

    whole = [(a, None, None) for a in (gain, cosines, sines, keys) + tuple(places)]
    half = shape_of((rows, heads_own * HD), LOW)
    return kernel_call(
        body,
        "attention",
        (heads,),
        head_specs(own, other, heads_own) + whole,
        head_specs(half, half, heads_own)
        + [(shape_of((heads, 1, rows), WIDE), (1, 1, rows), lambda h: (h, 0, 0))],
        scratch=[pltpu.VMEM((keys.shape[0], rows), WIDE)],
    )


def attention_back(own, other, heads, gain, cosines, sines, keys, places, total_rows, log_total, upstream, weights_own, weights_other):
    rows = own.shape[0]
    heads_own = heads // 2
    scale = HD ** (-0.5)
    tail = keys.shape[0] - 2 * rows

    def body(own_ref, other_ref, weight_own, weight_other, gain_ref, cos_ref, sin_ref, pair_ref, up_ref, qp, qs, kp, ks, log_ref, query_own, query_other, before_out, here_out, after_out, slope_out, hide_ref, total_ref):
        head = pl.program_id(0)

        @pl.when(head == 0)
        def _():
            hide_ref[...] = hidden_scores((qp[...], qs[...], kp[...], ks[...], total_rows))
            total_ref[...] = jnp.zeros_like(total_ref)
            slope_out[...] = jnp.zeros_like(slope_out)

        raw = jnp.where(head < heads_own, own_ref[...], other_ref[...])
        weight = jnp.where(head < heads_own, weight_own[...], weight_other[...])
        up = product(up_ref[...], weight).astype(LOW)
        gain_row, cos, sin = gain_ref[...], cos_ref[...], sin_ref[...]
        query, shrink = turned(raw, gain_row, cos, sin)
        key = pair_ref[:, :HD]
        scores = back_product(key, query) * scale + hide_ref[...]
        weights = jnp.exp(scores - log_ref[0])
        pulled = back_product(pair_ref[:, HD:], up)
        centre = jnp.sum(weights * pulled, axis=0, keepdims=True)
        scores_back = (weights * (pulled - centre)).astype(LOW)
        total_ref[:, :HD] += product(scores_back, query) * scale
        total_ref[:, HD:] += product(weights.astype(LOW), up)
        turned_back = outer_sum(scores_back, key) * scale
        normed_up = rotary(turned_back, cos, -sin)
        shape = raw * shrink
        slope_out[...] += jnp.sum(normed_up * shape, axis=0, keepdims=True)
        inner = normed_up * gain_row
        raw_back = shrink * (inner - shape * jnp.mean(inner * shape, axis=-1, keepdims=True))

        @pl.when(head < heads_own)
        def _():
            query_own[...] = raw_back.astype(LOW)

        @pl.when(head >= heads_own)
        def _():
            query_other[...] = raw_back.astype(LOW)

        @pl.when(head == heads - 1)
        def _():
            before_out[...] = total_ref[:rows].astype(LOW)
            here_out[...] = total_ref[rows : 2 * rows]
            after_out[...] = total_ref[2 * rows :].astype(LOW)

    whole = [(a, None, None) for a in (gain, cosines, sines, keys, upstream) + tuple(places)]
    half = shape_of((rows, heads_own * HD), LOW)
    deep = weights_own.shape[0]
    weight_specs = [
        (weights_own, (deep, HD), lambda h: (0, jnp.minimum(h, heads_own - 1))),
        (weights_other, (deep, HD), lambda h: (0, jnp.maximum(h - heads_own, 0))),
    ]
    return kernel_call(
        body,
        "attention_back",
        (heads,),
        head_specs(own, other, heads_own)
        + weight_specs
        + whole
        + [(log_total, (1, 1, rows), lambda h: (h, 0, 0))],
        head_specs(half, half, heads_own)
        + [
            (shape_of((rows, 2 * HD), LOW), None, None),
            (shape_of((rows, 2 * HD), WIDE), None, None),
            (shape_of((tail, 2 * HD), LOW), None, None),
            (shape_of((1, HD), WIDE), None, None),
        ],
        scratch=[pltpu.VMEM((keys.shape[0], rows), WIDE), pltpu.VMEM((keys.shape[0], 2 * HD), WIDE)],
    )


def keyed(own, other, cols, cosines, sines, gain, flag):
    def body(mine, theirs, cos, sin, gain_row, flag_row):
        first, second = mine[:, cols:], theirs[:, cols:]
        key = jnp.where(flag_row > 0, first, second)
        value = jnp.where(flag_row > 0, second, first)
        return (jnp.concatenate([rotary(normed(key, gain_row), cos, sin), value], axis=1),)

    return rowwise(
        body, "keyed", [own, other, cosines, sines], [gain, flag], [(2 * HD, LOW)], [], 256
    )[0]


def keyed_back(tp_table, here, later, earlier, query_own, query_other, own, other, cols, cosines, sines, gain, flag):
    rows = here.shape[0]
    block = earlier.shape[0]

    def body(tp_ref, here_ref, later_ref, earlier_ref, query_mine, query_theirs, mine, theirs, cos, sin, gain_row, flag_row, own_out, other_out, slope_out):
        got = (pl.program_id(0) == tp_ref[0]).astype(WIDE)
        total = here_ref[...] + later_ref[...].astype(WIDE) + earlier_ref[...].astype(WIDE) * got
        flagged = flag_row[...] > 0
        key = jnp.where(flagged, mine[...], theirs[...])
        key_back, slope = normed_back(
            key, gain_row[...], rotary(total[:, :HD], cos[...], -sin[...])
        )
        value_back = total[:, HD:]
        wide = query_mine.shape[1]
        own_out[:, :wide] = query_mine[...]
        other_out[:, :wide] = query_theirs[...]
        own_out[:, wide:] = jnp.where(flagged, key_back, value_back).astype(LOW)
        other_out[:, wide:] = jnp.where(flagged, value_back, key_back).astype(LOW)

        @pl.when(pl.program_id(0) == 0)
        def _():
            slope_out[...] = slope

        @pl.when(pl.program_id(0) > 0)
        def _():
            slope_out[...] += slope

    def strip(array):
        return (array, (block, array.shape[1]), lambda i, _: (i, 0))

    raw = [(a, (block, HD), lambda i, _: (i, cols // HD)) for a in (own, other)]
    out = strip(shape_of((rows, cols + HD), LOW))
    return kernel_call(
        body,
        "keyed_back",
        (rows // block,),
        [strip(here), strip(later), (earlier, None, None), strip(query_own), strip(query_other)]
        + raw
        + [strip(cosines), strip(sines), (gain, None, None), (flag, None, None)],
        [out, out, (shape_of((1, HD), WIDE), None, None)],
        prefetch=tp_table,
    )


def merged_rows(residual, mine, theirs, low, left, right, gains):
    def body(residual, mine, theirs, low, left, right, gains):
        gain_in, gain_mixer, gain_laurel, gain_next = (gains[i : i + 1] for i in range(4))
        mixer = mine + theirs.astype(WIDE)
        middle = product(low, left).astype(LOW)
        laurel = back_product(middle, right)
        total = (
            residual
            + normed(mixer, gain_mixer)
            + normed(residual, gain_in)
            + normed(laurel, gain_laurel)
        ) * HALF_ROOT
        return mixer, laurel, middle, total, normed(total, gain_next)

    width = residual.shape[1]
    kinds = [(width, WIDE), (width, WIDE), (left.shape[1], LOW), (width, WIDE), (width, LOW)]
    return rowwise(
        body, "merged_rows", [residual, mine, theirs, low], [left, right, gains], kinds, []
    )


def branched(merged, upstream, extra, dense, orders, branch, project, gains):
    def body(merged, upstream, extra, *rest):
        sums = rest[: 3 * len(orders)]
        branch, project, gains = rest[3 * len(orders) :]
        gain_dense, gain_branch = gains[4:5], gains[5:6]
        parts = {}
        for i, group in enumerate(orders):
            near, far, peer = sums[3 * i : 3 * i + 3]
            total = near + far.astype(WIDE) + peer.astype(WIDE)
            part = total.shape[1] // len(group)
            for k, offset in enumerate(group):
                parts[offset] = total[:, k * part : (k + 1) * part]
        dense = jnp.concatenate([parts[o] for o in sorted(parts)], axis=1)
        middle = merged + normed(dense, gain_dense)
        middle_low = middle.astype(LOW)
        raw = product(middle_low, branch)
        extra = extra.astype(WIDE)
        active = smooth_gate(raw)
        low = (active * extra).astype(LOW)
        projected = back_product(low, project)
        result = middle + normed(projected, gain_branch)
        project_back, branch_slope = normed_back(projected, gain_branch, upstream)
        project_low = project_back.astype(LOW)
        pulled = product(project_low, project)
        raw_back = gate_back(raw, pulled * extra).astype(LOW)
        middle_back = upstream + back_product(raw_back, branch)
        dense_back, dense_slope = normed_back(dense, gain_dense, middle_back)
        return (
            result, pulled * active, project_low, low, raw_back, middle_low, middle_back,
            dense_back, branch_slope, dense_slope,
        )

    width, side = merged.shape[1], extra.shape[1]
    kinds = [
        (width, LOW), (side, WIDE), (width, LOW), (side, LOW), (side, LOW), (width, LOW),
        (width, WIDE), (width, LOW),
    ]
    return rowwise(
        body,
        "branched",
        [merged, upstream, extra] + [a for group in dense for a in group],
        [branch, project, gains],
        kinds,
        [width, width],
    )


def merged_back(near, far, peer, merged, middle_back, mixer, laurel, right, gains):
    def body(merged, near, far, peer, middle_back, mixer, laurel, right, gains):
        gain_next, gain_mixer, gain_laurel = gains[3:4], gains[1:2], gains[2:3]
        pulled = near + far.astype(WIDE) + peer.astype(WIDE)
        extra, next_slope = normed_back(merged, gain_next, pulled)
        total = (middle_back + extra) * HALF_ROOT
        mixer_back, mixer_slope = normed_back(mixer, gain_mixer, total)
        laurel_back, laurel_slope = normed_back(laurel, gain_laurel, total)
        laurel_low = laurel_back.astype(LOW)
        middle = product(laurel_low, right)
        return total, mixer_back, laurel_low, middle, next_slope, mixer_slope, laurel_slope

    width = merged.shape[1]
    kinds = [(width, WIDE), (width, LOW), (width, LOW), (right.shape[1], LOW)]
    return rowwise(
        body,
        "merged_back",
        [merged, near, far, peer, middle_back, mixer, laurel],
        [right, gains],
        kinds,
        [width] * 3,
    )


def opened_back(mine, theirs, middle, total, residual, left, gain):
    def body(mine, theirs, middle, total, residual, left, gains):
        gain = gains[0:1]
        pulled = mine + theirs.astype(WIDE) + back_product(middle, left) + total
        back, slope = normed_back(residual, gain, pulled)
        return total + back, slope

    width = residual.shape[1]
    return rowwise(
        body,
        "opened_back",
        [mine, theirs, middle, total, residual],
        [left, gain],
        [(width, WIDE)],
        [width],
    )


def doubled(own, other, first_row, row_count, weights_own, weights_other, kind):
    def body(own_ref, other_ref, weight_own, weight_other, out_ref):
        total = back_product(own_ref[...], weight_own[...])
        total = total + back_product(other_ref[...], weight_other[...])
        out_ref[...] = total.astype(kind)

    start = first_row // row_count
    tall = weights_own.shape[0]
    block = 512
    return kernel_call(
        body,
        "doubled",
        (tall // block,),
        [
            (own, (row_count, own.shape[1]), lambda i: (start, 0)),
            (other, (row_count, other.shape[1]), lambda i: (start, 0)),
            (weights_own, (block, own.shape[1]), lambda i: (i, 0)),
            (weights_other, (block, other.shape[1]), lambda i: (i, 0)),
        ],
        [(shape_of((row_count, tall), kind), (row_count, block), lambda i: (0, i))],
    )[0]


def added_low(near, far, first_row):
    rows = near.shape[0] - first_row

    def body(near_ref, far_ref, out_ref):
        out_ref[...] = (near_ref[...] + far_ref[...].astype(WIDE)).astype(LOW)

    block = ((rows, near.shape[1]), lambda i: (first_row // rows, 0))
    return kernel_call(
        body,
        "added_low",
        (1,),
        [(near,) + block, (far,) + block],
        [(shape_of((rows, near.shape[1]), LOW), None, None)],
    )[0]


def shifted(block, distance):
    devices = range(lax.axis_size("seq"))
    route = [(i - distance, i) for i in devices if i - distance in devices]
    return lax.ppermute(block, "seq", route)


def tp_swap(block):
    return lax.ppermute(block, "tp", [(0, 1), (1, 0)])


def core_swap(block):
    return lax.ppermute(block, "seq", [(i, i ^ 1) for i in range(lax.axis_size("seq"))])


class Line:
    def __init__(self, mark):
        self.mark = mark

    def pin(self, values):
        values, self.mark = lax.optimization_barrier((values, self.mark))
        return values


class Ring:
    def __init__(self):
        self.chips = lax.axis_size("seq") // 2
        rows = self.chips // 2
        self.order = [2 * i for i in range(rows)] + [2 * i + 1 for i in reversed(range(rows))]
        place = [0] * self.chips
        for position, member in enumerate(self.order):
            place[member] = position
        mine = jnp.asarray(place, jnp.int32)[lax.axis_index("seq") // 2]
        offsets = (mine + jnp.arange(self.chips, dtype=jnp.int32)) % self.chips
        self.owners = jnp.asarray(self.order, jnp.int32)[offsets]

    def moved(self, block, step):
        n = self.chips
        route = [
            (self.order[p] * 2 + core, self.order[(p + step) % n] * 2 + core)
            for p in range(n)
            for core in range(2)
        ]
        return lax.ppermute(block, "seq", route)


class Gather:
    def __init__(self, ring, line, chunk, cut):
        self.ring = ring
        self.line = line
        self.cut = cut
        self.found = [None] * ring.chips
        self.found[0] = chunk
        self.count = 0

    def send(self):
        n = self.ring.chips
        self.count += 1
        k = self.count
        behind, ahead = (n - k + 1) % n, k - 1
        held = self.line.pin({o: self.found[o] for o in {behind, ahead}})
        self.found[behind], self.found[ahead] = held[behind], held[ahead]
        if k < n // 2:
            self.found[n - k] = self.ring.moved(held[behind], 1)
            self.found[k] = self.ring.moved(held[ahead], -1)
        else:
            self.found[k] = (
                self.ring.moved(held[behind][:, : self.cut], 1),
                self.ring.moved(held[ahead][:, self.cut :], -1),
            )

    def land(self):
        n = self.ring.chips
        new = {n - self.count, self.count}
        landed = self.line.pin({o: self.found[o] for o in new})
        for o in new:
            self.found[o] = landed[o]

    def finish(self):
        while self.count < self.ring.chips // 2:
            self.send()
            self.land()

    def columns(self, first, count):
        listed = []
        for chunk in self.found:
            if isinstance(chunk, tuple):
                half = first >= self.cut
                listed.append((chunk[half], first - self.cut * half))
            else:
                listed.append((chunk, first))
        return listed

    def joined(self, first, count):
        return jnp.concatenate(
            [a[:, start : start + count] for a, start in self.columns(first, count)], axis=0
        )


class Scatter:
    def __init__(self, ring, line, segments, part, cut):
        self.ring = ring
        self.line = line
        self.segments = segments
        self.part = part
        self.cut = cut
        self.count = 0
        self.front = self.back = None

    def prepare(self):
        n = self.ring.chips
        pair = ring_terms(
            self.segments,
            self.part,
            n // 2 - self.count,
            n // 2 + self.count,
            self.front,
            self.back,
            self.cut,
        )
        self.front, self.back = self.line.pin(tuple(pair))
        self.count += 1

    def send(self):
        front, back = self.line.pin((self.front, self.back))
        self.front, self.back = self.ring.moved(front, 1), self.ring.moved(back, -1)

    def land(self):
        self.front, self.back = self.line.pin((self.front, self.back))

    def left(self):
        return self.ring.chips // 2 - self.count

    def total(self, core):
        front, back = self.line.pin((self.front, self.back))
        results = []
        at = 0
        for left, right, added in self.segments:
            results.append(
                last_term(core, self.part, left, right, added, front, back, at)
            )
            at += right.shape[1]
        return results


def shards(
    hidden,
    layer_input,
    cotangent,
    span_starts,
    query_weight,
    key_weight,
    value_weight,
    output_weight,
    laurel_left,
    laurel_right,
    gate_weight,
    upward_weight,
    down_weight,
    branch_gate,
    branch_output,
    input_gain,
    query_gain,
    key_gain,
    mixer_gain,
    laurel_gain,
    prefeed_gain,
    postfeed_gain,
    branch_gain,
):
    tp_size = lax.axis_size("tp")
    seq_place = lax.axis_index("seq")
    tp_place = lax.axis_index("tp")
    core = seq_place % 2
    first_core = core == 0
    first_tp = tp_place == 0
    ring = Ring()
    line = Line(input_gain)
    pin = line.pin
    chips = ring.chips
    half_chips = chips // 2
    local_rows, width = hidden.shape
    block_rows = local_rows * tp_size
    total_rows = span_starts.shape[0]
    query_heads = QH // tp_size
    part = width // chips
    everywhere = ("seq", "tp")

    core_table = core[None].astype(jnp.int32)
    tp_table = tp_place[None].astype(jnp.int32)
    query_cols, output_width = query_weight.shape[1] // 2, output_weight.shape[0] // 2
    first_cols = query_cols + key_weight.shape[1]
    first_weights = (query_weight, (key_weight, value_weight), [output_weight])
    first_given = pin(weights_given(core_table, first_weights))
    first_theirs = core_swap(first_given)
    dense_weights = (gate_weight, upward_weight, [down_weight])
    units = gate_weight.shape[1] // 2
    side, rank = branch_gate.shape[1], laurel_left.shape[1]
    gains = jnp.stack(
        [line.mark, mixer_gain, laurel_gain, prefeed_gain, postfeed_gain, branch_gain] * 2
    )[:8]
    small = jnp.concatenate([branch_gate, branch_output.T, laurel_left, laurel_right.T], axis=1)
    gains, small = pin((gains, small))
    (first_pack,) = pin(
        weights_merged(core_table, first_weights, pin(first_theirs), ((0, 1, 2),))
    )
    first = Gather(ring, line, first_pack, first_cols)
    swapped_chunks = [None] * chips

    def swap_chunks(*offsets):
        for o in offsets:
            chunk = first.found[o]
            swapped_chunks[o] = (
                tuple(core_swap(a) for a in chunk) if isinstance(chunk, tuple) else core_swap(chunk)
            )

    def land_chunks(*offsets):
        for o in offsets:
            swapped_chunks[o] = pin(swapped_chunks[o])

    first.send()
    dense_weights = pin(dense_weights)
    dense_given = pin(weights_given(core_table, dense_weights))
    residual, upstream, gains = pin(
        permuted([hidden, cotangent, gains], [WIDE, WIDE, WIDE], ring.owners)
    )
    line.mark = gains
    (normed_low,) = rowwise(
        lambda value, gains: (normed(value, gains[0:1]),),
        "opened",
        [residual],
        [gains],
        [(width, LOW)],
        [],
    )
    normed_low = pin(normed_low)
    first.land()

    first.send()
    dense_theirs = core_swap(dense_given)
    rows_theirs = tp_swap(normed_low)
    swap_chunks(0, chips - 1, 1)
    expand_pack, down_pack = pin(
        weights_merged(core_table, dense_weights, pin(dense_theirs), ((0, 1), (2,)))
    )
    land_chunks(0, chips - 1, 1)
    first.land()
    while first.count < half_chips - 1:
        first.send()
        swap_chunks(chips - first.count + 1, first.count - 1)
        land_chunks(chips - first.count + 1, first.count - 1)
        first.land()
    expand = Gather(ring, line, expand_pack, units)
    down = Gather(ring, line, down_pack, units // 2)
    first.send()
    swap_chunks(half_chips + 1, half_chips - 1)
    start_row = seq_place * block_rows
    padded_starts = jnp.concatenate(
        [jnp.full((block_rows,), -1, jnp.int32), span_starts, jnp.full((PIC,), -1, jnp.int32)]
    )
    span = 2 * block_rows + PIC
    ahead_of = jnp.arange(span, dtype=jnp.int32)
    swapped = jnp.where(
        ahead_of < 2 * block_rows, ahead_of ^ (tp_place * local_rows), ahead_of
    )
    key_place = start_row - block_rows + swapped
    starts = lax.dynamic_slice_in_dim(padded_starts, start_row, span)
    blocks = [starts[i * local_rows : (i + 1) * local_rows] for i in range(4)]
    key_start = jnp.where(
        first_tp,
        starts,
        jnp.concatenate([blocks[1], blocks[0], blocks[3], blocks[2], starts[2 * block_rows :]]),
    )
    row_place = key_place[block_rows : 2 * block_rows]
    row_start = key_start[block_rows : 2 * block_rows]
    places = (row_place[None, :], row_start[None, :], key_place[:, None], key_start[:, None])
    frequency = ROPE_BASE ** (-(jnp.arange(HD // 2, dtype=WIDE) * 2.0) / HD)
    theta = row_place.astype(WIDE)[:, None] * frequency[None, :]
    flag = jnp.broadcast_to(jnp.where(first_core, 1.0, 0.0), (1, HD))
    cosines, sines, places, flag = pin((jnp.cos(theta), jnp.sin(theta), places, flag))
    query_gain_row, key_gain_row = query_gain[None, :], key_gain[None, :]
    land_chunks(half_chips + 1, half_chips - 1)
    rows_theirs = pin(rows_theirs)
    first.land()

    expand.send()
    small_full = lax.all_gather(pin(small), everywhere, axis=0, tiled=True)
    swap_chunks(half_chips)
    land_chunks(half_chips)
    rows_low = pin(stacked(normed_low, rows_theirs))

    def columns(found, start, count):
        listed = []
        for chunk in found:
            if isinstance(chunk, tuple):
                half = start >= first_cols
                listed.append((chunk[half], start - first_cols * half))
            else:
                listed.append((chunk, start))
        return joined_chunks(listed, 0, count)

    first_own = pin(columns(first.found, 0, first_cols))
    first_other = pin(columns(swapped_chunks, 0, first_cols))
    raw_own = pin(multiplied(rows_low, first_own))
    raw_other = pin(multiplied(rows_low, first_other))
    pair_low = pin(
        keyed(raw_own, raw_other, query_cols, cosines, sines, key_gain_row, flag)
    )
    early = pin(lax.dynamic_slice_in_dim(pair_low, tp_place * local_rows, PIC, 0))
    pairs_before, pairs_after = shifted(pair_low, 1), shifted(early, -1)
    output_own_full = pin(columns(first.found, first_cols, output_width))
    output_other_full = pin(columns(swapped_chunks, first_cols, output_width))
    pairs_before, pairs_after = pin((pairs_before, pairs_after))
    expand.land()
    expand.send()
    pairs_all = pin(stacked(pairs_before, pair_low, pairs_after))
    attended_own, attended_other, log_total = pin(
        attention(
            raw_own, raw_other, query_heads, query_gain_row, cosines, sines, pairs_all, pairs_all,
            places, total_rows,
        )
    )

    def output_product(first_row, kind):
        return pin(
            doubled(
                attended_own, attended_other, first_row, local_rows, output_own_full,
                output_other_full, kind,
            )
        )

    mixer_theirs = tp_swap(output_product(local_rows, LOW))
    mixer_mine = output_product(0, WIDE)
    mixer_theirs, small_full = pin((mixer_theirs, small_full))
    expand.land()
    expand.send()
    branch_full, project_full, left_full, right_full = pin(
        permuted_rows(small_full, ring.owners, (side, side, rank, rank))
    )
    mixer_raw, laurel_raw, laurel_mid, merged, dense_low = pin(
        merged_rows(
            residual, mixer_mine, mixer_theirs, normed_low, left_full, right_full, gains
        )
    )

    theirs, far = tp_swap(dense_low), core_swap(dense_low)
    theirs, far = pin((theirs, far))
    expand.land()
    while expand.count < half_chips - 1:
        expand.send()
        expand.land()
    expand.send()
    last = pin(core_swap(theirs))
    dense_rows = pin(stacked(dense_low, theirs, far, last))
    expand.land()
    down.send()
    gate_columns, upward_columns = pin(
        (
            [a for a, _ in expand.columns(0, units)],
            [a for a, _ in expand.columns(units, units)],
        )
    )
    gates = list(zip(gate_columns, (f for _, f in expand.columns(0, units))))
    upwards = list(zip(upward_columns, (f for _, f in expand.columns(units, units))))
    gate_raw, upward_raw, inner_low = pin(expanded(dense_rows, gates, upwards, units))
    down.land()
    orders, dense_sums = [], []

    def down_chunk(offset):
        chunk = down.found[offset]
        return chunk if isinstance(chunk, tuple) else (chunk,)

    def dense_send(offsets):
        chunks = pin([down_chunk(o) for o in offsets])
        far = pin(contracted(inner_low, block_rows, block_rows, chunks, LOW))
        far = core_swap(far)
        near = pin(contracted(inner_low, 0, block_rows, chunks, WIDE))
        far = pin(far)
        peer = pin(added_low(near, far, local_rows))
        orders.append(offsets)
        dense_sums.append((near, far, tp_swap(peer)))

    for near in range(1, half_chips + 1):
        if down.count < half_chips:
            down.send()
        if near == 1:
            dense_send([chips - 1, 0, 1])
        else:
            dense_send([chips - near, near] if near < half_chips else [near])
        if near < half_chips:
            down.land()
        if near > 1:
            dense_sums[near - 2] = pin(dense_sums[near - 2])
    dense_sums[-1] = pin(dense_sums[-1])
    (
        result, layer_delta, project_low, branch_low, branch_raw_back, middle_low, middle_back,
        dense_low_back, branch_slope, postfeed_slope,
    ) = pin(
        branched(
            merged, upstream, layer_input, dense_sums, orders, branch_full, project_full,
            gains,
        )
    )

    theirs, far = tp_swap(dense_low_back), core_swap(dense_low_back)
    gate_raw, upward_raw = pin(gate_slopes(*pin((gate_raw, upward_raw))))
    theirs, far = pin((theirs, far))
    last = pin(core_swap(theirs))
    dense_rows_back = pin(stacked(dense_low_back, theirs, far, last))
    down_ring = Scatter(ring, line, [(dense_rows_back, inner_low, None)], part, units // 2)
    down_ring.prepare()
    down_ring.send()
    gate_raw_back, upward_raw_back = pin(
        inner_pulled(
            pin(dense_rows_back), [down_chunk(o) for o in range(chips)], gate_raw, upward_raw
        )
    )
    gate_ring = Scatter(ring, line, [(dense_rows, gate_raw_back, None)], part, units // 2)
    upward_ring = Scatter(ring, line, [(dense_rows, upward_raw_back, None)], part, units // 2)
    gate_ring.prepare()
    down_ring.land()
    gate_ring.send()
    upward_ring.prepare()
    gate_ring.land()
    upward_ring.send()
    down_ring.prepare()
    upward_ring.land()

    def dense_back(first_row, row_count, kind):
        left, right = pin((gate_raw_back, upward_raw_back))
        return pin(rows_pulled(left, right, first_row, row_count, gates, upwards, kind))

    down_ring.send()
    far_given = dense_back(block_rows, block_rows, LOW)
    gate_ring.prepare()
    down_ring.land()
    gate_ring.send()
    far_back = core_swap(far_given)
    near_back = dense_back(0, block_rows, WIDE)
    upward_ring.prepare()
    far_back = pin(far_back)
    gate_ring.land()
    upward_ring.send()
    peer_given = pin(added_low(near_back, far_back, local_rows))
    down_ring.prepare()
    upward_ring.land()
    down_ring.send()
    peer_back = tp_swap(peer_given)
    (result,) = pin(permuted([result], [LOW], ring.owners, inverse=True))
    gate_ring.prepare()
    peer_back = pin(peer_back)
    down_ring.land()
    gate_ring.send()
    (
        summed_back, mixer_low_back, laurel_raw_low, laurel_mid_back, prefeed_slope, mixer_slope,
        laurel_slope,
    ) = pin(
        merged_back(
            near_back, far_back, peer_back, merged, middle_back, mixer_raw, laurel_raw,
            right_full, gains,
        )
    )
    upward_ring.prepare()
    gate_ring.land()
    upward_ring.send()
    mixer_theirs_back = tp_swap(mixer_low_back)
    small_delta = turned_products(
        [
            (middle_low, branch_raw_back),
            (project_low, branch_low),
            (normed_low, laurel_mid_back),
            (laurel_raw_low, laurel_mid),
        ],
        LOW,
    )
    (small_delta,) = pin(
        permuted_rows(pin(small_delta), ring.owners, (2 * side + 2 * rank,), inverse=True)
    )
    down_ring.prepare()
    mixer_theirs_back = pin(mixer_theirs_back)
    upward_ring.land()
    down_ring.send()
    small_delta = lax.psum_scatter(small_delta, everywhere, scatter_dimension=0, tiled=True)
    mixer_rows_back = pin(stacked(mixer_low_back, mixer_theirs_back))
    query_own_back, query_other_back, pairs_sent, pairs_here, pairs_late, query_slope = pin(
        attention_back(
            raw_own, raw_other, query_heads, query_gain_row, cosines, sines, pairs_all, places,
            total_rows, log_total, mixer_rows_back, output_own_full, output_other_full,
        )
    )
    gate_ring.prepare()
    down_ring.land()
    gate_ring.send()
    later, earlier = shifted(pairs_sent, -1), shifted(pairs_late, 1)
    output_given = pin(turned_products([(mixer_rows_back, attended_other)], LOW))
    upward_ring.prepare()
    later, earlier = pin((later, earlier))
    gate_ring.land()
    upward_ring.send()
    output_theirs = core_swap(output_given)
    first_own_back, first_other_back, key_slope = pin(
        keyed_back(
            tp_table, pairs_here, later, earlier, query_own_back, query_other_back, raw_own,
            raw_other, query_cols, cosines, sines, key_gain_row, flag,
        )
    )
    first_given_back = pin(turned_products([(rows_low, first_other_back)], LOW))
    first_theirs_back = core_swap(first_given_back)

    def rows_back(first_row, kind):
        return pin(
            doubled(
                first_own_back, first_other_back, first_row, local_rows, first_own, first_other,
                kind,
            )
        )

    rows_given = rows_back(local_rows, LOW)
    output_theirs = pin(output_theirs)
    output_ring = Scatter(
        ring, line, [(mixer_rows_back, attended_own, output_theirs)], part, output_width // 2
    )
    output_ring.prepare()
    rows_mine = rows_back(0, WIDE)
    while down_ring.left():
        down_ring.prepare()
        down_ring.send()
        down_ring.land()
    ((down_kept, down_given),) = pin(down_ring.total(core_table))
    first_theirs_back = pin(first_theirs_back)
    upward_ring.land()
    for stream in (gate_ring, upward_ring):
        while stream.left():
            stream.prepare()
            stream.send()
            stream.land()
    first_ring = Scatter(
        ring, line, [(rows_low, first_own_back, first_theirs_back)], part, first_cols - HD
    )
    output_ring.send()
    rows_theirs = tp_swap(rows_given)
    down_theirs = core_swap(down_given)
    first_ring.prepare()
    output_ring.land()
    first_ring.send()
    output_ring.prepare()
    rows_theirs = pin(rows_theirs)
    first_ring.land()
    output_ring.send()
    first_ring.prepare()
    hidden_delta, input_slope = opened_back(
        rows_mine, rows_theirs, laurel_mid_back, summed_back, residual, left_full, line.mark
    )
    slopes = jnp.concatenate(
        [
            input_slope,
            mixer_slope,
            laurel_slope,
            prefeed_slope,
            postfeed_slope,
            branch_slope,
            jnp.pad(jnp.concatenate([query_slope, key_slope], axis=1), ((0, 1), (0, width - 2 * HD))),
        ],
    )
    hidden_delta, gain_slopes = permuted(
        [hidden_delta, slopes], [WIDE, WIDE], ring.owners, inverse=True
    )
    slopes = jnp.concatenate([gain_slopes[:6], slopes[6:]])
    line.mark = hidden_delta
    output_ring.land()
    slopes = lax.all_gather(pin(slopes)[None], everywhere, axis=0, tiled=True)
    first_ring.send()
    output_ring.prepare()
    ((gate_kept, gate_given),) = pin(gate_ring.total(core_table))
    first_ring.land()
    output_ring.send()
    gate_theirs = core_swap(gate_given)
    first_ring.prepare()
    ((upward_kept, upward_given),) = pin(upward_ring.total(core_table))
    down_theirs, gate_theirs = pin((down_theirs, gate_theirs))
    output_ring.land()
    first_ring.send()
    upward_theirs = core_swap(upward_given)
    output_ring.prepare()
    down_delta = pin(assembled(core_table, down_kept, down_theirs, True))
    first_ring.land()
    output_ring.send()
    upward_theirs = pin(upward_theirs)
    first_ring.prepare()
    gate_delta = pin(assembled(core_table, gate_kept, gate_theirs))
    output_ring.land()
    while output_ring.left():
        output_ring.prepare()
        output_ring.send()
        output_ring.land()
    first_ring.send()
    upward_delta = pin(assembled(core_table, upward_kept, upward_theirs))
    ((output_kept, output_given),) = pin(output_ring.total(core_table))
    output_theirs = core_swap(output_given)
    output_theirs = pin(output_theirs)
    first_ring.land()
    while first_ring.left():
        first_ring.prepare()
        first_ring.send()
        first_ring.land()
    ((first_kept, first_given),) = pin(first_ring.total(core_table))
    first_theirs = core_swap(first_given)
    output_delta = pin(assembled(core_table, output_kept, output_theirs, True))
    query_delta, key_delta, value_delta = parted(
        core_table, first_kept, pin(first_theirs), query_cols
    )
    slopes = jnp.sum(slopes, axis=0)
    small_delta = small_delta.astype(WIDE)
    return (
        result,
        line.mark,
        layer_delta,
        query_delta,
        key_delta,
        value_delta,
        output_delta,
        small_delta[:, 2 * side : 2 * side + rank],
        small_delta[:, 2 * side + rank :].T,
        gate_delta,
        upward_delta,
        down_delta,
        small_delta[:, :side],
        small_delta[:, side : 2 * side].T,
        slopes[0],
        slopes[6, :HD],
        slopes[6, HD : 2 * HD],
        slopes[1],
        slopes[2],
        slopes[3],
        slopes[4],
        slopes[5],
    )


def solution(mesh):
    tokens = P(("seq", "tp"), None)
    spread = P(None, ("seq", "tp"))
    inward = P("seq", "tp")
    outward = P("tp", "seq")
    weights = (
        inward,
        inward,
        inward,
        outward,
        tokens,
        spread,
        inward,
        inward,
        outward,
        tokens,
        spread,
    )
    return jax.shard_map(
        shards,
        mesh=mesh,
        in_specs=(tokens, tokens, tokens, P()) + weights + (P(),) * 8,
        out_specs=(tokens, tokens, tokens) + weights + (P(),) * 8,
        check_vma=False,
    )
```
